256 devices in a mesh: row: 16 (over x, z_lo, core), col: 16 (over y, z_hi).
Axes of the slice: x: 4, y: 4, z: 8 (z_hi: 4, z_lo: 2; z = z_hi * 2 + z_lo), core: 2. Of those that a mesh axis runs over, the one named last changes fastest.
Arguments:
- swath: int32 [2560, 8192], P('row', 'col'), may hold values from 0 to 1
- coherence: int32 [2560, 8192], P('row', 'col'), may hold values from 0 to 7
- phase_counts: int32 [2560, 8192], P('row', 'col'), may hold values from 0 to 255
Outputs:
- unwrapped: float32 [2560, 8192], P('row', 'col')
The draws below stay inside these ranges and needn't reach their ends.
All inputs are finite; a program needn't handle non-finite values.
Results may differ from the reference program's by a relative error of at most 0.0012.
Values sent between devices are 32-bit elements; how exact they have to be, the bound alone decides.
A program may use at most 128 MiB of HBM per device.

```python
import jax
import jax.numpy as jnp
from jax import lax

GRIDS = 4
LEVELS = 256
NCLASS = 8
NX = 2560
NY = 8192


def draw_swath(key, part):
    rows = jnp.arange(NX, dtype=jnp.int32)[:, None]
    columns = jnp.arange(NY, dtype=jnp.int32)[None, :]
    threshold = 300 + 325 * rows // NX + 325 * columns // NY
    sample = jax.random.randint(jax.random.fold_in(key, 11), (NX, NY), 0, 1000, dtype=jnp.int32)
    return (sample < threshold).astype(jnp.int32)


def with_ends(array, rng, low, high):
    longest = array.shape.index(max(array.shape))
    spots = []
    for shift in (0, 1):
        where = [jax.random.randint(jax.random.fold_in(rng, axis), (), 0, length) for axis, length in enumerate(array.shape)]
        where[longest] = (where[longest] + shift) % array.shape[longest]
        spots.append(tuple(where))
    return array.at[spots[0]].set(low).at[spots[1]].set(high)


def setup_inputs(seed: int = 0) -> dict:
    seeds = jax.random.split(jax.random.key(seed), 4)
    swath = draw_swath(jax.random.fold_in(seeds[3], 71), 0)
    coherence = with_ends(jax.random.randint(seeds[1], (NX, NY), 0, NCLASS), jax.random.fold_in(seeds[1], 1), 0, NCLASS - 1).astype(jnp.int32)
    phase_counts = with_ends(jax.random.randint(seeds[2], (NX, NY), 0, LEVELS), jax.random.fold_in(seeds[2], 1), 0, LEVELS - 1).astype(jnp.int32)
    return dict(swath=swath, coherence=coherence, phase_counts=phase_counts)


damping = 0.8
diag_floor = 0.5
error_floor = 0.5
epsilon = 1e-06
screen_width = 4.0
highest = lax.Precision.HIGHEST

def cosine_table(count):
    freq = jnp.arange(count, dtype=jnp.float32)[:, None]
    place = jnp.arange(count, dtype=jnp.float32)[None, :]
    table = jnp.cos(jnp.pi * (place + 0.5) * freq / count) * jnp.sqrt(2.0 / count)
    return jnp.where(freq == 0, table * jnp.sqrt(0.5), table)

def eigen_values(freq, count):
    return 2.0 - 2.0 * jnp.cos(jnp.pi * freq / count)

def weight_diagonal(w_down, w_right):
    w_up = jnp.pad(w_down, ((1, 0), (0, 0)))[:-1]
    w_left = jnp.pad(w_right, ((0, 0), (1, 0)))[:, :-1]
    return w_down + w_up + w_right + w_left

def operate(estimate, w_down, w_right, diagonal):
    padded = jnp.pad(estimate, 1)
    w_up = jnp.pad(w_down, ((1, 0), (0, 0)))[:-1]
    w_left = jnp.pad(w_right, ((0, 0), (1, 0)))[:, :-1]
    beside = w_down * padded[2:, 1:-1] + w_up * padded[:-2, 1:-1] + w_right * padded[1:-1, 2:] + w_left * padded[1:-1, :-2]
    return diagonal * estimate - beside

def coarse_solve(source, w_down, w_right):
    rows, cols = source.shape
    count = (rows - 1) * cols + rows * (cols - 1)
    mean = (jnp.sum(w_down) + jnp.sum(w_right)) / count + epsilon
    table_x = cosine_table(rows)
    table_y = cosine_table(cols)
    spectrum = jnp.dot(jnp.dot(table_x, source, precision=highest), table_y.T, precision=highest)
    lam_x = eigen_values(jnp.arange(rows, dtype=jnp.float32), rows)
    lam_y = eigen_values(jnp.arange(cols, dtype=jnp.float32), cols)
    spectrum = spectrum / (mean * (lam_x[:, None] + lam_y[None, :] + (screen_width / cols) ** 2))
    return jnp.dot(table_x.T, jnp.dot(spectrum, table_y, precision=highest), precision=highest)

def cycle(estimate, source, w_down, w_right, depth):
    if depth == GRIDS:
        return coarse_solve(source, w_down, w_right)
    diagonal = weight_diagonal(w_down, w_right)
    divisor = jnp.maximum(diagonal, diag_floor)
    estimate = estimate + damping * (source - operate(estimate, w_down, w_right, diagonal)) / divisor
    residual = source - operate(estimate, w_down, w_right, diagonal)
    rows, cols = residual.shape
    coarse_source = residual.reshape(rows // 2, 2, cols // 2, 2).sum(axis=(1, 3))
    coarse_down = w_down[1::2, 0::2] + w_down[1::2, 1::2]
    coarse_right = w_right[0::2, 1::2] + w_right[1::2, 1::2]
    correction = cycle(jnp.zeros_like(coarse_source), coarse_source, coarse_down, coarse_right, depth + 1)
    estimate = estimate + jnp.repeat(jnp.repeat(correction, 2, axis=0), 2, axis=1)
    return estimate + damping * (source - operate(estimate, w_down, w_right, diagonal)) / divisor

def build_source(w_down, w_right, slope_down, slope_right):
    flux_down = w_down * slope_down
    flux_right = w_right * slope_right
    flux_up = jnp.pad(flux_down, ((1, 0), (0, 0)))[:-1]
    flux_left = jnp.pad(flux_right, ((0, 0), (1, 0)))[:, :-1]
    return flux_up - flux_down + flux_left - flux_right

def reference(swath, coherence, phase_counts):
    quality = swath.astype(jnp.float32) * (coherence.astype(jnp.float32) / (NCLASS - 1)) ** 2
    zero_row = jnp.zeros((1, NY), jnp.float32)
    zero_column = jnp.zeros((NX, 1), jnp.float32)
    w_down = jnp.concatenate([jnp.minimum(quality[:-1], quality[1:]), zero_row], 0)
    w_right = jnp.concatenate([jnp.minimum(quality[:, :-1], quality[:, 1:]), zero_column], 1)
    half = LEVELS // 2
    turn = 2.0 * jnp.pi / LEVELS
    step_down = jnp.mod(phase_counts[1:] - phase_counts[:-1] + half, LEVELS) - half
    step_right = jnp.mod(phase_counts[:, 1:] - phase_counts[:, :-1] + half, LEVELS) - half
    slope_down = jnp.concatenate([step_down.astype(jnp.float32) * turn, zero_row], 0)
    slope_right = jnp.concatenate([step_right.astype(jnp.float32) * turn, zero_column], 1)
    source = build_source(w_down, w_right, slope_down, slope_right)
    first = cycle(jnp.zeros((NX, NY), jnp.float32), source, w_down, w_right, 0)
    padded = jnp.pad(first, 1)
    error_down = padded[2:, 1:-1] - first - slope_down
    error_right = padded[1:-1, 2:] - first - slope_right
    reweighted_down = w_down / jnp.maximum(jnp.abs(error_down), error_floor)
    reweighted_right = w_right / jnp.maximum(jnp.abs(error_right), error_floor)
    source = build_source(reweighted_down, reweighted_right, slope_down, slope_right)
    return cycle(first, source, reweighted_down, reweighted_right, 0)
```

```python
import functools

import jax
import jax.numpy as jnp
import numpy as np
from jax import lax
from jax.experimental import pallas as pl
from jax.experimental.pallas import tpu as pltpu
from jax.sharding import PartitionSpec as P

MESH = pl.DeviceIdType.MESH
HIGHEST = lax.Precision.HIGHEST
F32 = jnp.float32

GRIDS = 4
NCLASS = 8
LEVELS = 256
DAMPING = 0.8
DIAG_FLOOR = 0.5
TURN = 2.0 * np.pi
ERROR_FLOOR = 0.5
EPSILON = 1e-6
SCREEN_WIDTH = 4.0

STEP = 2**GRIDS
HALO = 48
ROWS = 160
COLS = 512
CROWS = ROWS // STEP
CCOLS = COLS // STEP
EXT = ROWS + 2 * HALO
SUB = EXT // STEP
OWN_CHUNKS = COLS // 128
CHUNKS = OWN_CHUNKS + 1
WIDTH = CHUNKS * 128
FREQ = 256
PAD = 48
SHIFTS = (1, 2, 4, 8, 16, 32)
HALVES = tuple(slice(h, h + 8) for h in range(0, SUB, 8))


def tables(rows, cols):
    devices = rows // CROWS
    freq = np.arange(rows)[:, None]
    cosine = np.cos(np.pi * (np.arange(rows)[None, :] + 0.5) * freq / rows) * np.sqrt(2.0 / rows)
    cosine[0] *= np.sqrt(0.5)
    forward = np.zeros((2, devices, 8, FREQ))
    backward = np.zeros((devices, SUB, FREQ))
    for d in range(devices):
        for k in range(CROWS):
            forward[k // 8, d, k % 8, :rows] = cosine[:, d * CROWS + k]
        for k in range(SUB):
            place = d * CROWS + (k if k < CROWS + HALO // STEP else k - SUB)
            if 0 <= place < rows:
                backward[d, k, :rows] = cosine[:, place]
    shift = 2.0 - 2.0 * np.cos(np.pi * np.arange(rows) / rows) + (SCREEN_WIDTH / cols) ** 2
    theta = 2.0 * np.arcsinh(np.sqrt(shift) / 2.0)
    constants = np.zeros((16, FREQ))
    constants[0] = 1.0
    constants[0, :rows] = theta
    constants[1, :rows] = 1.0 / (2.0 * np.sinh(theta))
    constants[2] = 1.0
    constants[2, :rows] = 1.0 / (1.0 - np.exp(-2.0 * cols * theta))
    for i, s in enumerate(SHIFTS):
        constants[3 + i] = np.exp(-s * constants[0])
    return (
        forward.reshape(2, devices * 8, FREQ).astype(np.float32),
        backward.astype(np.float32),
        constants.astype(np.float32),
    )


def ahead(x, s):
    return pltpu.roll(x, WIDTH - s, 1)


def behind(x, s):
    return pltpu.roll(x, s, 1)


def wrap(ref, above=True, below=True):
    last = ref.shape[0] - 2
    if above:
        ref[0] = pltpu.roll(ref[last], 1, 0)
    if below:
        ref[last + 1] = pltpu.roll(ref[1], SUB - 1, 0)


def steps(count, body):
    if count <= 2:
        for i in range(count):
            body(i)
    else:

        def step(i, carry):
            body(i)
            return carry

        lax.fori_loop(0, count, step, 0)


def kernel(R, C, *refs):
    (
        swath_h,
        coherence_h,
        counts_h,
        forward_h,
        backward_h,
        constants_h,
        out_h,
        swath,
        coherence,
        counts,
        forward,
        backward,
        constants,
        nat,
        left_pack,
        right_pack,
        from_left,
        from_right,
        result,
        qual,
        phase,
        wd,
        wr,
        sd,
        sr,
        v0,
        rdiv0,
        first,
        gd,
        gr,
        *rest,
    ) = refs
    levels = []
    for _ in range(3):
        levels.append(rest[:6])
        rest = rest[6:]
    (
        coarse,
        select,
        spread,
        blocks,
        amps,
        near_send,
        near_left,
        near_right,
        ext,
        powers,
        coef,
        load_sem,
        p1_send,
        p1_recv,
        p2_send,
        p2_recv,
        p3_send,
        p3_recv,
        nb_send,
        nb_recv,
        out_sem,
    ) = rest

    r = lax.axis_index("row")
    c = lax.axis_index("col")
    N = CCOLS * C

    loads = [
        pltpu.make_async_copy(swath_h, swath, load_sem.at[0]),
        pltpu.make_async_copy(coherence_h, coherence, load_sem.at[1]),
        pltpu.make_async_copy(counts_h, counts, load_sem.at[2]),
        pltpu.make_async_copy(constants_h, constants, load_sem.at[3]),
        pltpu.make_async_copy(forward_h, forward, load_sem.at[4]),
        pltpu.make_async_copy(backward_h.at[r], backward, load_sem.at[5]),
    ]
    for copy in loads:
        copy.start()

    for a in range(2):
        for k in range(OWN_CHUNKS):
            nat[a, k, ROWS:EXT, :] = jnp.zeros((EXT - ROWS, 128), F32)
    from_left[...] = jnp.zeros((EXT, 128), F32)
    from_right[...] = jnp.zeros((EXT, 128), F32)
    near_left[...] = jnp.zeros(near_left.shape, F32)
    near_right[...] = jnp.zeros(near_right.shape, F32)

    barrier = pltpu.get_barrier_semaphore()
    for i in range(1, R):
        pl.semaphore_signal(barrier, inc=1, device_id=(lax.rem(r + i, R), c), device_id_type=MESH)
    for i in range(1, C):
        pl.semaphore_signal(barrier, inc=1, device_id=(r, lax.rem(c + i, C)), device_id_type=MESH)
    for i in (1, R - 1):
        for j in (1, C - 1):
            pl.semaphore_signal(
                barrier, inc=1, device_id=(lax.rem(r + i, R), lax.rem(c + j, C)), device_id_type=MESH
            )

    for copy in loads[:3]:
        copy.wait()
    lane = lax.broadcasted_iota(jnp.int32, (32, 128), 1)

    def prepare(i):
        rows = pl.ds(pl.multiple_of(i * 32, 32), 32)
        for k in range(OWN_CHUNKS):
            span = slice(128 * k, 128 * k + 128)
            level = coherence[rows, span].astype(F32) * (1.0 / (NCLASS - 1))
            q = swath[rows, span].astype(F32) * (level * level)
            ph = counts[rows, span].astype(F32) * (1.0 / LEVELS)
            nat[0, k, rows, :] = q
            nat[1, k, rows, :] = ph
            if k == 0:
                left_pack[rows, :] = jnp.where(lane < 64, q, pltpu.roll(ph, 64, 1))
            if k == OWN_CHUNKS - 1:
                right_pack[rows, :] = jnp.where(lane < 64, pltpu.roll(ph, 64, 1), q)

    steps(ROWS // 32, prepare)
    pl.semaphore_wait(barrier, R + C + 2)

    top, bottom = slice(0, HALO), slice(ROWS - HALO, ROWS)
    own, below, above = slice(0, ROWS), slice(ROWS, ROWS + HALO), slice(ROWS + HALO, EXT)
    chunks = slice(0, OWN_CHUNKS)
    is_up, is_down = r > 0, r < R - 1
    is_left, is_right = c > 0, c < C - 1
    both = jnp.logical_and
    plan = [
        (is_up, -1, 0, nat.at[:, chunks, top, :], nat.at[:, chunks, below, :], is_down),
        (is_down, 1, 0, nat.at[:, chunks, bottom, :], nat.at[:, chunks, above, :], is_up),
        (is_left, 0, -1, left_pack, from_right.at[own], is_right),
        (is_right, 0, 1, right_pack, from_left.at[own], is_left),
        (both(is_up, is_left), -1, -1, left_pack.at[top], from_right.at[below], both(is_down, is_right)),
        (both(is_down, is_left), 1, -1, left_pack.at[bottom], from_right.at[above], both(is_up, is_right)),
        (both(is_up, is_right), -1, 1, right_pack.at[top], from_left.at[below], both(is_down, is_left)),
        (both(is_down, is_right), 1, 1, right_pack.at[bottom], from_left.at[above], both(is_up, is_left)),
    ]
    halo_copies = []
    for i, (sends, dr, dc, source, target, receives) in enumerate(plan):
        copy = pltpu.make_async_remote_copy(
            src_ref=source,
            dst_ref=target,
            send_sem=p1_send.at[i],
            recv_sem=p1_recv.at[i],
            device_id=(lax.rem(r + dr + R, R), lax.rem(c + dc + C, C)),
            device_id_type=MESH,
        )
        halo_copies.append((sends, receives, copy))
        pl.when(sends)(copy.start)

    for copy in loads[3:]:
        copy.wait()
    theta = constants[0:1, :]
    green = constants[1:2, :]
    inverse = constants[2:3, :]
    yy = lax.broadcasted_iota(jnp.int32, (CCOLS, FREQ), 0)
    last = CCOLS - 1
    powers[0] = jnp.exp(-theta * (last - yy).astype(F32))
    powers[1] = jnp.exp(-theta * yy.astype(F32))
    powers[2] = jnp.where(yy <= last - 3, jnp.exp(-theta * jnp.maximum(last - 3 - yy, 0).astype(F32)), 0.0)
    powers[3] = jnp.where(yy >= 3, jnp.exp(-theta * jnp.maximum(yy - 3, 0).astype(F32)), 0.0)

    def decay(n):
        return jnp.exp(-theta * n.astype(F32))

    def directly(n, inside):
        return jnp.where(inside, decay(jnp.maximum(n, 0)), 0.0)

    for i in range(C):
        rev = C - 1 - i
        coef[0, i, 0:1, :] = directly(CCOLS * (c - 1 - i) - 3, i < c - 1) + inverse * decay(
            N + CCOLS * rev + CCOLS * c - 3
        )
        coef[0, i, 1:2, :] = inverse * decay(CCOLS * i + CCOLS * c - 3)
        coef[1, i, 0:1, :] = inverse * decay(CCOLS * (C - 1 - c) + CCOLS * rev - 3)
        coef[1, i, 1:2, :] = directly(CCOLS * (i - c - 1) - 3, i > c + 1) + inverse * decay(
            2 * N - CCOLS * (c + 1) + CCOLS * i - 3
        )
    at = lax.broadcasted_iota(jnp.int32, (COLS, 128), 0)
    to = lax.broadcasted_iota(jnp.int32, (COLS, 128), 1)
    select[...] = jnp.where((to < 64) & (at == STEP * (to & 31)), 1.0, 0.0).astype(F32)
    at = lax.broadcasted_iota(jnp.int32, (PAD, WIDTH), 0)
    to = lax.broadcasted_iota(jnp.int32, (PAD, WIDTH), 1) >> GRIDS
    spread[...] = jnp.where(at == jnp.where(to < CCOLS + 3, to + 8, to + 8 - WIDTH // STEP), 1.0, 0.0).astype(F32)
    ext[...] = jnp.zeros((PAD, FREQ), F32)

    for _, receives, copy in halo_copies:
        pl.when(receives)(copy.wait_recv)

    lane = lax.broadcasted_iota(jnp.int32, (SUB, 128), 1)
    for p in range(STEP):
        rows = pl.ds(p, SUB, stride=STEP)
        for k in range(OWN_CHUNKS):
            span = slice(128 * k, 128 * k + 128)
            qual[p + 1, :, span] = nat.at[0, k][rows, :]
            phase[p + 1, :, span] = nat.at[1, k][rows, :]
        a, b = from_right[rows, :], from_left[rows, :]
        qual[p + 1, :, COLS:WIDTH] = jnp.where(lane < 64, a, b)
        phase[p + 1, :, COLS:WIDTH] = pltpu.roll(jnp.where(lane < 64, b, a), 64, 1)
    wrap(qual, above=False)
    wrap(phase, above=False)

    def steep(u):
        return u - jnp.floor(u + 0.5)

    def make_faces(p):
        for h in HALVES:
            q, ph = qual[p + 1, h], phase[p + 1, h]
            wd[p + 1, h] = jnp.minimum(q, qual[p + 2, h])
            wr[p, h] = jnp.minimum(q, ahead(q, 1))
            sd[p + 1, h] = steep(phase[p + 2, h] - ph)
            sr[p, h] = steep(ahead(ph, 1) - ph)

    steps(STEP, make_faces)
    wrap(wd, below=False)
    wrap(sd, below=False)

    def start_first(p):
        for h in HALVES:
            a, au, b = wd[p + 1, h], wd[p, h], wr[p, h]
            fr = b * sr[p, h]
            source = au * sd[p, h] - a * sd[p + 1, h] + behind(fr, 1) - fr
            rdiv = DAMPING / jnp.maximum(a + au + b + behind(b, 1), DIAG_FLOOR)
            rdiv0[p, h] = rdiv
            v0[p + 1, h] = source * rdiv

    steps(STEP, start_first)
    wrap(v0)

    def restrict_fine():
        src, a1, b1 = levels[0][0], levels[0][1], levels[0][2]

        def body(i):
            for h in HALVES:
                va, v1, v2, vb = v0[2 * i, h], v0[2 * i + 1, h], v0[2 * i + 2, h], v0[2 * i + 3, h]
                a_odd = wd[2 * i + 2, h]
                y = a_odd * (vb - v2 - sd[2 * i + 2, h]) - wd[2 * i, h] * (v1 - va - sd[2 * i, h])
                b0, b_odd = wr[2 * i, h], wr[2 * i + 1, h]
                g = b0 * (ahead(v1, 1) - v1 - sr[2 * i, h]) + b_odd * (ahead(v2, 1) - v2 - sr[2 * i + 1, h])
                src[i, h] = y + ahead(y + g, 1) - behind(g, 1)
                a1[i + 1, h] = a_odd + ahead(a_odd, 1)
                b1[i, h] = ahead(b0 + b_odd, 1)

        steps(STEP // 2, body)
        wrap(a1, below=False)

    def down(level):
        s = 2**level
        count = STEP // s
        src, a, b, rdiv, v, _ = levels[level - 1]

        def smooth(p):
            for h in HALVES:
                bb = b[p, h]
                d = DAMPING / jnp.maximum(a[p + 1, h] + a[p, h] + bb + behind(bb, s), DIAG_FLOOR)
                rdiv[p, h] = d
                v[p + 1, h] = src[p, h] * d

        steps(count, smooth)
        wrap(v)
        if level < GRIDS - 1:
            src_n, a_n, b_n = levels[level][0], levels[level][1], levels[level][2]
        else:
            src_n, a_n, b_n = None, None, None

        def body(i):
            for h in HALVES:
                va, v1, v2, vb = v[2 * i, h], v[2 * i + 1, h], v[2 * i + 2, h], v[2 * i + 3, h]
                a_odd = a[2 * i + 2, h]
                t = src[2 * i, h] + src[2 * i + 1, h] + a_odd * (vb - v2) - a[2 * i, h] * (v1 - va)
                b0, b_odd = b[2 * i, h], b[2 * i + 1, h]
                g = b0 * (ahead(v1, s) - v1) + b_odd * (ahead(v2, s) - v2)
                out = t + ahead(t + g, s) - behind(g, s)
                if src_n is None:
                    coarse[h] = out
                else:
                    src_n[i, h] = out
                    a_n[i + 1, h] = a_odd + ahead(a_odd, s)
                    b_n[i, h] = ahead(b0 + b_odd, s)

        steps(count // 2, body)
        if a_n is not None:
            wrap(a_n, below=False)

    def up(level):
        s = 2**level
        count = STEP // s
        src, a, b, rdiv, v, out = levels[level - 1]

        def add(i):
            for h in HALVES:
                if level == GRIDS - 1:
                    x = coarse[h]
                else:
                    x = levels[level][5][i, h]
                    column = lax.broadcasted_iota(jnp.int32, x.shape, 1)
                    x = jnp.where((column & s) == 0, x, behind(x, s))
                v[2 * i + 1, h] = v[2 * i + 1, h] + x
                v[2 * i + 2, h] = v[2 * i + 2, h] + x

        steps(count // 2, add)
        wrap(v)

        def smooth(i):
            for h in HALVES:
                va, v1, v2, vb = v[2 * i, h], v[2 * i + 1, h], v[2 * i + 2, h], v[2 * i + 3, h]
                g0 = a[2 * i, h] * (v1 - va)
                g1 = a[2 * i + 1, h] * (v2 - v1)
                g2 = a[2 * i + 2, h] * (vb - v2)
                f1 = b[2 * i, h] * (ahead(v1, s) - v1)
                f2 = b[2 * i + 1, h] * (ahead(v2, s) - v2)
                out[2 * i, h] = v1 + (src[2 * i, h] + g1 - g0 + f1 - behind(f1, s)) * rdiv[2 * i, h]
                out[2 * i + 1, h] = v2 + (src[2 * i + 1, h] + g2 - g1 + f2 - behind(f2, s)) * rdiv[2 * i + 1, h]

        steps(count // 2, smooth)

    def up_fine():
        def add(i):
            for h in HALVES:
                x = levels[0][5][i, h]
                column = lax.broadcasted_iota(jnp.int32, x.shape, 1)
                x = jnp.where((column & 1) == 0, x, behind(x, 1))
                v0[2 * i + 1, h] = v0[2 * i + 1, h] + x
                v0[2 * i + 2, h] = v0[2 * i + 2, h] + x

        steps(STEP // 2, add)
        wrap(v0)

        def smooth(i):
            for h in HALVES:
                va, v1, v2, vb = v0[2 * i, h], v0[2 * i + 1, h], v0[2 * i + 2, h], v0[2 * i + 3, h]
                g0 = wd[2 * i, h] * (v1 - va - sd[2 * i, h])
                g1 = wd[2 * i + 1, h] * (v2 - v1 - sd[2 * i + 1, h])
                g2 = wd[2 * i + 2, h] * (vb - v2 - sd[2 * i + 2, h])
                f1 = wr[2 * i, h] * (ahead(v1, 1) - v1 - sr[2 * i, h])
                f2 = wr[2 * i + 1, h] * (ahead(v2, 1) - v2 - sr[2 * i + 1, h])
                first[2 * i + 1, h] = v1 + (g1 - g0 + f1 - behind(f1, 1)) * rdiv0[2 * i, h]
                first[2 * i + 2, h] = v2 + (g2 - g1 + f2 - behind(f2, 1)) * rdiv0[2 * i + 1, h]

        steps(STEP // 2, smooth)

    def coarse_solve(turn):
        _, a3, b3, _, _, _ = levels[2]
        column = lax.broadcasted_iota(jnp.int32, (SUB, COLS), 1)
        line = lax.broadcasted_iota(jnp.int32, (SUB, COLS), 0)
        here = slice(0, COLS)
        part = jnp.where((column & 7) == 0, a3[2, :, here], 0.0) + jnp.where(
            (column & 15) == 8, b3[0, :, here] + b3[1, :, here], 0.0
        )
        part = jnp.where((line < CROWS) & ((column & 7) == 0), part, 0.0)
        local = jnp.sum(jnp.sum(part, axis=1, keepdims=True), axis=0, keepdims=True)
        mine = jnp.dot(coarse[:, here], select[...], precision=HIGHEST, preferred_element_type=F32)
        spot = lax.broadcasted_iota(jnp.int32, (8, 128), 1)
        blocks[turn, r] = jnp.where(spot < 32, mine[0:8], jnp.where(spot < 64, mine[8:16], local))
        copies = []
        for i in range(1, R):
            copy = pltpu.make_async_remote_copy(
                src_ref=blocks.at[turn, r],
                dst_ref=blocks.at[turn, r],
                send_sem=p2_send.at[turn, i - 1],
                recv_sem=p2_recv.at[turn, i - 1],
                device_id=(lax.rem(r + i, R), c),
                device_id_type=MESH,
            )
            copy.start()
            copies.append(copy)
        for copy in copies:
            copy.wait_recv()
        every = blocks[turn].reshape(R * 8, 128).T
        hat = jnp.dot(every[0:32], forward[0], precision=HIGHEST, preferred_element_type=F32) + jnp.dot(
            every[32:64], forward[1], precision=HIGHEST, preferred_element_type=F32
        )
        rows_sum = jnp.sum(every[64:65], axis=1, keepdims=True) * 0.125

        def total(n):
            return jnp.sum(powers[n] * hat, axis=0, keepdims=True)

        mode = lax.broadcasted_iota(jnp.int32, (1, FREQ), 1)
        amps[turn, c, 0:1, :] = jnp.where(mode < CROWS * R, total(0), rows_sum)
        amps[turn, c, 1:2, :] = total(1)
        near_send[turn, 0, 0:1, :] = total(2)
        near_send[turn, 0, 1:4, :] = hat[CCOLS - 3 : CCOLS]
        near_send[turn, 1, 0:3, :] = hat[0:3]
        near_send[turn, 1, 3:4, :] = total(3)
        for i in range(1, C):
            copy = pltpu.make_async_remote_copy(
                src_ref=amps.at[turn, c],
                dst_ref=amps.at[turn, c],
                send_sem=p3_send.at[turn, i - 1],
                recv_sem=p3_recv.at[turn, i - 1],
                device_id=(r, lax.rem(c + i, C)),
                device_id_type=MESH,
            )
            copy.start()
            copies.append(copy)
        rightward = pltpu.make_async_remote_copy(
            src_ref=near_send.at[turn, 0],
            dst_ref=near_left.at[turn],
            send_sem=nb_send.at[turn, 0],
            recv_sem=nb_recv.at[turn, 0],
            device_id=(r, lax.rem(c + 1, C)),
            device_id_type=MESH,
        )
        leftward = pltpu.make_async_remote_copy(
            src_ref=near_send.at[turn, 1],
            dst_ref=near_right.at[turn],
            send_sem=nb_send.at[turn, 1],
            recv_sem=nb_recv.at[turn, 1],
            device_id=(r, lax.rem(c + C - 1, C)),
            device_id_type=MESH,
        )
        pl.when(is_right)(rightward.start)
        pl.when(is_left)(leftward.start)
        pl.when(is_left)(rightward.wait_recv)
        pl.when(is_right)(leftward.wait_recv)
        for copy in copies[R - 1 :]:
            copy.wait_recv()
        into_left = jnp.zeros((2, FREQ), F32)
        into_right = jnp.zeros((2, FREQ), F32)
        weight = jnp.zeros((2, FREQ), F32)
        for i in range(C):
            x = amps[turn, i]
            into_left += coef[0, i] * x
            into_right += coef[1, i] * x
            weight += x
        into_left = into_left[0:1] + into_left[1:2]
        into_right = into_right[0:1] + into_right[1:2]
        weight = jnp.sum(jnp.where(mode == FREQ - 1, weight[0:1], 0.0), axis=1, keepdims=True)
        grid_rows, grid_cols = CROWS * R, CCOLS * C
        mean = weight * (1.0 / ((grid_rows - 1) * grid_cols + grid_rows * (grid_cols - 1))) + EPSILON
        ext[4:8, :] = near_left[turn]
        ext[4:5, :] = near_left[turn, 0:1, :] + into_left
        ext[8 : 8 + CCOLS, :] = hat
        ext[8 + CCOLS : 12 + CCOLS, :] = near_right[turn]
        ext[11 + CCOLS : 12 + CCOLS, :] = near_right[turn, 3:4, :] + into_right
        hats = ext[...]
        place = lax.broadcasted_iota(jnp.int32, (PAD, FREQ), 0)
        going_right = hats
        going_left = hats
        for i, s in enumerate(SHIFTS):
            q = constants[3 + i : 4 + i, :]
            going_right += q * jnp.where(place >= s, pltpu.roll(going_right, s, 0), 0.0)
            going_left += q * jnp.where(place < PAD - s, pltpu.roll(going_left, PAD - s, 0), 0.0)
        modes = (going_right + going_left - hats) * (green / mean)
        values = lax.dot_general(
            backward[...], modes, (((1,), (1,)), ((), ())), precision=HIGHEST, preferred_element_type=F32
        )
        coarse[...] = jnp.dot(values, spread[...], precision=HIGHEST, preferred_element_type=F32)
        return copies, rightward, leftward

    def cycle(turn):
        restrict_fine()
        for level in range(1, GRIDS):
            down(level)
        sent = coarse_solve(turn)
        for level in range(GRIDS - 1, 0, -1):
            up(level)
        up_fine()
        return sent

    sent = [cycle(0)]
    wrap(first)

    def reweight(p):
        for h in HALVES:
            f = first[p + 1, h]
            e = first[p + 2, h] - f - sd[p + 1, h]
            a = wd[p + 1, h] / jnp.maximum(jnp.abs(e) * TURN, ERROR_FLOOR)
            wd[p + 1, h] = a
            gd[p + 1, h] = a * e
            e = ahead(f, 1) - f - sr[p, h]
            b = wr[p, h] / jnp.maximum(jnp.abs(e) * TURN, ERROR_FLOOR)
            wr[p, h] = b
            gr[p, h] = b * e

    steps(STEP, reweight)
    wrap(wd, below=False)
    wrap(gd, below=False)

    def start_second(p):
        for h in HALVES:
            b, f = wr[p, h], gr[p, h]
            rdiv = DAMPING / jnp.maximum(wd[p + 1, h] + wd[p, h] + b + behind(b, 1), DIAG_FLOOR)
            rdiv0[p, h] = rdiv
            v0[p + 1, h] = first[p + 1, h] + (gd[p + 1, h] - gd[p, h] + f - behind(f, 1)) * rdiv

    steps(STEP, start_second)
    wrap(v0)
    sent.append(cycle(1))

    outs = []
    for k in range(OWN_CHUNKS):
        span = slice(128 * k, 128 * k + 128)
        for p in range(STEP):
            result.at[k][pl.ds(p, SUB, stride=STEP), :] = first[p + 1, :, span] * TURN
        copy = pltpu.make_async_copy(result.at[k, own, :], out_h.at[:, span], out_sem.at[k])
        copy.start()
        outs.append(copy)
    for sends, _, copy in halo_copies:
        pl.when(sends)(copy.wait_send)
    for copies, rightward, leftward in sent:
        for copy in copies:
            copy.wait_send()
        pl.when(is_right)(rightward.wait_send)
        pl.when(is_left)(leftward.wait_send)
    for copy in outs:
        copy.wait()


def scratch(R, C):
    def field(count):
        return pltpu.VMEM((count, SUB, WIDTH), F32)

    shapes = [
        pltpu.VMEM((ROWS, COLS), jnp.int32),
        pltpu.VMEM((ROWS, COLS), jnp.int32),
        pltpu.VMEM((ROWS, COLS), jnp.int32),
        pltpu.VMEM((2, R * 8, FREQ), F32),
        pltpu.VMEM((SUB, FREQ), F32),
        pltpu.VMEM((16, FREQ), F32),
        pltpu.VMEM((2, OWN_CHUNKS, EXT, 128), F32),
        pltpu.VMEM((ROWS, 128), F32),
        pltpu.VMEM((ROWS, 128), F32),
        pltpu.VMEM((EXT, 128), F32),
        pltpu.VMEM((EXT, 128), F32),
        pltpu.VMEM((OWN_CHUNKS, EXT, 128), F32),
    ]
    padded, plain = STEP + 2, STEP
    shapes += [field(n) for n in (padded, padded, padded, plain, padded, plain, padded, plain, padded, padded, plain)]
    for level in range(1, GRIDS):
        n = STEP >> level
        shapes += [field(m) for m in (n, n + 2, n, n, n + 2, n)]
    shapes += [
        pltpu.VMEM((SUB, WIDTH), F32),
        pltpu.VMEM((COLS, 128), F32),
        pltpu.VMEM((PAD, WIDTH), F32),
        pltpu.VMEM((2, R, 8, 128), F32),
        pltpu.VMEM((2, C, 2, FREQ), F32),
        pltpu.VMEM((2, 2, 4, FREQ), F32),
        pltpu.VMEM((2, 4, FREQ), F32),
        pltpu.VMEM((2, 4, FREQ), F32),
        pltpu.VMEM((PAD, FREQ), F32),
        pltpu.VMEM((4, CCOLS, FREQ), F32),
        pltpu.VMEM((2, C, 2, FREQ), F32),
        pltpu.SemaphoreType.DMA((6,)),
        pltpu.SemaphoreType.DMA((8,)),
        pltpu.SemaphoreType.DMA((8,)),
        pltpu.SemaphoreType.DMA((2, R - 1)),
        pltpu.SemaphoreType.DMA((2, R - 1)),
        pltpu.SemaphoreType.DMA((2, C - 1)),
        pltpu.SemaphoreType.DMA((2, C - 1)),
        pltpu.SemaphoreType.DMA((2, 2)),
        pltpu.SemaphoreType.DMA((2, 2)),
        pltpu.SemaphoreType.DMA((OWN_CHUNKS,)),
    ]
    return shapes


def solution(mesh):
    R, C = mesh.shape["row"], mesh.shape["col"]
    forward, backward, constants = tables(CROWS * R, CCOLS * C)

    def body(swath, coherence, counts):
        return pl.pallas_call(
            functools.partial(kernel, R, C),
            out_shape=jax.ShapeDtypeStruct((ROWS, COLS), F32),
            in_specs=[pl.BlockSpec(memory_space=pl.ANY)] * 6,
            out_specs=pl.BlockSpec(memory_space=pl.ANY),
            scratch_shapes=scratch(R, C),
            compiler_params=pltpu.CompilerParams(
                collective_id=0, has_side_effects=True, vmem_limit_bytes=48 * 1024 * 1024
            ),
        )(swath, coherence, counts, jnp.asarray(forward), jnp.asarray(backward), jnp.asarray(constants))

    return jax.shard_map(
        body,
        mesh=mesh,
        in_specs=(P("row", "col"), P("row", "col"), P("row", "col")),
        out_specs=P("row", "col"),
        check_vma=False,
    )
```

```python
import functools

import jax
import jax.numpy as jnp
import numpy as np
from jax import lax
from jax.experimental import pallas as pl
from jax.experimental.pallas import tpu as pltpu
from jax.sharding import PartitionSpec as P

MESH = pl.DeviceIdType.MESH
HIGHEST = lax.Precision.HIGHEST
F32 = jnp.float32

GRIDS = 4
NCLASS = 8
LEVELS = 256
DAMPING = 0.8
DIAG_FLOOR = 0.5
TURN = 2.0 * np.pi
ERROR_FLOOR = 0.5
EPSILON = 1e-6
SCREEN_WIDTH = 4.0

STEP = 2**GRIDS
HALO = 48
ROWS = 160
COLS = 512
CROWS = ROWS // STEP
CCOLS = COLS // STEP
EXT = ROWS + 2 * HALO
SUB = EXT // STEP
OWN_CHUNKS = COLS // 128
CHUNKS = OWN_CHUNKS + 1
WIDTH = CHUNKS * 128
FREQ = 256
PAD = 48
SHIFTS = (1, 2, 4, 8, 16, 32)
UNROLL = 8
HALVES = tuple(slice(h, h + 8) for h in range(0, SUB, 8))


def tables(rows, cols):
    devices = rows // CROWS
    freq = np.arange(rows)[:, None]
    cosine = np.cos(np.pi * (np.arange(rows)[None, :] + 0.5) * freq / rows) * np.sqrt(2.0 / rows)
    cosine[0] *= np.sqrt(0.5)
    forward = np.zeros((2, devices, 8, FREQ))
    backward = np.zeros((devices, SUB, FREQ))
    for d in range(devices):
        for k in range(CROWS):
            forward[k // 8, d, k % 8, :rows] = cosine[:, d * CROWS + k]
        for k in range(SUB):
            place = d * CROWS + (k if k < CROWS + HALO // STEP else k - SUB)
            if 0 <= place < rows:
                backward[d, k, :rows] = cosine[:, place]
    shift = 2.0 - 2.0 * np.cos(np.pi * np.arange(rows) / rows) + (SCREEN_WIDTH / cols) ** 2
    theta = 2.0 * np.arcsinh(np.sqrt(shift) / 2.0)
    constants = np.zeros((16, FREQ))
    constants[0] = 1.0
    constants[0, :rows] = theta
    constants[1, :rows] = 1.0 / (2.0 * np.sinh(theta))
    constants[2] = 1.0
    constants[2, :rows] = 1.0 / (1.0 - np.exp(-2.0 * cols * theta))
    for i, s in enumerate(SHIFTS):
        constants[3 + i] = np.exp(-s * constants[0])
    return (
        forward.reshape(2, devices * 8, FREQ).astype(np.float32),
        backward.astype(np.float32),
        constants.astype(np.float32),
    )


def ahead(x, s):
    return pltpu.roll(x, WIDTH - s, 1)


def behind(x, s):
    return pltpu.roll(x, s, 1)


def wrap(ref, above=True, below=True):
    last = ref.shape[0] - 2
    if above:
        ref[0] = pltpu.roll(ref[last], 1, 0)
    if below:
        ref[last + 1] = pltpu.roll(ref[1], SUB - 1, 0)


def steps(count, body):
    if count <= UNROLL:
        for i in range(count):
            body(i)
    else:

        def step(i, carry):
            for j in range(UNROLL):
                body(i * UNROLL + j)
            return carry

        lax.fori_loop(0, count // UNROLL, step, 0)


def kernel(R, C, *refs):
    (
        swath_h,
        coherence_h,
        counts_h,
        forward_h,
        backward_h,
        constants_h,
        out_h,
        swath,
        coherence,
        counts,
        forward,
        backward,
        constants,
        nat,
        left_pack,
        right_pack,
        from_left,
        from_right,
        result,
        qual,
        phase,
        wd,
        wr,
        sd,
        sr,
        v0,
        rdiv0,
        first,
        gd,
        gr,
        *rest,
    ) = refs
    levels = []
    for _ in range(3):
        levels.append(rest[:6])
        rest = rest[6:]
    (
        coarse,
        select,
        spread,
        blocks,
        amps,
        near_send,
        near_left,
        near_right,
        ext,
        powers,
        coef,
        load_sem,
        p1_send,
        p1_recv,
        p2_send,
        p2_recv,
        p3_send,
        p3_recv,
        nb_send,
        nb_recv,
        out_sem,
    ) = rest

    r = lax.axis_index("row")
    c = lax.axis_index("col")
    N = CCOLS * C

    loads = [
        pltpu.make_async_copy(swath_h, swath, load_sem.at[0]),
        pltpu.make_async_copy(coherence_h, coherence, load_sem.at[1]),
        pltpu.make_async_copy(counts_h, counts, load_sem.at[2]),
        pltpu.make_async_copy(constants_h, constants, load_sem.at[3]),
        pltpu.make_async_copy(forward_h, forward, load_sem.at[4]),
        pltpu.make_async_copy(backward_h.at[r], backward, load_sem.at[5]),
    ]
    for copy in loads:
        copy.start()

    for a in range(2):
        for k in range(OWN_CHUNKS):
            nat[a, k, ROWS:EXT, :] = jnp.zeros((EXT - ROWS, 128), F32)
    from_left[...] = jnp.zeros((EXT, 128), F32)
    from_right[...] = jnp.zeros((EXT, 128), F32)
    near_left[...] = jnp.zeros(near_left.shape, F32)
    near_right[...] = jnp.zeros(near_right.shape, F32)

    barrier = pltpu.get_barrier_semaphore()
    for i in range(1, R):
        pl.semaphore_signal(barrier, inc=1, device_id=(lax.rem(r + i, R), c), device_id_type=MESH)
    for i in range(1, C):
        pl.semaphore_signal(barrier, inc=1, device_id=(r, lax.rem(c + i, C)), device_id_type=MESH)
    for i in (1, R - 1):
        for j in (1, C - 1):
            pl.semaphore_signal(
                barrier, inc=1, device_id=(lax.rem(r + i, R), lax.rem(c + j, C)), device_id_type=MESH
            )

    for copy in loads[:3]:
        copy.wait()
    lane = lax.broadcasted_iota(jnp.int32, (32, 128), 1)

    def prepare(i):
        rows = pl.ds(pl.multiple_of(i * 32, 32), 32)
        for k in range(OWN_CHUNKS):
            span = slice(128 * k, 128 * k + 128)
            level = coherence[rows, span].astype(F32) * (1.0 / (NCLASS - 1))
            q = swath[rows, span].astype(F32) * (level * level)
            ph = counts[rows, span].astype(F32) * (1.0 / LEVELS)
            nat[0, k, rows, :] = q
            nat[1, k, rows, :] = ph
            if k == 0:
                left_pack[rows, :] = jnp.where(lane < 64, q, pltpu.roll(ph, 64, 1))
            if k == OWN_CHUNKS - 1:
                right_pack[rows, :] = jnp.where(lane < 64, pltpu.roll(ph, 64, 1), q)

    steps(ROWS // 32, prepare)
    pl.semaphore_wait(barrier, R + C + 2)

    top, bottom = slice(0, HALO), slice(ROWS - HALO, ROWS)
    own, below, above = slice(0, ROWS), slice(ROWS, ROWS + HALO), slice(ROWS + HALO, EXT)
    chunks = slice(0, OWN_CHUNKS)
    is_up, is_down = r > 0, r < R - 1
    is_left, is_right = c > 0, c < C - 1
    both = jnp.logical_and
    plan = [
        (is_up, -1, 0, nat.at[:, chunks, top, :], nat.at[:, chunks, below, :], is_down),
        (is_down, 1, 0, nat.at[:, chunks, bottom, :], nat.at[:, chunks, above, :], is_up),
        (is_left, 0, -1, left_pack, from_right.at[own], is_right),
        (is_right, 0, 1, right_pack, from_left.at[own], is_left),
        (both(is_up, is_left), -1, -1, left_pack.at[top], from_right.at[below], both(is_down, is_right)),
        (both(is_down, is_left), 1, -1, left_pack.at[bottom], from_right.at[above], both(is_up, is_right)),
        (both(is_up, is_right), -1, 1, right_pack.at[top], from_left.at[below], both(is_down, is_left)),
        (both(is_down, is_right), 1, 1, right_pack.at[bottom], from_left.at[above], both(is_up, is_left)),
    ]
    halo_copies = []
    for i, (sends, dr, dc, source, target, receives) in enumerate(plan):
        copy = pltpu.make_async_remote_copy(
            src_ref=source,
            dst_ref=target,
            send_sem=p1_send.at[i],
            recv_sem=p1_recv.at[i],
            device_id=(lax.rem(r + dr + R, R), lax.rem(c + dc + C, C)),
            device_id_type=MESH,
        )
        halo_copies.append((sends, receives, copy))
        pl.when(sends)(copy.start)

    for copy in loads[3:]:
        copy.wait()
    theta = constants[0:1, :]
    green = constants[1:2, :]
    inverse = constants[2:3, :]
    yy = lax.broadcasted_iota(jnp.int32, (CCOLS, FREQ), 0)
    last = CCOLS - 1
    powers[0] = jnp.exp(-theta * (last - yy).astype(F32))
    powers[1] = jnp.exp(-theta * yy.astype(F32))
    powers[2] = jnp.where(yy <= last - 3, jnp.exp(-theta * jnp.maximum(last - 3 - yy, 0).astype(F32)), 0.0)
    powers[3] = jnp.where(yy >= 3, jnp.exp(-theta * jnp.maximum(yy - 3, 0).astype(F32)), 0.0)

    def decay(n):
        return jnp.exp(-theta * n.astype(F32))

    def directly(n, inside):
        return jnp.where(inside, decay(jnp.maximum(n, 0)), 0.0)

    for i in range(C):
        rev = C - 1 - i
        coef[0, i, 0:1, :] = directly(CCOLS * (c - 1 - i) - 3, i < c - 1) + inverse * decay(
            N + CCOLS * rev + CCOLS * c - 3
        )
        coef[0, i, 1:2, :] = inverse * decay(CCOLS * i + CCOLS * c - 3)
        coef[1, i, 0:1, :] = inverse * decay(CCOLS * (C - 1 - c) + CCOLS * rev - 3)
        coef[1, i, 1:2, :] = directly(CCOLS * (i - c - 1) - 3, i > c + 1) + inverse * decay(
            2 * N - CCOLS * (c + 1) + CCOLS * i - 3
        )
    at = lax.broadcasted_iota(jnp.int32, (COLS, 128), 0)
    to = lax.broadcasted_iota(jnp.int32, (COLS, 128), 1)
    select[...] = jnp.where((to < 64) & (at == STEP * (to & 31)), 1.0, 0.0).astype(F32)
    at = lax.broadcasted_iota(jnp.int32, (PAD, WIDTH), 0)
    to = lax.broadcasted_iota(jnp.int32, (PAD, WIDTH), 1) >> GRIDS
    spread[...] = jnp.where(at == jnp.where(to < CCOLS + 3, to + 8, to + 8 - WIDTH // STEP), 1.0, 0.0).astype(F32)
    ext[...] = jnp.zeros((PAD, FREQ), F32)

    for _, receives, copy in halo_copies:
        pl.when(receives)(copy.wait_recv)

    lane = lax.broadcasted_iota(jnp.int32, (SUB, 128), 1)
    for p in range(STEP):
        rows = pl.ds(p, SUB, stride=STEP)
        for k in range(OWN_CHUNKS):
            span = slice(128 * k, 128 * k + 128)
            qual[p + 1, :, span] = nat.at[0, k][rows, :]
            phase[p + 1, :, span] = nat.at[1, k][rows, :]
        a, b = from_right[rows, :], from_left[rows, :]
        qual[p + 1, :, COLS:WIDTH] = jnp.where(lane < 64, a, b)
        phase[p + 1, :, COLS:WIDTH] = pltpu.roll(jnp.where(lane < 64, b, a), 64, 1)
    wrap(qual, above=False)
    wrap(phase, above=False)

    def steep(u):
        return u - jnp.floor(u + 0.5)

    def make_faces(p):
        for h in HALVES:
            q, ph = qual[p + 1, h], phase[p + 1, h]
            wd[p + 1, h] = jnp.minimum(q, qual[p + 2, h])
            wr[p, h] = jnp.minimum(q, ahead(q, 1))
            sd[p + 1, h] = steep(phase[p + 2, h] - ph)
            sr[p, h] = steep(ahead(ph, 1) - ph)

    steps(STEP, make_faces)
    wrap(wd, below=False)
    wrap(sd, below=False)

    def start_first(p):
        for h in HALVES:
            a, au, b = wd[p + 1, h], wd[p, h], wr[p, h]
            fr = b * sr[p, h]
            source = au * sd[p, h] - a * sd[p + 1, h] + behind(fr, 1) - fr
            rdiv = DAMPING / jnp.maximum(a + au + b + behind(b, 1), DIAG_FLOOR)
            rdiv0[p, h] = rdiv
            v0[p + 1, h] = source * rdiv

    steps(STEP, start_first)
    wrap(v0)

    def restrict_fine():
        src, a1, b1 = levels[0][0], levels[0][1], levels[0][2]

        def body(i):
            for h in HALVES:
                va, v1, v2, vb = v0[2 * i, h], v0[2 * i + 1, h], v0[2 * i + 2, h], v0[2 * i + 3, h]
                a_odd = wd[2 * i + 2, h]
                y = a_odd * (vb - v2 - sd[2 * i + 2, h]) - wd[2 * i, h] * (v1 - va - sd[2 * i, h])
                b0, b_odd = wr[2 * i, h], wr[2 * i + 1, h]
                g = b0 * (ahead(v1, 1) - v1 - sr[2 * i, h]) + b_odd * (ahead(v2, 1) - v2 - sr[2 * i + 1, h])
                src[i, h] = y + ahead(y + g, 1) - behind(g, 1)
                a1[i + 1, h] = a_odd + ahead(a_odd, 1)
                b1[i, h] = ahead(b0 + b_odd, 1)

        steps(STEP // 2, body)
        wrap(a1, below=False)

    def down(level):
        s = 2**level
        count = STEP // s
        src, a, b, rdiv, v, _ = levels[level - 1]

        def smooth(p):
            for h in HALVES:
                bb = b[p, h]
                d = DAMPING / jnp.maximum(a[p + 1, h] + a[p, h] + bb + behind(bb, s), DIAG_FLOOR)
                rdiv[p, h] = d
                v[p + 1, h] = src[p, h] * d

        steps(count, smooth)
        wrap(v)
        if level < GRIDS - 1:
            src_n, a_n, b_n = levels[level][0], levels[level][1], levels[level][2]
        else:
            src_n, a_n, b_n = None, None, None

        def body(i):
            for h in HALVES:
                va, v1, v2, vb = v[2 * i, h], v[2 * i + 1, h], v[2 * i + 2, h], v[2 * i + 3, h]
                a_odd = a[2 * i + 2, h]
                t = src[2 * i, h] + src[2 * i + 1, h] + a_odd * (vb - v2) - a[2 * i, h] * (v1 - va)
                b0, b_odd = b[2 * i, h], b[2 * i + 1, h]
                g = b0 * (ahead(v1, s) - v1) + b_odd * (ahead(v2, s) - v2)
                out = t + ahead(t + g, s) - behind(g, s)
                if src_n is None:
                    coarse[h] = out
                else:
                    src_n[i, h] = out
                    a_n[i + 1, h] = a_odd + ahead(a_odd, s)
                    b_n[i, h] = ahead(b0 + b_odd, s)

        steps(count // 2, body)
        if a_n is not None:
            wrap(a_n, below=False)

    def up(level):
        s = 2**level
        count = STEP // s
        src, a, b, rdiv, v, out = levels[level - 1]

        def add(i):
            for h in HALVES:
                if level == GRIDS - 1:
                    x = coarse[h]
                else:
                    x = levels[level][5][i, h]
                    column = lax.broadcasted_iota(jnp.int32, x.shape, 1)
                    x = jnp.where((column & s) == 0, x, behind(x, s))
                v[2 * i + 1, h] = v[2 * i + 1, h] + x
                v[2 * i + 2, h] = v[2 * i + 2, h] + x

        steps(count // 2, add)
        wrap(v)

        def smooth(i):
            for h in HALVES:
                va, v1, v2, vb = v[2 * i, h], v[2 * i + 1, h], v[2 * i + 2, h], v[2 * i + 3, h]
                g0 = a[2 * i, h] * (v1 - va)
                g1 = a[2 * i + 1, h] * (v2 - v1)
                g2 = a[2 * i + 2, h] * (vb - v2)
                f1 = b[2 * i, h] * (ahead(v1, s) - v1)
                f2 = b[2 * i + 1, h] * (ahead(v2, s) - v2)
                out[2 * i, h] = v1 + (src[2 * i, h] + g1 - g0 + f1 - behind(f1, s)) * rdiv[2 * i, h]
                out[2 * i + 1, h] = v2 + (src[2 * i + 1, h] + g2 - g1 + f2 - behind(f2, s)) * rdiv[2 * i + 1, h]

        steps(count // 2, smooth)

    def up_fine():
        def add(i):
            for h in HALVES:
                x = levels[0][5][i, h]
                column = lax.broadcasted_iota(jnp.int32, x.shape, 1)
                x = jnp.where((column & 1) == 0, x, behind(x, 1))
                v0[2 * i + 1, h] = v0[2 * i + 1, h] + x
                v0[2 * i + 2, h] = v0[2 * i + 2, h] + x

        steps(STEP // 2, add)
        wrap(v0)

        def smooth(i):
            for h in HALVES:
                va, v1, v2, vb = v0[2 * i, h], v0[2 * i + 1, h], v0[2 * i + 2, h], v0[2 * i + 3, h]
                g0 = wd[2 * i, h] * (v1 - va - sd[2 * i, h])
                g1 = wd[2 * i + 1, h] * (v2 - v1 - sd[2 * i + 1, h])
                g2 = wd[2 * i + 2, h] * (vb - v2 - sd[2 * i + 2, h])
                f1 = wr[2 * i, h] * (ahead(v1, 1) - v1 - sr[2 * i, h])
                f2 = wr[2 * i + 1, h] * (ahead(v2, 1) - v2 - sr[2 * i + 1, h])
                first[2 * i + 1, h] = v1 + (g1 - g0 + f1 - behind(f1, 1)) * rdiv0[2 * i, h]
                first[2 * i + 2, h] = v2 + (g2 - g1 + f2 - behind(f2, 1)) * rdiv0[2 * i + 1, h]

        steps(STEP // 2, smooth)

    def coarse_solve(turn):
        _, a3, b3, _, _, _ = levels[2]
        column = lax.broadcasted_iota(jnp.int32, (SUB, COLS), 1)
        line = lax.broadcasted_iota(jnp.int32, (SUB, COLS), 0)
        here = slice(0, COLS)
        part = jnp.where((column & 7) == 0, a3[2, :, here], 0.0) + jnp.where(
            (column & 15) == 8, b3[0, :, here] + b3[1, :, here], 0.0
        )
        part = jnp.where((line < CROWS) & ((column & 7) == 0), part, 0.0)
        local = jnp.sum(jnp.sum(part, axis=1, keepdims=True), axis=0, keepdims=True)
        mine = jnp.dot(coarse[:, here], select[...], precision=HIGHEST, preferred_element_type=F32)
        spot = lax.broadcasted_iota(jnp.int32, (8, 128), 1)
        blocks[turn, r] = jnp.where(spot < 32, mine[0:8], jnp.where(spot < 64, mine[8:16], local))
        copies = []
        for i in range(1, R):
            copy = pltpu.make_async_remote_copy(
                src_ref=blocks.at[turn, r],
                dst_ref=blocks.at[turn, r],
                send_sem=p2_send.at[turn, i - 1],
                recv_sem=p2_recv.at[turn, i - 1],
                device_id=(lax.rem(r + i, R), c),
                device_id_type=MESH,
            )
            copy.start()
            copies.append(copy)
        for copy in copies:
            copy.wait_recv()
        every = blocks[turn].reshape(R * 8, 128).T
        hat = jnp.dot(every[0:32], forward[0], precision=HIGHEST, preferred_element_type=F32) + jnp.dot(
            every[32:64], forward[1], precision=HIGHEST, preferred_element_type=F32
        )
        rows_sum = jnp.sum(every[64:65], axis=1, keepdims=True) * 0.125

        def total(n):
            return jnp.sum(powers[n] * hat, axis=0, keepdims=True)

        mode = lax.broadcasted_iota(jnp.int32, (1, FREQ), 1)
        amps[turn, c, 0:1, :] = jnp.where(mode < CROWS * R, total(0), rows_sum)
        amps[turn, c, 1:2, :] = total(1)
        near_send[turn, 0, 0:1, :] = total(2)
        near_send[turn, 0, 1:4, :] = hat[CCOLS - 3 : CCOLS]
        near_send[turn, 1, 0:3, :] = hat[0:3]
        near_send[turn, 1, 3:4, :] = total(3)
        for i in range(1, C):
            copy = pltpu.make_async_remote_copy(
                src_ref=amps.at[turn, c],
                dst_ref=amps.at[turn, c],
                send_sem=p3_send.at[turn, i - 1],
                recv_sem=p3_recv.at[turn, i - 1],
                device_id=(r, lax.rem(c + i, C)),
                device_id_type=MESH,
            )
            copy.start()
            copies.append(copy)
        rightward = pltpu.make_async_remote_copy(
            src_ref=near_send.at[turn, 0],
            dst_ref=near_left.at[turn],
            send_sem=nb_send.at[turn, 0],
            recv_sem=nb_recv.at[turn, 0],
            device_id=(r, lax.rem(c + 1, C)),
            device_id_type=MESH,
        )
        leftward = pltpu.make_async_remote_copy(
            src_ref=near_send.at[turn, 1],
            dst_ref=near_right.at[turn],
            send_sem=nb_send.at[turn, 1],
            recv_sem=nb_recv.at[turn, 1],
            device_id=(r, lax.rem(c + C - 1, C)),
            device_id_type=MESH,
        )
        pl.when(is_right)(rightward.start)
        pl.when(is_left)(leftward.start)
        pl.when(is_left)(rightward.wait_recv)
        pl.when(is_right)(leftward.wait_recv)
        for copy in copies[R - 1 :]:
            copy.wait_recv()
        into_left = jnp.zeros((2, FREQ), F32)
        into_right = jnp.zeros((2, FREQ), F32)
        weight = jnp.zeros((2, FREQ), F32)
        for i in range(C):
            x = amps[turn, i]
            into_left += coef[0, i] * x
            into_right += coef[1, i] * x
            weight += x
        into_left = into_left[0:1] + into_left[1:2]
        into_right = into_right[0:1] + into_right[1:2]
        weight = jnp.sum(jnp.where(mode == FREQ - 1, weight[0:1], 0.0), axis=1, keepdims=True)
        grid_rows, grid_cols = CROWS * R, CCOLS * C
        mean = weight * (1.0 / ((grid_rows - 1) * grid_cols + grid_rows * (grid_cols - 1))) + EPSILON
        ext[4:8, :] = near_left[turn]
        ext[4:5, :] = near_left[turn, 0:1, :] + into_left
        ext[8 : 8 + CCOLS, :] = hat
        ext[8 + CCOLS : 12 + CCOLS, :] = near_right[turn]
        ext[11 + CCOLS : 12 + CCOLS, :] = near_right[turn, 3:4, :] + into_right
        hats = ext[...]
        place = lax.broadcasted_iota(jnp.int32, (PAD, FREQ), 0)
        going_right = hats
        going_left = hats
        for i, s in enumerate(SHIFTS):
            q = constants[3 + i : 4 + i, :]
            going_right += q * jnp.where(place >= s, pltpu.roll(going_right, s, 0), 0.0)
            going_left += q * jnp.where(place < PAD - s, pltpu.roll(going_left, PAD - s, 0), 0.0)
        modes = (going_right + going_left - hats) * (green / mean)
        values = lax.dot_general(
            backward[...], modes, (((1,), (1,)), ((), ())), precision=HIGHEST, preferred_element_type=F32
        )
        coarse[...] = jnp.dot(values, spread[...], precision=HIGHEST, preferred_element_type=F32)
        return copies, rightward, leftward

    def cycle(turn):
        restrict_fine()
        for level in range(1, GRIDS):
            down(level)
        sent = coarse_solve(turn)
        for level in range(GRIDS - 1, 0, -1):
            up(level)
        up_fine()
        return sent

    sent = [cycle(0)]
    wrap(first)

    def reweight(p):
        for h in HALVES:
            f = first[p + 1, h]
            e = first[p + 2, h] - f - sd[p + 1, h]
            a = wd[p + 1, h] / jnp.maximum(jnp.abs(e) * TURN, ERROR_FLOOR)
            wd[p + 1, h] = a
            gd[p + 1, h] = a * e
            e = ahead(f, 1) - f - sr[p, h]
            b = wr[p, h] / jnp.maximum(jnp.abs(e) * TURN, ERROR_FLOOR)
            wr[p, h] = b
            gr[p, h] = b * e

    steps(STEP, reweight)
    wrap(wd, below=False)
    wrap(gd, below=False)

    def start_second(p):
        for h in HALVES:
            b, f = wr[p, h], gr[p, h]
            rdiv = DAMPING / jnp.maximum(wd[p + 1, h] + wd[p, h] + b + behind(b, 1), DIAG_FLOOR)
            rdiv0[p, h] = rdiv
            v0[p + 1, h] = first[p + 1, h] + (gd[p + 1, h] - gd[p, h] + f - behind(f, 1)) * rdiv

    steps(STEP, start_second)
    wrap(v0)
    sent.append(cycle(1))

    outs = []
    for k in range(OWN_CHUNKS):
        span = slice(128 * k, 128 * k + 128)
        for p in range(STEP):
            result.at[k][pl.ds(p, SUB, stride=STEP), :] = first[p + 1, :, span] * TURN
        copy = pltpu.make_async_copy(result.at[k, own, :], out_h.at[:, span], out_sem.at[k])
        copy.start()
        outs.append(copy)
    for sends, _, copy in halo_copies:
        pl.when(sends)(copy.wait_send)
    for copies, rightward, leftward in sent:
        for copy in copies:
            copy.wait_send()
        pl.when(is_right)(rightward.wait_send)
        pl.when(is_left)(leftward.wait_send)
    for copy in outs:
        copy.wait()


def scratch(R, C):
    def field(count):
        return pltpu.VMEM((count, SUB, WIDTH), F32)

    shapes = [
        pltpu.VMEM((ROWS, COLS), jnp.int32),
        pltpu.VMEM((ROWS, COLS), jnp.int32),
        pltpu.VMEM((ROWS, COLS), jnp.int32),
        pltpu.VMEM((2, R * 8, FREQ), F32),
        pltpu.VMEM((SUB, FREQ), F32),
        pltpu.VMEM((16, FREQ), F32),
        pltpu.VMEM((2, OWN_CHUNKS, EXT, 128), F32),
        pltpu.VMEM((ROWS, 128), F32),
        pltpu.VMEM((ROWS, 128), F32),
        pltpu.VMEM((EXT, 128), F32),
        pltpu.VMEM((EXT, 128), F32),
        pltpu.VMEM((OWN_CHUNKS, EXT, 128), F32),
    ]
    padded, plain = STEP + 2, STEP
    shapes += [field(n) for n in (padded, padded, padded, plain, padded, plain, padded, plain, padded, padded, plain)]
    for level in range(1, GRIDS):
        n = STEP >> level
        shapes += [field(m) for m in (n, n + 2, n, n, n + 2, n)]
    shapes += [
        pltpu.VMEM((SUB, WIDTH), F32),
        pltpu.VMEM((COLS, 128), F32),
        pltpu.VMEM((PAD, WIDTH), F32),
        pltpu.VMEM((2, R, 8, 128), F32),
        pltpu.VMEM((2, C, 2, FREQ), F32),
        pltpu.VMEM((2, 2, 4, FREQ), F32),
        pltpu.VMEM((2, 4, FREQ), F32),
        pltpu.VMEM((2, 4, FREQ), F32),
        pltpu.VMEM((PAD, FREQ), F32),
        pltpu.VMEM((4, CCOLS, FREQ), F32),
        pltpu.VMEM((2, C, 2, FREQ), F32),
        pltpu.SemaphoreType.DMA((6,)),
        pltpu.SemaphoreType.DMA((8,)),
        pltpu.SemaphoreType.DMA((8,)),
        pltpu.SemaphoreType.DMA((2, R - 1)),
        pltpu.SemaphoreType.DMA((2, R - 1)),
        pltpu.SemaphoreType.DMA((2, C - 1)),
        pltpu.SemaphoreType.DMA((2, C - 1)),
        pltpu.SemaphoreType.DMA((2, 2)),
        pltpu.SemaphoreType.DMA((2, 2)),
        pltpu.SemaphoreType.DMA((OWN_CHUNKS,)),
    ]
    return shapes


def solution(mesh):
    R, C = mesh.shape["row"], mesh.shape["col"]
    forward, backward, constants = tables(CROWS * R, CCOLS * C)

    def body(swath, coherence, counts):
        return pl.pallas_call(
            functools.partial(kernel, R, C),
            out_shape=jax.ShapeDtypeStruct((ROWS, COLS), F32),
            in_specs=[pl.BlockSpec(memory_space=pl.ANY)] * 6,
            out_specs=pl.BlockSpec(memory_space=pl.ANY),
            scratch_shapes=scratch(R, C),
            compiler_params=pltpu.CompilerParams(
                collective_id=0, has_side_effects=True
            ),
        )(swath, coherence, counts, jnp.asarray(forward), jnp.asarray(backward), jnp.asarray(constants))

    return jax.shard_map(
        body,
        mesh=mesh,
        in_specs=(P("row", "col"), P("row", "col"), P("row", "col")),
        out_specs=P("row", "col"),
        check_vma=False,
    )
```

```python
import functools

import jax
import jax.numpy as jnp
import numpy as np
from jax import lax
from jax.experimental import pallas as pl
from jax.experimental.pallas import tpu as pltpu
from jax.sharding import PartitionSpec as P

MESH = pl.DeviceIdType.MESH
HIGHEST = lax.Precision.HIGHEST
F32 = jnp.float32

GRIDS = 4
NCLASS = 8
LEVELS = 256
DAMPING = 0.8
DIAG_FLOOR = 0.5
TURN = 2.0 * np.pi
ERROR_FLOOR = 0.5
EPSILON = 1e-6
SCREEN_WIDTH = 4.0

STEP = 2**GRIDS
HALO = 48
NEAR = 16
ROWS = 160
COLS = 512
CROWS = ROWS // STEP
CCOLS = COLS // STEP
EXT = ROWS + 2 * HALO
SUB = EXT // STEP
OWN_CHUNKS = COLS // 128
CHUNKS = OWN_CHUNKS + 1
WIDTH = CHUNKS * 128
FREQ = 256
PAD = 48
SHIFTS = (1, 2, 4, 8, 16, 32)
UNROLL = 8
HALVES = tuple(slice(h, h + 8) for h in range(0, SUB, 8))


def tables(rows, cols):
    devices = rows // CROWS
    freq = np.arange(rows)[:, None]
    cosine = np.cos(np.pi * (np.arange(rows)[None, :] + 0.5) * freq / rows) * np.sqrt(2.0 / rows)
    cosine[0] *= np.sqrt(0.5)
    forward = np.zeros((2, devices, 8, FREQ))
    backward = np.zeros((devices, SUB, FREQ))
    for d in range(devices):
        for k in range(CROWS):
            forward[k // 8, d, k % 8, :rows] = cosine[:, d * CROWS + k]
        for k in range(SUB):
            place = d * CROWS + (k if k < CROWS + HALO // STEP else k - SUB)
            if 0 <= place < rows:
                backward[d, k, :rows] = cosine[:, place]
    shift = 2.0 - 2.0 * np.cos(np.pi * np.arange(rows) / rows) + (SCREEN_WIDTH / cols) ** 2
    theta = 2.0 * np.arcsinh(np.sqrt(shift) / 2.0)
    constants = np.zeros((16, FREQ))
    constants[0] = 1.0
    constants[0, :rows] = theta
    constants[1, :rows] = 1.0 / (2.0 * np.sinh(theta))
    constants[2] = 1.0
    constants[2, :rows] = 1.0 / (1.0 - np.exp(-2.0 * cols * theta))
    for i, s in enumerate(SHIFTS):
        constants[3 + i] = np.exp(-s * constants[0])
    return (
        forward.reshape(2, devices * 8, FREQ).astype(np.float32),
        backward.astype(np.float32),
        constants.astype(np.float32),
    )


def ahead(x, s):
    return pltpu.roll(x, WIDTH - s, 1)


def behind(x, s):
    return pltpu.roll(x, s, 1)


def wrap(ref, above=True, below=True):
    last = ref.shape[0] - 2
    if above:
        ref[0] = pltpu.roll(ref[last], 1, 0)
    if below:
        ref[last + 1] = pltpu.roll(ref[1], SUB - 1, 0)


def steps(count, body):
    if count <= UNROLL:
        for i in range(count):
            body(i)
    else:

        def step(i, carry):
            for j in range(UNROLL):
                body(i * UNROLL + j)
            return carry

        lax.fori_loop(0, count // UNROLL, step, 0)


def kernel(R, C, *refs):
    (
        swath_h,
        coherence_h,
        counts_h,
        forward_h,
        backward_h,
        constants_h,
        out_h,
        swath,
        coherence,
        counts,
        forward,
        backward,
        constants,
        nat,
        left_pack,
        right_pack,
        near_pack,
        near_got,
        in_left,
        in_right,
        outer,
        from_left,
        from_right,
        result,
        qual,
        phase,
        wd,
        wr,
        sd,
        sr,
        v0,
        rdiv0,
        first,
        gd,
        gr,
        *rest,
    ) = refs
    levels = []
    for _ in range(3):
        levels.append(rest[:6])
        rest = rest[6:]
    (
        coarse,
        select,
        spread,
        blocks,
        amps,
        near_send,
        near_left,
        near_right,
        ext,
        powers,
        coef,
        load_sem,
        p1_send,
        p1_recv,
        p2_send,
        p2_recv,
        p3_send,
        p3_recv,
        nb_send,
        nb_recv,
        out_sem,
    ) = rest

    r = lax.axis_index("row")
    c = lax.axis_index("col")
    N = CCOLS * C

    loads = [
        pltpu.make_async_copy(swath_h, swath, load_sem.at[0]),
        pltpu.make_async_copy(coherence_h, coherence, load_sem.at[1]),
        pltpu.make_async_copy(counts_h, counts, load_sem.at[2]),
        pltpu.make_async_copy(constants_h, constants, load_sem.at[3]),
        pltpu.make_async_copy(forward_h, forward, load_sem.at[4]),
        pltpu.make_async_copy(backward_h.at[r], backward, load_sem.at[5]),
    ]
    for copy in loads:
        copy.start()

    barrier = pltpu.get_barrier_semaphore()
    for i in sorted(range(1, C), key=lambda i: -min(i, C - i)):
        pl.semaphore_signal(barrier, inc=1, device_id=(r, lax.rem(c + i, C)), device_id_type=MESH)
    for i in (1, R - 1):
        for j in (1, C - 1):
            pl.semaphore_signal(
                barrier, inc=1, device_id=(lax.rem(r + i, R), lax.rem(c + j, C)), device_id_type=MESH
            )
    for i in range(1, R):
        pl.semaphore_signal(barrier, inc=1, device_id=(lax.rem(r + i, R), c), device_id_type=MESH)

    is_up, is_down = r > 0, r < R - 1
    is_left, is_right = c > 0, c < C - 1
    chunks = slice(0, OWN_CHUNKS)
    own, below, above = slice(0, ROWS), slice(ROWS, ROWS + HALO), slice(ROWS + HALO, EXT)
    near_below, near_above = slice(ROWS, ROWS + NEAR), slice(EXT - NEAR, EXT)
    far = slice(ROWS + NEAR, EXT - NEAR)
    far_rows = EXT - ROWS - 2 * NEAR
    far_below, far_above = slice(0, far_rows // 2), slice(far_rows // 2, far_rows)

    def clear(ref, *where):
        ref[where] = jnp.zeros(ref.at[where].shape, F32)

    every = slice(None)
    clear(nat, every, chunks, far)
    clear(in_left, far)
    clear(in_right, far)

    @pl.when(jnp.logical_not(is_down))
    def _():
        clear(nat, every, chunks, near_below)
        clear(outer, every, chunks, far_below)
        for ref in (in_left, in_right):
            clear(ref, near_below)
        for ref in (from_left, from_right):
            clear(ref, below)

    @pl.when(jnp.logical_not(is_up))
    def _():
        clear(nat, every, chunks, near_above)
        clear(outer, every, chunks, far_above)
        for ref in (in_left, in_right):
            clear(ref, near_above)
        for ref in (from_left, from_right):
            clear(ref, above)

    @pl.when(jnp.logical_not(is_right))
    def _():
        clear(near_got, 0)
        clear(in_right, near_below)
        clear(in_right, near_above)
        clear(from_right, slice(0, EXT))
        clear(near_right, every)

    @pl.when(jnp.logical_not(is_left))
    def _():
        clear(near_got, 1)
        clear(in_left, near_below)
        clear(in_left, near_above)
        clear(from_left, slice(0, EXT))
        clear(near_left, every)

    for copy in loads[:3]:
        copy.wait()
    lane = lax.broadcasted_iota(jnp.int32, (32, 128), 1)

    def prepare(i):
        rows = slice(i * 32, i * 32 + 32)
        for k in range(OWN_CHUNKS):
            span = slice(128 * k, 128 * k + 128)
            level = coherence[rows, span].astype(F32) * (1.0 / (NCLASS - 1))
            q = swath[rows, span].astype(F32) * (level * level)
            ph = counts[rows, span].astype(F32) * (1.0 / LEVELS)
            nat[0, k, rows, :] = q
            nat[1, k, rows, :] = ph
            if k == 0:
                left_pack[rows, :] = jnp.where(lane < 64, q, pltpu.roll(ph, 64, 1))
            if k == OWN_CHUNKS - 1:
                right_pack[rows, :] = jnp.where(lane < 64, pltpu.roll(ph, 64, 1), q)

    for i in range(ROWS // 32):
        prepare(i)
    quarter = ROWS // 4
    lane = lax.broadcasted_iota(jnp.int32, (quarter, 128), 1)
    packed = [jnp.zeros((quarter, 128), F32)] * 2
    for g in range(4):
        rows = slice(quarter * g, quarter * g + quarter)
        turned = (pltpu.roll(left_pack[rows, :], NEAR * g, 1), pltpu.roll(right_pack[rows, :], NEAR * g + 80, 1))
        packed = [jnp.where((lane & 48) == NEAR * g, x, y) for x, y in zip(turned, packed)]
    near_pack[0] = packed[0]
    near_pack[1] = packed[1]
    pl.semaphore_wait(barrier, R + C + 2)

    both = jnp.logical_and
    first_rows, last_rows = slice(0, NEAR), slice(ROWS - NEAR, ROWS)
    top, bottom = slice(0, HALO), slice(ROWS - HALO, ROWS)
    top_far, bottom_far = slice(NEAR, HALO), slice(ROWS - HALO, ROWS - NEAR)
    up_left, down_left = both(is_up, is_left), both(is_down, is_left)
    up_right, down_right = both(is_up, is_right), both(is_down, is_right)
    plan = [
        (is_left, 0, -1, near_pack.at[0], near_got.at[0], is_right),
        (is_right, 0, 1, near_pack.at[1], near_got.at[1], is_left),
        (up_left, -1, -1, left_pack.at[first_rows], in_right.at[near_below], down_right),
        (down_left, 1, -1, left_pack.at[last_rows], in_right.at[near_above], up_right),
        (up_right, -1, 1, right_pack.at[first_rows], in_left.at[near_below], down_left),
        (down_right, 1, 1, right_pack.at[last_rows], in_left.at[near_above], up_left),
        (is_up, -1, 0, nat.at[:, chunks, first_rows, :], nat.at[:, chunks, near_below, :], is_down),
        (is_down, 1, 0, nat.at[:, chunks, last_rows, :], nat.at[:, chunks, near_above, :], is_up),
        (is_left, 0, -1, left_pack, from_right.at[own], is_right),
        (is_right, 0, 1, right_pack, from_left.at[own], is_left),
        (up_left, -1, -1, left_pack.at[top], from_right.at[below], down_right),
        (down_left, 1, -1, left_pack.at[bottom], from_right.at[above], up_right),
        (up_right, -1, 1, right_pack.at[top], from_left.at[below], down_left),
        (down_right, 1, 1, right_pack.at[bottom], from_left.at[above], up_left),
        (is_up, -1, 0, nat.at[:, chunks, top_far, :], outer.at[:, chunks, far_below, :], is_down),
        (is_down, 1, 0, nat.at[:, chunks, bottom_far, :], outer.at[:, chunks, far_above, :], is_up),
    ]
    halo_copies = []
    for i, (sends, dr, dc, source, target, receives) in enumerate(plan):
        copy = pltpu.make_async_remote_copy(
            src_ref=source,
            dst_ref=target,
            send_sem=p1_send.at[i],
            recv_sem=p1_recv.at[i],
            device_id=(lax.rem(r + dr + R, R), lax.rem(c + dc + C, C)),
            device_id_type=MESH,
        )
        halo_copies.append((sends, receives, copy))
        pl.when(sends)(copy.start)

    for copy in loads[3:]:
        copy.wait()
    theta = constants[0:1, :]
    green = constants[1:2, :]
    inverse = constants[2:3, :]
    yy = lax.broadcasted_iota(jnp.int32, (CCOLS, FREQ), 0)
    last = CCOLS - 1
    powers[0] = jnp.exp(-theta * (last - yy).astype(F32))
    powers[1] = jnp.exp(-theta * yy.astype(F32))
    powers[2] = jnp.where(yy <= last - 3, jnp.exp(-theta * jnp.maximum(last - 3 - yy, 0).astype(F32)), 0.0)
    powers[3] = jnp.where(yy >= 3, jnp.exp(-theta * jnp.maximum(yy - 3, 0).astype(F32)), 0.0)

    def decay(n):
        return jnp.exp(-theta * n.astype(F32))

    def directly(n, inside):
        return jnp.where(inside, decay(jnp.maximum(n, 0)), 0.0)

    for i in range(C):
        rev = C - 1 - i
        coef[0, i, 0:1, :] = directly(CCOLS * (c - 1 - i) - 3, i < c - 1) + inverse * decay(
            N + CCOLS * rev + CCOLS * c - 3
        )
        coef[0, i, 1:2, :] = inverse * decay(CCOLS * i + CCOLS * c - 3)
        coef[1, i, 0:1, :] = inverse * decay(CCOLS * (C - 1 - c) + CCOLS * rev - 3)
        coef[1, i, 1:2, :] = directly(CCOLS * (i - c - 1) - 3, i > c + 1) + inverse * decay(
            2 * N - CCOLS * (c + 1) + CCOLS * i - 3
        )
    at = lax.broadcasted_iota(jnp.int32, (COLS, 128), 0)
    to = lax.broadcasted_iota(jnp.int32, (COLS, 128), 1)
    select[...] = jnp.where((to < 64) & (at == STEP * (to & 31)), 1.0, 0.0).astype(F32)
    at = lax.broadcasted_iota(jnp.int32, (PAD, WIDTH), 0)
    to = lax.broadcasted_iota(jnp.int32, (PAD, WIDTH), 1) >> GRIDS
    spread[...] = jnp.where(at == jnp.where(to < CCOLS + 3, to + 8, to + 8 - WIDTH // STEP), 1.0, 0.0).astype(F32)
    ext[...] = jnp.zeros((PAD, FREQ), F32)

    for _, receives, copy in halo_copies[:8]:
        pl.when(receives)(copy.wait_recv)
    lane = lax.broadcasted_iota(jnp.int32, (quarter, 128), 1)
    for g in range(4):
        rows = slice(quarter * g, quarter * g + quarter)
        in_right[rows, :] = jnp.where((lane & 63) < NEAR, pltpu.roll(near_got[0], (128 - NEAR * g) % 128, 1), 0.0)
        in_left[rows, :] = jnp.where((lane & 63) >= 64 - NEAR, pltpu.roll(near_got[1], 48 - NEAR * g, 1), 0.0)

    def arrange(left, right):
        lane = lax.broadcasted_iota(jnp.int32, (SUB, 128), 1)
        for p in range(STEP):
            rows = pl.ds(p, SUB, stride=STEP)
            for k in range(OWN_CHUNKS):
                span = slice(128 * k, 128 * k + 128)
                qual[p + 1, :, span] = nat.at[0, k][rows, :]
                phase[p + 1, :, span] = nat.at[1, k][rows, :]
            a, b = right[rows, :], left[rows, :]
            qual[p + 1, :, COLS:WIDTH] = jnp.where(lane < 64, a, b)
            phase[p + 1, :, COLS:WIDTH] = pltpu.roll(jnp.where(lane < 64, b, a), 64, 1)
        wrap(qual, above=False)
        wrap(phase, above=False)

    def steep(u):
        return u - jnp.floor(u + 0.5)

    def make_faces(p):
        for h in HALVES:
            q, ph = qual[p + 1, h], phase[p + 1, h]
            wd[p + 1, h] = jnp.minimum(q, qual[p + 2, h])
            wr[p, h] = jnp.minimum(q, ahead(q, 1))
            sd[p + 1, h] = steep(phase[p + 2, h] - ph)
            sr[p, h] = steep(ahead(ph, 1) - ph)

    def start_first(p):
        for h in HALVES:
            a, au, b = wd[p + 1, h], wd[p, h], wr[p, h]
            fr = b * sr[p, h]
            source = au * sd[p, h] - a * sd[p + 1, h] + behind(fr, 1) - fr
            rdiv = DAMPING / jnp.maximum(a + au + b + behind(b, 1), DIAG_FLOOR)
            rdiv0[p, h] = rdiv
            v0[p + 1, h] = source * rdiv

    def open_first(left, right):
        arrange(left, right)
        steps(STEP, make_faces)
        wrap(wd, below=False)
        wrap(sd, below=False)
        steps(STEP, start_first)
        wrap(v0)

    def restrict_fine():
        src, a1, b1 = levels[0][0], levels[0][1], levels[0][2]

        def body(i):
            for h in HALVES:
                va, v1, v2, vb = v0[2 * i, h], v0[2 * i + 1, h], v0[2 * i + 2, h], v0[2 * i + 3, h]
                a_odd = wd[2 * i + 2, h]
                y = a_odd * (vb - v2 - sd[2 * i + 2, h]) - wd[2 * i, h] * (v1 - va - sd[2 * i, h])
                b0, b_odd = wr[2 * i, h], wr[2 * i + 1, h]
                g = b0 * (ahead(v1, 1) - v1 - sr[2 * i, h]) + b_odd * (ahead(v2, 1) - v2 - sr[2 * i + 1, h])
                src[i, h] = y + ahead(y + g, 1) - behind(g, 1)
                a1[i + 1, h] = a_odd + ahead(a_odd, 1)
                b1[i, h] = ahead(b0 + b_odd, 1)

        steps(STEP // 2, body)
        wrap(a1, below=False)

    def down(level):
        s = 2**level
        count = STEP // s
        src, a, b, rdiv, v, _ = levels[level - 1]

        def smooth(p):
            for h in HALVES:
                bb = b[p, h]
                d = DAMPING / jnp.maximum(a[p + 1, h] + a[p, h] + bb + behind(bb, s), DIAG_FLOOR)
                rdiv[p, h] = d
                v[p + 1, h] = src[p, h] * d

        steps(count, smooth)
        wrap(v)
        if level < GRIDS - 1:
            src_n, a_n, b_n = levels[level][0], levels[level][1], levels[level][2]
        else:
            src_n, a_n, b_n = None, None, None

        def body(i):
            for h in HALVES:
                va, v1, v2, vb = v[2 * i, h], v[2 * i + 1, h], v[2 * i + 2, h], v[2 * i + 3, h]
                a_odd = a[2 * i + 2, h]
                t = src[2 * i, h] + src[2 * i + 1, h] + a_odd * (vb - v2) - a[2 * i, h] * (v1 - va)
                b0, b_odd = b[2 * i, h], b[2 * i + 1, h]
                g = b0 * (ahead(v1, s) - v1) + b_odd * (ahead(v2, s) - v2)
                out = t + ahead(t + g, s) - behind(g, s)
                if src_n is None:
                    coarse[h] = out
                else:
                    src_n[i, h] = out
                    a_n[i + 1, h] = a_odd + ahead(a_odd, s)
                    b_n[i, h] = ahead(b0 + b_odd, s)

        steps(count // 2, body)
        if a_n is not None:
            wrap(a_n, below=False)

    def up(level):
        s = 2**level
        count = STEP // s
        src, a, b, rdiv, v, out = levels[level - 1]

        def add(i):
            for h in HALVES:
                if level == GRIDS - 1:
                    x = coarse[h]
                else:
                    x = levels[level][5][i, h]
                    column = lax.broadcasted_iota(jnp.int32, x.shape, 1)
                    x = jnp.where((column & s) == 0, x, behind(x, s))
                v[2 * i + 1, h] = v[2 * i + 1, h] + x
                v[2 * i + 2, h] = v[2 * i + 2, h] + x

        steps(count // 2, add)
        wrap(v)

        def smooth(i):
            for h in HALVES:
                va, v1, v2, vb = v[2 * i, h], v[2 * i + 1, h], v[2 * i + 2, h], v[2 * i + 3, h]
                g0 = a[2 * i, h] * (v1 - va)
                g1 = a[2 * i + 1, h] * (v2 - v1)
                g2 = a[2 * i + 2, h] * (vb - v2)
                f1 = b[2 * i, h] * (ahead(v1, s) - v1)
                f2 = b[2 * i + 1, h] * (ahead(v2, s) - v2)
                out[2 * i, h] = v1 + (src[2 * i, h] + g1 - g0 + f1 - behind(f1, s)) * rdiv[2 * i, h]
                out[2 * i + 1, h] = v2 + (src[2 * i + 1, h] + g2 - g1 + f2 - behind(f2, s)) * rdiv[2 * i + 1, h]

        steps(count // 2, smooth)

    def up_fine():
        def add(i):
            for h in HALVES:
                x = levels[0][5][i, h]
                column = lax.broadcasted_iota(jnp.int32, x.shape, 1)
                x = jnp.where((column & 1) == 0, x, behind(x, 1))
                v0[2 * i + 1, h] = v0[2 * i + 1, h] + x
                v0[2 * i + 2, h] = v0[2 * i + 2, h] + x

        steps(STEP // 2, add)
        wrap(v0)

        def smooth(i):
            for h in HALVES:
                va, v1, v2, vb = v0[2 * i, h], v0[2 * i + 1, h], v0[2 * i + 2, h], v0[2 * i + 3, h]
                g0 = wd[2 * i, h] * (v1 - va - sd[2 * i, h])
                g1 = wd[2 * i + 1, h] * (v2 - v1 - sd[2 * i + 1, h])
                g2 = wd[2 * i + 2, h] * (vb - v2 - sd[2 * i + 2, h])
                f1 = wr[2 * i, h] * (ahead(v1, 1) - v1 - sr[2 * i, h])
                f2 = wr[2 * i + 1, h] * (ahead(v2, 1) - v2 - sr[2 * i + 1, h])
                first[2 * i + 1, h] = v1 + (g1 - g0 + f1 - behind(f1, 1)) * rdiv0[2 * i, h]
                first[2 * i + 2, h] = v2 + (g2 - g1 + f2 - behind(f2, 1)) * rdiv0[2 * i + 1, h]

        steps(STEP // 2, smooth)

    def coarse_solve(turn, meanwhile):
        _, a3, b3, _, _, _ = levels[2]
        column = lax.broadcasted_iota(jnp.int32, (SUB, COLS), 1)
        line = lax.broadcasted_iota(jnp.int32, (SUB, COLS), 0)
        here = slice(0, COLS)
        part = jnp.where((column & 7) == 0, a3[2, :, here], 0.0) + jnp.where(
            (column & 15) == 8, b3[0, :, here] + b3[1, :, here], 0.0
        )
        part = jnp.where((line < CROWS) & ((column & 7) == 0), part, 0.0)
        local = jnp.sum(jnp.sum(part, axis=1, keepdims=True), axis=0, keepdims=True)
        mine = jnp.dot(coarse[:, here], select[...], precision=HIGHEST, preferred_element_type=F32)
        spot = lax.broadcasted_iota(jnp.int32, (8, 128), 1)
        blocks[turn, r] = jnp.where(spot < 32, mine[0:8], jnp.where(spot < 64, mine[8:16], local))
        copies = []
        for i in range(1, R):
            copy = pltpu.make_async_remote_copy(
                src_ref=blocks.at[turn, r],
                dst_ref=blocks.at[turn, r],
                send_sem=p2_send.at[turn, i - 1],
                recv_sem=p2_recv.at[turn, i - 1],
                device_id=(lax.rem(r + i, R), c),
                device_id_type=MESH,
            )
            copy.start()
            copies.append(copy)
        for copy in copies:
            copy.wait_recv()
        every = blocks[turn].reshape(R * 8, 128).T
        hat = jnp.dot(every[0:32], forward[0], precision=HIGHEST, preferred_element_type=F32) + jnp.dot(
            every[32:64], forward[1], precision=HIGHEST, preferred_element_type=F32
        )
        rows_sum = jnp.sum(every[64:65], axis=1, keepdims=True) * 0.125

        def total(n):
            return jnp.sum(powers[n] * hat, axis=0, keepdims=True)

        mode = lax.broadcasted_iota(jnp.int32, (1, FREQ), 1)
        amps[turn, c, 0:1, :] = jnp.where(mode < CROWS * R, total(0), rows_sum)
        amps[turn, c, 1:2, :] = total(1)
        near_send[turn, 0, 0:1, :] = total(2)
        near_send[turn, 0, 1:4, :] = hat[CCOLS - 3 : CCOLS]
        near_send[turn, 1, 0:3, :] = hat[0:3]
        near_send[turn, 1, 3:4, :] = total(3)
        for i in range(1, C):
            copy = pltpu.make_async_remote_copy(
                src_ref=amps.at[turn, c],
                dst_ref=amps.at[turn, c],
                send_sem=p3_send.at[turn, i - 1],
                recv_sem=p3_recv.at[turn, i - 1],
                device_id=(r, lax.rem(c + i, C)),
                device_id_type=MESH,
            )
            copy.start()
            copies.append(copy)
        rightward = pltpu.make_async_remote_copy(
            src_ref=near_send.at[turn, 0],
            dst_ref=near_left.at[turn],
            send_sem=nb_send.at[turn, 0],
            recv_sem=nb_recv.at[turn, 0],
            device_id=(r, lax.rem(c + 1, C)),
            device_id_type=MESH,
        )
        leftward = pltpu.make_async_remote_copy(
            src_ref=near_send.at[turn, 1],
            dst_ref=near_right.at[turn],
            send_sem=nb_send.at[turn, 1],
            recv_sem=nb_recv.at[turn, 1],
            device_id=(r, lax.rem(c + C - 1, C)),
            device_id_type=MESH,
        )
        pl.when(is_right)(rightward.start)
        pl.when(is_left)(leftward.start)
        meanwhile()
        pl.when(is_left)(rightward.wait_recv)
        pl.when(is_right)(leftward.wait_recv)
        for copy in copies[R - 1 :]:
            copy.wait_recv()
        into_left = jnp.zeros((2, FREQ), F32)
        into_right = jnp.zeros((2, FREQ), F32)
        weight = jnp.zeros((2, FREQ), F32)
        for i in range(C):
            x = amps[turn, i]
            into_left += coef[0, i] * x
            into_right += coef[1, i] * x
            weight += x
        into_left = into_left[0:1] + into_left[1:2]
        into_right = into_right[0:1] + into_right[1:2]
        weight = jnp.sum(jnp.where(mode == FREQ - 1, weight[0:1], 0.0), axis=1, keepdims=True)
        grid_rows, grid_cols = CROWS * R, CCOLS * C
        mean = weight * (1.0 / ((grid_rows - 1) * grid_cols + grid_rows * (grid_cols - 1))) + EPSILON
        ext[4:8, :] = near_left[turn]
        ext[4:5, :] = near_left[turn, 0:1, :] + into_left
        ext[8 : 8 + CCOLS, :] = hat
        ext[8 + CCOLS : 12 + CCOLS, :] = near_right[turn]
        ext[11 + CCOLS : 12 + CCOLS, :] = near_right[turn, 3:4, :] + into_right
        hats = ext[...]
        place = lax.broadcasted_iota(jnp.int32, (PAD, FREQ), 0)
        going_right = hats
        going_left = hats
        for i, s in enumerate(SHIFTS):
            q = constants[3 + i : 4 + i, :]
            going_right += q * jnp.where(place >= s, pltpu.roll(going_right, s, 0), 0.0)
            going_left += q * jnp.where(place < PAD - s, pltpu.roll(going_left, PAD - s, 0), 0.0)
        modes = (going_right + going_left - hats) * (green / mean)
        values = lax.dot_general(
            backward[...], modes, (((1,), (1,)), ((), ())), precision=HIGHEST, preferred_element_type=F32
        )
        coarse[...] = jnp.dot(values, spread[...], precision=HIGHEST, preferred_element_type=F32)
        return copies, rightward, leftward

    def descend():
        restrict_fine()
        for level in range(1, GRIDS):
            down(level)

    def ascend():
        for level in range(GRIDS - 1, 0, -1):
            up(level)
        up_fine()

    def widen():
        for _, receives, copy in halo_copies[8:]:
            pl.when(receives)(copy.wait_recv)
        nat[:, chunks, far, :] = outer[...]
        open_first(from_left, from_right)
        descend()

    open_first(in_left, in_right)
    descend()
    sent = [coarse_solve(0, widen)]
    ascend()
    wrap(first)

    def reweight(p):
        for h in HALVES:
            f = first[p + 1, h]
            e = first[p + 2, h] - f - sd[p + 1, h]
            a = wd[p + 1, h] / jnp.maximum(jnp.abs(e) * TURN, ERROR_FLOOR)
            wd[p + 1, h] = a
            gd[p + 1, h] = a * e
            e = ahead(f, 1) - f - sr[p, h]
            b = wr[p, h] / jnp.maximum(jnp.abs(e) * TURN, ERROR_FLOOR)
            wr[p, h] = b
            gr[p, h] = b * e

    steps(STEP, reweight)
    wrap(wd, below=False)
    wrap(gd, below=False)

    def start_second(p):
        for h in HALVES:
            b, f = wr[p, h], gr[p, h]
            rdiv = DAMPING / jnp.maximum(wd[p + 1, h] + wd[p, h] + b + behind(b, 1), DIAG_FLOOR)
            rdiv0[p, h] = rdiv
            v0[p + 1, h] = first[p + 1, h] + (gd[p + 1, h] - gd[p, h] + f - behind(f, 1)) * rdiv

    steps(STEP, start_second)
    wrap(v0)
    descend()
    sent.append(coarse_solve(1, lambda: None))
    ascend()

    outs = []
    for k in range(OWN_CHUNKS):
        span = slice(128 * k, 128 * k + 128)
        for p in range(STEP):
            result.at[k][pl.ds(p, SUB, stride=STEP), :] = first[p + 1, :, span] * TURN
        copy = pltpu.make_async_copy(result.at[k, own, :], out_h.at[:, span], out_sem.at[k])
        copy.start()
        outs.append(copy)
    for sends, _, copy in halo_copies:
        pl.when(sends)(copy.wait_send)
    for copies, rightward, leftward in sent:
        for copy in copies:
            copy.wait_send()
        pl.when(is_right)(rightward.wait_send)
        pl.when(is_left)(leftward.wait_send)
    for copy in outs:
        copy.wait()


def scratch(R, C):
    def field(count):
        return pltpu.VMEM((count, SUB, WIDTH), F32)

    shapes = [
        pltpu.VMEM((ROWS, COLS), jnp.int32),
        pltpu.VMEM((ROWS, COLS), jnp.int32),
        pltpu.VMEM((ROWS, COLS), jnp.int32),
        pltpu.VMEM((2, R * 8, FREQ), F32),
        pltpu.VMEM((SUB, FREQ), F32),
        pltpu.VMEM((16, FREQ), F32),
        pltpu.VMEM((2, OWN_CHUNKS, EXT, 128), F32),
        pltpu.VMEM((ROWS, 128), F32),
        pltpu.VMEM((ROWS, 128), F32),
        pltpu.VMEM((2, ROWS // 4, 128), F32),
        pltpu.VMEM((2, ROWS // 4, 128), F32),
        pltpu.VMEM((EXT, 128), F32),
        pltpu.VMEM((EXT, 128), F32),
        pltpu.VMEM((2, OWN_CHUNKS, EXT - ROWS - 2 * NEAR, 128), F32),
        pltpu.VMEM((EXT, 128), F32),
        pltpu.VMEM((EXT, 128), F32),
        pltpu.VMEM((OWN_CHUNKS, EXT, 128), F32),
    ]
    padded, plain = STEP + 2, STEP
    shapes += [field(n) for n in (padded, padded, padded, plain, padded, plain, padded, plain, padded, padded, plain)]
    for level in range(1, GRIDS):
        n = STEP >> level
        shapes += [field(m) for m in (n, n + 2, n, n, n + 2, n)]
    shapes += [
        pltpu.VMEM((SUB, WIDTH), F32),
        pltpu.VMEM((COLS, 128), F32),
        pltpu.VMEM((PAD, WIDTH), F32),
        pltpu.VMEM((2, R, 8, 128), F32),
        pltpu.VMEM((2, C, 2, FREQ), F32),
        pltpu.VMEM((2, 2, 4, FREQ), F32),
        pltpu.VMEM((2, 4, FREQ), F32),
        pltpu.VMEM((2, 4, FREQ), F32),
        pltpu.VMEM((PAD, FREQ), F32),
        pltpu.VMEM((4, CCOLS, FREQ), F32),
        pltpu.VMEM((2, C, 2, FREQ), F32),
        pltpu.SemaphoreType.DMA((6,)),
        pltpu.SemaphoreType.DMA((16,)),
        pltpu.SemaphoreType.DMA((16,)),
        pltpu.SemaphoreType.DMA((2, R - 1)),
        pltpu.SemaphoreType.DMA((2, R - 1)),
        pltpu.SemaphoreType.DMA((2, C - 1)),
        pltpu.SemaphoreType.DMA((2, C - 1)),
        pltpu.SemaphoreType.DMA((2, 2)),
        pltpu.SemaphoreType.DMA((2, 2)),
        pltpu.SemaphoreType.DMA((OWN_CHUNKS,)),
    ]
    return shapes


def solution(mesh):
    R, C = mesh.shape["row"], mesh.shape["col"]
    forward, backward, constants = tables(CROWS * R, CCOLS * C)

    def body(swath, coherence, counts):
        return pl.pallas_call(
            functools.partial(kernel, R, C),
            out_shape=jax.ShapeDtypeStruct((ROWS, COLS), F32),
            in_specs=[pl.BlockSpec(memory_space=pl.ANY)] * 6,
            out_specs=pl.BlockSpec(memory_space=pl.ANY),
            scratch_shapes=scratch(R, C),
            compiler_params=pltpu.CompilerParams(
                collective_id=0, has_side_effects=True
            ),
        )(swath, coherence, counts, jnp.asarray(forward), jnp.asarray(backward), jnp.asarray(constants))

    return jax.shard_map(
        body,
        mesh=mesh,
        in_specs=(P("row", "col"), P("row", "col"), P("row", "col")),
        out_specs=P("row", "col"),
        check_vma=False,
    )
```

```python
import functools

import jax
import jax.numpy as jnp
import numpy as np
from jax import lax
from jax.experimental import pallas as pl
from jax.experimental.pallas import tpu as pltpu
from jax.sharding import PartitionSpec as P

MESH = pl.DeviceIdType.MESH
HIGHEST = lax.Precision.HIGHEST
F32 = jnp.float32

GRIDS = 4
NCLASS = 8
LEVELS = 256
DAMPING = 0.8
DIAG_FLOOR = 0.5
TURN = 2.0 * np.pi
ERROR_FLOOR = 0.5
EPSILON = 1e-6
SCREEN_WIDTH = 4.0

STEP = 2**GRIDS
HALO = 48
NEAR = 16
ROWS = 160
COLS = 512
CROWS = ROWS // STEP
CCOLS = COLS // STEP
EXT = ROWS + 2 * HALO
SUB = EXT // STEP
OWN_CHUNKS = COLS // 128
CHUNKS = OWN_CHUNKS + 1
WIDTH = CHUNKS * 128
FREQ = 256
PAD = 48
SHIFTS = (1, 2, 4, 8, 16, 32)
UNROLL = 8
HALVES = tuple(slice(h, h + 8) for h in range(0, SUB, 8))


def tables(rows, cols):
    devices = rows // CROWS
    freq = np.arange(rows)[:, None]
    cosine = np.cos(np.pi * (np.arange(rows)[None, :] + 0.5) * freq / rows) * np.sqrt(2.0 / rows)
    cosine[0] *= np.sqrt(0.5)
    forward = np.zeros((2, devices, 8, FREQ))
    backward = np.zeros((devices, SUB, FREQ))
    for d in range(devices):
        for k in range(CROWS):
            forward[k // 8, d, k % 8, :rows] = cosine[:, d * CROWS + k]
        for k in range(SUB):
            place = d * CROWS + (k if k < CROWS + HALO // STEP else k - SUB)
            if 0 <= place < rows:
                backward[d, k, :rows] = cosine[:, place]
    shift = 2.0 - 2.0 * np.cos(np.pi * np.arange(rows) / rows) + (SCREEN_WIDTH / cols) ** 2
    theta = 2.0 * np.arcsinh(np.sqrt(shift) / 2.0)
    constants = np.zeros((16, FREQ))
    constants[0] = 1.0
    constants[0, :rows] = theta
    constants[1, :rows] = 1.0 / (2.0 * np.sinh(theta))
    constants[2] = 1.0
    constants[2, :rows] = 1.0 / (1.0 - np.exp(-2.0 * cols * theta))
    for i, s in enumerate(SHIFTS):
        constants[3 + i] = np.exp(-s * constants[0])
    return (
        forward.reshape(2, devices * 8, FREQ).astype(np.float32),
        backward.astype(np.float32),
        constants.astype(np.float32),
    )


def ahead(x, s):
    return pltpu.roll(x, WIDTH - s, 1)


def behind(x, s):
    return pltpu.roll(x, s, 1)


def wrap(ref, above=True, below=True):
    last = ref.shape[0] - 2
    if above:
        ref[0] = pltpu.roll(ref[last], 1, 0)
    if below:
        ref[last + 1] = pltpu.roll(ref[1], SUB - 1, 0)


def steps(count, body):
    if count <= UNROLL:
        for i in range(count):
            body(i)
    else:

        def step(i, carry):
            for j in range(UNROLL):
                body(i * UNROLL + j)
            return carry

        lax.fori_loop(0, count // UNROLL, step, 0)


def kernel(R, C, *refs):
    (
        swath_h,
        coherence_h,
        counts_h,
        forward_h,
        backward_h,
        constants_h,
        out_h,
        swath,
        coherence,
        counts,
        forward,
        backward,
        constants,
        nat,
        left_pack,
        right_pack,
        near_pack,
        near_got,
        in_left,
        in_right,
        outer,
        from_left,
        from_right,
        result,
        qual,
        phase,
        wd,
        wr,
        sd,
        sr,
        v0,
        rdiv0,
        base0,
        first,
        gd,
        gr,
        *rest,
    ) = refs
    levels = []
    for _ in range(3):
        levels.append(rest[:7])
        rest = rest[7:]
    (
        coarse,
        select,
        spread,
        blocks,
        amps,
        near_send,
        near_left,
        near_right,
        ext,
        powers,
        coef,
        load_sem,
        p1_send,
        p1_recv,
        p2_send,
        p2_recv,
        p3_send,
        p3_recv,
        nb_send,
        nb_recv,
        out_sem,
    ) = rest

    r = lax.axis_index("row")
    c = lax.axis_index("col")
    N = CCOLS * C

    loads = [
        pltpu.make_async_copy(swath_h, swath, load_sem.at[0]),
        pltpu.make_async_copy(coherence_h, coherence, load_sem.at[1]),
        pltpu.make_async_copy(counts_h, counts, load_sem.at[2]),
        pltpu.make_async_copy(constants_h, constants, load_sem.at[3]),
        pltpu.make_async_copy(forward_h, forward, load_sem.at[4]),
        pltpu.make_async_copy(backward_h.at[r], backward, load_sem.at[5]),
    ]
    for copy in loads:
        copy.start()

    barrier = pltpu.get_barrier_semaphore()
    for i in sorted(range(1, C), key=lambda i: -min(i, C - i)):
        pl.semaphore_signal(barrier, inc=1, device_id=(r, lax.rem(c + i, C)), device_id_type=MESH)
    for i in (1, R - 1):
        for j in (1, C - 1):
            pl.semaphore_signal(
                barrier, inc=1, device_id=(lax.rem(r + i, R), lax.rem(c + j, C)), device_id_type=MESH
            )
    for i in range(1, R):
        pl.semaphore_signal(barrier, inc=1, device_id=(lax.rem(r + i, R), c), device_id_type=MESH)

    is_up, is_down = r > 0, r < R - 1
    is_left, is_right = c > 0, c < C - 1
    chunks = slice(0, OWN_CHUNKS)
    own, below, above = slice(0, ROWS), slice(ROWS, ROWS + HALO), slice(ROWS + HALO, EXT)
    near_below, near_above = slice(ROWS, ROWS + NEAR), slice(EXT - NEAR, EXT)
    far = slice(ROWS + NEAR, EXT - NEAR)
    far_rows = EXT - ROWS - 2 * NEAR
    far_below, far_above = slice(0, far_rows // 2), slice(far_rows // 2, far_rows)

    def clear(ref, *where):
        ref[where] = jnp.zeros(ref.at[where].shape, F32)

    every = slice(None)
    clear(nat, every, chunks, far)
    clear(in_left, far)
    clear(in_right, far)

    @pl.when(jnp.logical_not(is_down))
    def _():
        clear(nat, every, chunks, near_below)
        clear(outer, every, chunks, far_below)
        for ref in (in_left, in_right):
            clear(ref, near_below)
        for ref in (from_left, from_right):
            clear(ref, below)

    @pl.when(jnp.logical_not(is_up))
    def _():
        clear(nat, every, chunks, near_above)
        clear(outer, every, chunks, far_above)
        for ref in (in_left, in_right):
            clear(ref, near_above)
        for ref in (from_left, from_right):
            clear(ref, above)

    @pl.when(jnp.logical_not(is_right))
    def _():
        clear(near_got, 0)
        clear(in_right, near_below)
        clear(in_right, near_above)
        clear(from_right, slice(0, EXT))
        clear(near_right, every)

    @pl.when(jnp.logical_not(is_left))
    def _():
        clear(near_got, 1)
        clear(in_left, near_below)
        clear(in_left, near_above)
        clear(from_left, slice(0, EXT))
        clear(near_left, every)

    for copy in loads[:3]:
        copy.wait()
    lane = lax.broadcasted_iota(jnp.int32, (32, 128), 1)

    def prepare(i):
        rows = slice(i * 32, i * 32 + 32)
        for k in range(OWN_CHUNKS):
            span = slice(128 * k, 128 * k + 128)
            level = coherence[rows, span].astype(F32) * (1.0 / (NCLASS - 1))
            q = swath[rows, span].astype(F32) * (level * level)
            ph = counts[rows, span].astype(F32) * (1.0 / LEVELS)
            nat[0, k, rows, :] = q
            nat[1, k, rows, :] = ph
            if k == 0:
                left_pack[rows, :] = jnp.where(lane < 64, q, pltpu.roll(ph, 64, 1))
            if k == OWN_CHUNKS - 1:
                right_pack[rows, :] = jnp.where(lane < 64, pltpu.roll(ph, 64, 1), q)

    for i in range(ROWS // 32):
        prepare(i)
    quarter = ROWS // 4
    lane = lax.broadcasted_iota(jnp.int32, (quarter, 128), 1)
    packed = [jnp.zeros((quarter, 128), F32)] * 2
    for g in range(4):
        rows = slice(quarter * g, quarter * g + quarter)
        turned = (pltpu.roll(left_pack[rows, :], NEAR * g, 1), pltpu.roll(right_pack[rows, :], NEAR * g + 80, 1))
        packed = [jnp.where((lane & 48) == NEAR * g, x, y) for x, y in zip(turned, packed)]
    near_pack[0] = packed[0]
    near_pack[1] = packed[1]
    pl.semaphore_wait(barrier, R + C + 2)

    both = jnp.logical_and
    first_rows, last_rows = slice(0, NEAR), slice(ROWS - NEAR, ROWS)
    top, bottom = slice(0, HALO), slice(ROWS - HALO, ROWS)
    top_far, bottom_far = slice(NEAR, HALO), slice(ROWS - HALO, ROWS - NEAR)
    up_left, down_left = both(is_up, is_left), both(is_down, is_left)
    up_right, down_right = both(is_up, is_right), both(is_down, is_right)
    plan = [
        (is_left, 0, -1, near_pack.at[0], near_got.at[0], is_right),
        (is_right, 0, 1, near_pack.at[1], near_got.at[1], is_left),
        (up_left, -1, -1, left_pack.at[first_rows], in_right.at[near_below], down_right),
        (down_left, 1, -1, left_pack.at[last_rows], in_right.at[near_above], up_right),
        (up_right, -1, 1, right_pack.at[first_rows], in_left.at[near_below], down_left),
        (down_right, 1, 1, right_pack.at[last_rows], in_left.at[near_above], up_left),
        (is_up, -1, 0, nat.at[:, chunks, first_rows, :], nat.at[:, chunks, near_below, :], is_down),
        (is_down, 1, 0, nat.at[:, chunks, last_rows, :], nat.at[:, chunks, near_above, :], is_up),
        (is_left, 0, -1, left_pack, from_right.at[own], is_right),
        (is_right, 0, 1, right_pack, from_left.at[own], is_left),
        (up_left, -1, -1, left_pack.at[top], from_right.at[below], down_right),
        (down_left, 1, -1, left_pack.at[bottom], from_right.at[above], up_right),
        (up_right, -1, 1, right_pack.at[top], from_left.at[below], down_left),
        (down_right, 1, 1, right_pack.at[bottom], from_left.at[above], up_left),
        (is_up, -1, 0, nat.at[:, chunks, top_far, :], outer.at[:, chunks, far_below, :], is_down),
        (is_down, 1, 0, nat.at[:, chunks, bottom_far, :], outer.at[:, chunks, far_above, :], is_up),
    ]
    halo_copies = []
    for i, (sends, dr, dc, source, target, receives) in enumerate(plan):
        copy = pltpu.make_async_remote_copy(
            src_ref=source,
            dst_ref=target,
            send_sem=p1_send.at[i],
            recv_sem=p1_recv.at[i],
            device_id=(lax.rem(r + dr + R, R), lax.rem(c + dc + C, C)),
            device_id_type=MESH,
        )
        halo_copies.append((sends, receives, copy))
        pl.when(sends)(copy.start)

    for copy in loads[3:]:
        copy.wait()
    theta = constants[0:1, :]
    green = constants[1:2, :]
    inverse = constants[2:3, :]
    yy = lax.broadcasted_iota(jnp.int32, (CCOLS, FREQ), 0)
    last = CCOLS - 1
    powers[0] = jnp.exp(-theta * (last - yy).astype(F32))
    powers[1] = jnp.exp(-theta * yy.astype(F32))
    powers[2] = jnp.where(yy <= last - 3, jnp.exp(-theta * jnp.maximum(last - 3 - yy, 0).astype(F32)), 0.0)
    powers[3] = jnp.where(yy >= 3, jnp.exp(-theta * jnp.maximum(yy - 3, 0).astype(F32)), 0.0)

    def decay(n):
        return jnp.exp(-theta * n.astype(F32))

    def directly(n, inside):
        return jnp.where(inside, decay(jnp.maximum(n, 0)), 0.0)

    for i in range(C):
        rev = C - 1 - i
        coef[0, i, 0:1, :] = directly(CCOLS * (c - 1 - i) - 3, i < c - 1) + inverse * decay(
            N + CCOLS * rev + CCOLS * c - 3
        )
        coef[0, i, 1:2, :] = inverse * decay(CCOLS * i + CCOLS * c - 3)
        coef[1, i, 0:1, :] = inverse * decay(CCOLS * (C - 1 - c) + CCOLS * rev - 3)
        coef[1, i, 1:2, :] = directly(CCOLS * (i - c - 1) - 3, i > c + 1) + inverse * decay(
            2 * N - CCOLS * (c + 1) + CCOLS * i - 3
        )
    at = lax.broadcasted_iota(jnp.int32, (COLS, 128), 0)
    to = lax.broadcasted_iota(jnp.int32, (COLS, 128), 1)
    select[...] = jnp.where((to < 64) & (at == STEP * (to & 31)), 1.0, 0.0).astype(F32)
    at = lax.broadcasted_iota(jnp.int32, (PAD, WIDTH), 0)
    to = lax.broadcasted_iota(jnp.int32, (PAD, WIDTH), 1) >> GRIDS
    spread[...] = jnp.where(at == jnp.where(to < CCOLS + 3, to + 8, to + 8 - WIDTH // STEP), 1.0, 0.0).astype(F32)
    ext[...] = jnp.zeros((PAD, FREQ), F32)

    for _, receives, copy in halo_copies[:8]:
        pl.when(receives)(copy.wait_recv)
    lane = lax.broadcasted_iota(jnp.int32, (quarter, 128), 1)
    for g in range(4):
        rows = slice(quarter * g, quarter * g + quarter)
        in_right[rows, :] = jnp.where((lane & 63) < NEAR, pltpu.roll(near_got[0], (128 - NEAR * g) % 128, 1), 0.0)
        in_left[rows, :] = jnp.where((lane & 63) >= 64 - NEAR, pltpu.roll(near_got[1], 48 - NEAR * g, 1), 0.0)

    def arrange(left, right):
        lane = lax.broadcasted_iota(jnp.int32, (SUB, 128), 1)
        for p in range(STEP):
            rows = pl.ds(p, SUB, stride=STEP)
            for k in range(OWN_CHUNKS):
                span = slice(128 * k, 128 * k + 128)
                qual[p + 1, :, span] = nat.at[0, k][rows, :]
                phase[p + 1, :, span] = nat.at[1, k][rows, :]
            a, b = right[rows, :], left[rows, :]
            qual[p + 1, :, COLS:WIDTH] = jnp.where(lane < 64, a, b)
            phase[p + 1, :, COLS:WIDTH] = pltpu.roll(jnp.where(lane < 64, b, a), 64, 1)
        wrap(qual, above=False)
        wrap(phase, above=False)

    def steep(u):
        return u - jnp.floor(u + 0.5)

    def make_faces(p):
        for h in HALVES:
            q, ph = qual[p + 1, h], phase[p + 1, h]
            wd[p + 1, h] = jnp.minimum(q, qual[p + 2, h])
            wr[p, h] = jnp.minimum(q, ahead(q, 1))
            sd[p + 1, h] = steep(phase[p + 2, h] - ph)
            sr[p, h] = steep(ahead(ph, 1) - ph)

    def start_first(p):
        for h in HALVES:
            a, au, b = wd[p + 1, h], wd[p, h], wr[p, h]
            fr = b * sr[p, h]
            source = au * sd[p, h] - a * sd[p + 1, h] + behind(fr, 1) - fr
            rdiv = DAMPING / jnp.maximum(a + au + b + behind(b, 1), DIAG_FLOOR)
            rdiv0[p, h] = rdiv
            v0[p + 1, h] = source * rdiv

    def open_first(left, right):
        arrange(left, right)
        steps(STEP, make_faces)
        wrap(wd, below=False)
        wrap(sd, below=False)
        steps(STEP, start_first)
        wrap(v0)

    def restrict_fine():
        src, a1, b1 = levels[0][0], levels[0][1], levels[0][2]

        def body(i):
            for h in HALVES:
                va, v1, v2, vb = v0[2 * i, h], v0[2 * i + 1, h], v0[2 * i + 2, h], v0[2 * i + 3, h]
                a_odd = wd[2 * i + 2, h]
                y = a_odd * (vb - v2 - sd[2 * i + 2, h]) - wd[2 * i, h] * (v1 - va - sd[2 * i, h])
                b0, b_odd = wr[2 * i, h], wr[2 * i + 1, h]
                g = b0 * (ahead(v1, 1) - v1 - sr[2 * i, h]) + b_odd * (ahead(v2, 1) - v2 - sr[2 * i + 1, h])
                src[i, h] = y + ahead(y + g, 1) - behind(g, 1)
                a1[i + 1, h] = a_odd + ahead(a_odd, 1)
                b1[i, h] = ahead(b0 + b_odd, 1)

        steps(STEP // 2, body)
        wrap(a1, below=False)

    def down(level):
        s = 2**level
        count = STEP // s
        src, a, b, rdiv, v, _, _ = levels[level - 1]

        def smooth(p):
            for h in HALVES:
                bb = b[p, h]
                d = DAMPING / jnp.maximum(a[p + 1, h] + a[p, h] + bb + behind(bb, s), DIAG_FLOOR)
                rdiv[p, h] = d
                v[p + 1, h] = src[p, h] * d

        steps(count, smooth)
        wrap(v)
        if level < GRIDS - 1:
            src_n, a_n, b_n = levels[level][0], levels[level][1], levels[level][2]
        else:
            src_n, a_n, b_n = None, None, None

        def body(i):
            for h in HALVES:
                va, v1, v2, vb = v[2 * i, h], v[2 * i + 1, h], v[2 * i + 2, h], v[2 * i + 3, h]
                a_odd = a[2 * i + 2, h]
                t = src[2 * i, h] + src[2 * i + 1, h] + a_odd * (vb - v2) - a[2 * i, h] * (v1 - va)
                b0, b_odd = b[2 * i, h], b[2 * i + 1, h]
                g = b0 * (ahead(v1, s) - v1) + b_odd * (ahead(v2, s) - v2)
                out = t + ahead(t + g, s) - behind(g, s)
                if src_n is None:
                    coarse[h] = out
                else:
                    src_n[i, h] = out
                    a_n[i + 1, h] = a_odd + ahead(a_odd, s)
                    b_n[i, h] = ahead(b0 + b_odd, s)

        steps(count // 2, body)
        if a_n is not None:
            wrap(a_n, below=False)

    def settle(level):
        s = 2**level
        count = STEP // s
        src, a, b, rdiv, v, base, _ = levels[level - 1]

        def body(i):
            for h in HALVES:
                va, v1, v2, vb = v[2 * i, h], v[2 * i + 1, h], v[2 * i + 2, h], v[2 * i + 3, h]
                g0 = a[2 * i, h] * (v1 - va)
                g1 = a[2 * i + 1, h] * (v2 - v1)
                g2 = a[2 * i + 2, h] * (vb - v2)
                f1 = b[2 * i, h] * (ahead(v1, s) - v1)
                f2 = b[2 * i + 1, h] * (ahead(v2, s) - v2)
                base[2 * i, h] = v1 + (src[2 * i, h] + g1 - g0 + f1 - behind(f1, s)) * rdiv[2 * i, h]
                base[2 * i + 1, h] = v2 + (src[2 * i + 1, h] + g2 - g1 + f2 - behind(f2, s)) * rdiv[2 * i + 1, h]

        steps(count // 2, body)

    def settle_fine():
        def body(i):
            for h in HALVES:
                va, v1, v2, vb = v0[2 * i, h], v0[2 * i + 1, h], v0[2 * i + 2, h], v0[2 * i + 3, h]
                g0 = wd[2 * i, h] * (v1 - va - sd[2 * i, h])
                g1 = wd[2 * i + 1, h] * (v2 - v1 - sd[2 * i + 1, h])
                g2 = wd[2 * i + 2, h] * (vb - v2 - sd[2 * i + 2, h])
                f1 = wr[2 * i, h] * (ahead(v1, 1) - v1 - sr[2 * i, h])
                f2 = wr[2 * i + 1, h] * (ahead(v2, 1) - v2 - sr[2 * i + 1, h])
                base0[2 * i, h] = v1 + (g1 - g0 + f1 - behind(f1, 1)) * rdiv0[2 * i, h]
                base0[2 * i + 1, h] = v2 + (g2 - g1 + f2 - behind(f2, 1)) * rdiv0[2 * i + 1, h]

        steps(STEP // 2, body)

    def settle_all():
        settle_fine()
        for level in range(1, GRIDS):
            settle(level)

    def climb(level, put):
        s = 2**level
        count = STEP // s
        if level:
            _, a, b, rdiv, _, base, _ = levels[level - 1]
        else:
            a, b, rdiv, base = wd, wr, rdiv0, base0
        if level == GRIDS - 1:
            above_it, below_it = pltpu.roll(coarse[...], 1, 0), pltpu.roll(coarse[...], SUB - 1, 0)

        def correction(i, h):
            if level == GRIDS - 1:
                return (above_it[h], coarse[h], below_it[h])[i + 1]
            x = levels[level][6][i + 1, h]
            column = lax.broadcasted_iota(jnp.int32, x.shape, 1)
            return jnp.where((column & s) == 0, x, behind(x, s))

        for h in HALVES:
            x = correction(0, h)
            upper = x - correction(-1, h)
            for i in range(count // 2):
                after = correction(i + 1, h)
                lower = after - x
                side = ahead(x, s) - x
                f1, f2 = b[2 * i, h] * side, b[2 * i + 1, h] * side
                put(2 * i, h, base[2 * i, h] + x + (f1 - behind(f1, s) - a[2 * i, h] * upper) * rdiv[2 * i, h])
                put(
                    2 * i + 1,
                    h,
                    base[2 * i + 1, h] + x + (f2 - behind(f2, s) + a[2 * i + 2, h] * lower) * rdiv[2 * i + 1, h],
                )
                x, upper = after, lower

    def ascend(put_fine):
        for level in range(GRIDS - 1, 0, -1):
            out = levels[level - 1][6]

            def put(p, h, x, out=out):
                out[p + 1, h] = x

            climb(level, put)
            wrap(out)
        climb(0, put_fine)

    def coarse_solve(turn, meanwhile, later):
        a3, b3 = levels[2][1:3]
        column = lax.broadcasted_iota(jnp.int32, (SUB, COLS), 1)
        line = lax.broadcasted_iota(jnp.int32, (SUB, COLS), 0)
        here = slice(0, COLS)
        part = jnp.where((column & 7) == 0, a3[2, :, here], 0.0) + jnp.where(
            (column & 15) == 8, b3[0, :, here] + b3[1, :, here], 0.0
        )
        part = jnp.where((line < CROWS) & ((column & 7) == 0), part, 0.0)
        local = jnp.sum(jnp.sum(part, axis=1, keepdims=True), axis=0, keepdims=True)
        mine = jnp.dot(coarse[:, here], select[...], precision=HIGHEST, preferred_element_type=F32)
        spot = lax.broadcasted_iota(jnp.int32, (8, 128), 1)
        blocks[turn, r] = jnp.where(spot < 32, mine[0:8], jnp.where(spot < 64, mine[8:16], local))
        copies = []
        for i in sorted(range(1, R), key=lambda i: -min(i, R - i)):
            copy = pltpu.make_async_remote_copy(
                src_ref=blocks.at[turn, r],
                dst_ref=blocks.at[turn, r],
                send_sem=p2_send.at[turn, i - 1],
                recv_sem=p2_recv.at[turn, i - 1],
                device_id=(lax.rem(r + i, R), c),
                device_id_type=MESH,
            )
            copy.start()
            copies.append(copy)
        meanwhile()
        for copy in copies:
            copy.wait_recv()
        every = blocks[turn].reshape(R * 8, 128).T
        hat = jnp.dot(every[0:32], forward[0], precision=HIGHEST, preferred_element_type=F32) + jnp.dot(
            every[32:64], forward[1], precision=HIGHEST, preferred_element_type=F32
        )
        rows_sum = jnp.sum(every[64:65], axis=1, keepdims=True) * 0.125

        def total(n):
            return jnp.sum(powers[n] * hat, axis=0, keepdims=True)

        mode = lax.broadcasted_iota(jnp.int32, (1, FREQ), 1)
        amps[turn, c, 0:1, :] = jnp.where(mode < CROWS * R, total(0), rows_sum)
        amps[turn, c, 1:2, :] = total(1)
        near_send[turn, 0, 0:1, :] = total(2)
        near_send[turn, 0, 1:4, :] = hat[CCOLS - 3 : CCOLS]
        near_send[turn, 1, 0:3, :] = hat[0:3]
        near_send[turn, 1, 3:4, :] = total(3)
        for i in sorted(range(1, C), key=lambda i: -min(i, C - i)):
            copy = pltpu.make_async_remote_copy(
                src_ref=amps.at[turn, c],
                dst_ref=amps.at[turn, c],
                send_sem=p3_send.at[turn, i - 1],
                recv_sem=p3_recv.at[turn, i - 1],
                device_id=(r, lax.rem(c + i, C)),
                device_id_type=MESH,
            )
            copy.start()
            copies.append(copy)
        rightward = pltpu.make_async_remote_copy(
            src_ref=near_send.at[turn, 0],
            dst_ref=near_left.at[turn],
            send_sem=nb_send.at[turn, 0],
            recv_sem=nb_recv.at[turn, 0],
            device_id=(r, lax.rem(c + 1, C)),
            device_id_type=MESH,
        )
        leftward = pltpu.make_async_remote_copy(
            src_ref=near_send.at[turn, 1],
            dst_ref=near_right.at[turn],
            send_sem=nb_send.at[turn, 1],
            recv_sem=nb_recv.at[turn, 1],
            device_id=(r, lax.rem(c + C - 1, C)),
            device_id_type=MESH,
        )
        pl.when(is_right)(rightward.start)
        pl.when(is_left)(leftward.start)
        later()
        pl.when(is_left)(rightward.wait_recv)
        pl.when(is_right)(leftward.wait_recv)
        for copy in copies[R - 1 :]:
            copy.wait_recv()
        into_left = jnp.zeros((2, FREQ), F32)
        into_right = jnp.zeros((2, FREQ), F32)
        weight = jnp.zeros((2, FREQ), F32)
        for i in range(C):
            x = amps[turn, i]
            into_left += coef[0, i] * x
            into_right += coef[1, i] * x
            weight += x
        into_left = into_left[0:1] + into_left[1:2]
        into_right = into_right[0:1] + into_right[1:2]
        weight = jnp.sum(jnp.where(mode == FREQ - 1, weight[0:1], 0.0), axis=1, keepdims=True)
        grid_rows, grid_cols = CROWS * R, CCOLS * C
        mean = weight * (1.0 / ((grid_rows - 1) * grid_cols + grid_rows * (grid_cols - 1))) + EPSILON
        ext[4:8, :] = near_left[turn]
        ext[4:5, :] = near_left[turn, 0:1, :] + into_left
        ext[8 : 8 + CCOLS, :] = hat
        ext[8 + CCOLS : 12 + CCOLS, :] = near_right[turn]
        ext[11 + CCOLS : 12 + CCOLS, :] = near_right[turn, 3:4, :] + into_right
        hats = ext[...]
        place = lax.broadcasted_iota(jnp.int32, (PAD, FREQ), 0)
        going_right = hats
        going_left = hats
        for i, s in enumerate(SHIFTS):
            q = constants[3 + i : 4 + i, :]
            going_right += q * jnp.where(place >= s, pltpu.roll(going_right, s, 0), 0.0)
            going_left += q * jnp.where(place < PAD - s, pltpu.roll(going_left, PAD - s, 0), 0.0)
        modes = (going_right + going_left - hats) * (green / mean)
        values = lax.dot_general(
            backward[...], modes, (((1,), (1,)), ((), ())), precision=HIGHEST, preferred_element_type=F32
        )
        coarse[...] = jnp.dot(values, spread[...], precision=HIGHEST, preferred_element_type=F32)
        return copies, rightward, leftward

    def descend():
        restrict_fine()
        for level in range(1, GRIDS):
            down(level)

    def widen():
        for _, receives, copy in halo_copies[8:]:
            pl.when(receives)(copy.wait_recv)
        nat[:, chunks, far, :] = outer[...]
        open_first(from_left, from_right)

    def finish_wide():
        descend()
        settle_all()

    def put_first(p, h, x):
        first[p + 1, h] = x

    def put_result(p, h, x):
        rows = pl.ds(STEP * h.start + p, 8, stride=STEP)
        for k in range(OWN_CHUNKS):
            result.at[k][rows, :] = x[:, 128 * k : 128 * k + 128] * TURN

    open_first(in_left, in_right)
    descend()
    sent = [coarse_solve(0, widen, finish_wide)]
    ascend(put_first)
    wrap(first)

    def reweight(p):
        for h in HALVES:
            f = first[p + 1, h]
            e = first[p + 2, h] - f - sd[p + 1, h]
            a = wd[p + 1, h] / jnp.maximum(jnp.abs(e) * TURN, ERROR_FLOOR)
            wd[p + 1, h] = a
            gd[p + 1, h] = a * e
            e = ahead(f, 1) - f - sr[p, h]
            b = wr[p, h] / jnp.maximum(jnp.abs(e) * TURN, ERROR_FLOOR)
            wr[p, h] = b
            gr[p, h] = b * e

    steps(STEP, reweight)
    wrap(wd, below=False)
    wrap(gd, below=False)

    def start_second(p):
        for h in HALVES:
            b, f = wr[p, h], gr[p, h]
            rdiv = DAMPING / jnp.maximum(wd[p + 1, h] + wd[p, h] + b + behind(b, 1), DIAG_FLOOR)
            rdiv0[p, h] = rdiv
            v0[p + 1, h] = first[p + 1, h] + (gd[p + 1, h] - gd[p, h] + f - behind(f, 1)) * rdiv

    steps(STEP, start_second)
    wrap(v0)
    descend()
    sent.append(coarse_solve(1, settle_all, lambda: None))
    ascend(put_result)

    outs = []
    for k in range(OWN_CHUNKS):
        span = slice(128 * k, 128 * k + 128)
        copy = pltpu.make_async_copy(result.at[k, own, :], out_h.at[:, span], out_sem.at[k])
        copy.start()
        outs.append(copy)
    for sends, _, copy in halo_copies:
        pl.when(sends)(copy.wait_send)
    for copies, rightward, leftward in sent:
        for copy in copies:
            copy.wait_send()
        pl.when(is_right)(rightward.wait_send)
        pl.when(is_left)(leftward.wait_send)
    for copy in outs:
        copy.wait()


def scratch(R, C):
    def field(count):
        return pltpu.VMEM((count, SUB, WIDTH), F32)

    shapes = [
        pltpu.VMEM((ROWS, COLS), jnp.int32),
        pltpu.VMEM((ROWS, COLS), jnp.int32),
        pltpu.VMEM((ROWS, COLS), jnp.int32),
        pltpu.VMEM((2, R * 8, FREQ), F32),
        pltpu.VMEM((SUB, FREQ), F32),
        pltpu.VMEM((16, FREQ), F32),
        pltpu.VMEM((2, OWN_CHUNKS, EXT, 128), F32),
        pltpu.VMEM((ROWS, 128), F32),
        pltpu.VMEM((ROWS, 128), F32),
        pltpu.VMEM((2, ROWS // 4, 128), F32),
        pltpu.VMEM((2, ROWS // 4, 128), F32),
        pltpu.VMEM((EXT, 128), F32),
        pltpu.VMEM((EXT, 128), F32),
        pltpu.VMEM((2, OWN_CHUNKS, EXT - ROWS - 2 * NEAR, 128), F32),
        pltpu.VMEM((EXT, 128), F32),
        pltpu.VMEM((EXT, 128), F32),
        pltpu.VMEM((OWN_CHUNKS, EXT, 128), F32),
    ]
    padded, plain = STEP + 2, STEP
    shapes += [field(n) for n in (padded, padded, padded, plain, padded, plain, padded, plain, plain, padded, padded, plain)]
    for level in range(1, GRIDS):
        n = STEP >> level
        shapes += [field(m) for m in (n, n + 2, n, n, n + 2, n, n + 2)]
    shapes += [
        pltpu.VMEM((SUB, WIDTH), F32),
        pltpu.VMEM((COLS, 128), F32),
        pltpu.VMEM((PAD, WIDTH), F32),
        pltpu.VMEM((2, R, 8, 128), F32),
        pltpu.VMEM((2, C, 2, FREQ), F32),
        pltpu.VMEM((2, 2, 4, FREQ), F32),
        pltpu.VMEM((2, 4, FREQ), F32),
        pltpu.VMEM((2, 4, FREQ), F32),
        pltpu.VMEM((PAD, FREQ), F32),
        pltpu.VMEM((4, CCOLS, FREQ), F32),
        pltpu.VMEM((2, C, 2, FREQ), F32),
        pltpu.SemaphoreType.DMA((6,)),
        pltpu.SemaphoreType.DMA((16,)),
        pltpu.SemaphoreType.DMA((16,)),
        pltpu.SemaphoreType.DMA((2, R - 1)),
        pltpu.SemaphoreType.DMA((2, R - 1)),
        pltpu.SemaphoreType.DMA((2, C - 1)),
        pltpu.SemaphoreType.DMA((2, C - 1)),
        pltpu.SemaphoreType.DMA((2, 2)),
        pltpu.SemaphoreType.DMA((2, 2)),
        pltpu.SemaphoreType.DMA((OWN_CHUNKS,)),
    ]
    return shapes


def solution(mesh):
    R, C = mesh.shape["row"], mesh.shape["col"]
    forward, backward, constants = tables(CROWS * R, CCOLS * C)

    def body(swath, coherence, counts):
        return pl.pallas_call(
            functools.partial(kernel, R, C),
            out_shape=jax.ShapeDtypeStruct((ROWS, COLS), F32),
            in_specs=[pl.BlockSpec(memory_space=pl.ANY)] * 6,
            out_specs=pl.BlockSpec(memory_space=pl.ANY),
            scratch_shapes=scratch(R, C),
            compiler_params=pltpu.CompilerParams(
                collective_id=0, has_side_effects=True
            ),
        )(swath, coherence, counts, jnp.asarray(forward), jnp.asarray(backward), jnp.asarray(constants))

    return jax.shard_map(
        body,
        mesh=mesh,
        in_specs=(P("row", "col"), P("row", "col"), P("row", "col")),
        out_specs=P("row", "col"),
        check_vma=False,
    )
```

```python
import functools

import jax
import jax.numpy as jnp
import numpy as np
from jax import lax
from jax.experimental import pallas as pl
from jax.experimental.pallas import tpu as pltpu
from jax.sharding import PartitionSpec as P

MESH = pl.DeviceIdType.MESH
HIGHEST = lax.Precision.HIGHEST
F32 = jnp.float32

GRIDS = 4
NCLASS = 8
LEVELS = 256
DAMPING = 0.8
DIAG_FLOOR = 0.5
TURN = 2.0 * np.pi
ERROR_FLOOR = 0.5
EPSILON = 1e-6
SCREEN_WIDTH = 4.0

STEP = 2**GRIDS
HALO = 48
NEAR = 16
ROWS = 160
COLS = 512
CROWS = ROWS // STEP
CCOLS = COLS // STEP
EXT = ROWS + 2 * HALO
SUB = EXT // STEP
OWN_CHUNKS = COLS // 128
CHUNKS = OWN_CHUNKS + 1
WIDTH = CHUNKS * 128
FREQ = 256
PAD = 48
SHIFTS = (1, 2, 4, 8, 16, 32)
UNROLL = 8
HALVES = tuple(slice(h, h + 8) for h in range(0, SUB, 8))


def tables(rows, cols):
    devices = rows // CROWS
    freq = np.arange(rows)[:, None]
    cosine = np.cos(np.pi * (np.arange(rows)[None, :] + 0.5) * freq / rows) * np.sqrt(2.0 / rows)
    cosine[0] *= np.sqrt(0.5)
    forward = np.zeros((2, devices, 8, FREQ))
    backward = np.zeros((devices, SUB, FREQ))
    for d in range(devices):
        for k in range(CROWS):
            forward[k // 8, d, k % 8, :rows] = cosine[:, d * CROWS + k]
        for k in range(SUB):
            place = d * CROWS + (k if k < CROWS + HALO // STEP else k - SUB)
            if 0 <= place < rows:
                backward[d, k, :rows] = cosine[:, place]
    shift = 2.0 - 2.0 * np.cos(np.pi * np.arange(rows) / rows) + (SCREEN_WIDTH / cols) ** 2
    theta = 2.0 * np.arcsinh(np.sqrt(shift) / 2.0)
    constants = np.zeros((16, FREQ))
    constants[0] = 1.0
    constants[0, :rows] = theta
    constants[1, :rows] = 1.0 / (2.0 * np.sinh(theta))
    constants[2] = 1.0
    constants[2, :rows] = 1.0 / (1.0 - np.exp(-2.0 * cols * theta))
    for i, s in enumerate(SHIFTS):
        constants[3 + i] = np.exp(-s * constants[0])
    return (
        forward.reshape(2, devices * 8, FREQ).astype(np.float32),
        backward.astype(np.float32),
        constants.astype(np.float32),
    )


def ahead(x, s):
    return pltpu.roll(x, WIDTH - s, 1)


def behind(x, s):
    return pltpu.roll(x, s, 1)


def wrap(ref, above=True, below=True):
    last = ref.shape[0] - 2
    if above:
        ref[0] = pltpu.roll(ref[last], 1, 0)
    if below:
        ref[last + 1] = pltpu.roll(ref[1], SUB - 1, 0)


def steps(count, body):
    if count <= UNROLL:
        for i in range(count):
            body(i)
    else:

        def step(i, carry):
            for j in range(UNROLL):
                body(i * UNROLL + j)
            return carry

        lax.fori_loop(0, count // UNROLL, step, 0)


def kernel(R, C, *refs):
    (
        swath_h,
        coherence_h,
        counts_h,
        forward_h,
        backward_h,
        constants_h,
        out_h,
        swath,
        coherence,
        counts,
        forward,
        backward,
        constants,
        nat,
        left_pack,
        right_pack,
        near_pack,
        near_got,
        in_left,
        in_right,
        outer,
        far_pack,
        far_got,
        far_corner,
        result,
        qual,
        phase,
        wd,
        wr,
        sd,
        sr,
        v0,
        rdiv0,
        base0,
        first,
        gd,
        gr,
        *rest,
    ) = refs
    levels = []
    for _ in range(3):
        levels.append(rest[:7])
        rest = rest[7:]
    (
        coarse,
        select,
        spread,
        blocks,
        amps,
        near_send,
        near_left,
        near_right,
        ext,
        powers,
        coef,
        load_sem,
        p1_send,
        p1_recv,
        p2_send,
        p2_recv,
        p3_send,
        p3_recv,
        nb_send,
        nb_recv,
        out_sem,
    ) = rest

    r = lax.axis_index("row")
    c = lax.axis_index("col")
    N = CCOLS * C

    loads = [
        pltpu.make_async_copy(swath_h, swath, load_sem.at[0]),
        pltpu.make_async_copy(coherence_h, coherence, load_sem.at[1]),
        pltpu.make_async_copy(counts_h, counts, load_sem.at[2]),
        pltpu.make_async_copy(constants_h, constants, load_sem.at[3]),
        pltpu.make_async_copy(forward_h, forward, load_sem.at[4]),
        pltpu.make_async_copy(backward_h.at[r], backward, load_sem.at[5]),
    ]
    for copy in loads:
        copy.start()

    barrier = pltpu.get_barrier_semaphore()
    for i in sorted(range(1, C), key=lambda i: -min(i, C - i)):
        pl.semaphore_signal(barrier, inc=1, device_id=(r, lax.rem(c + i, C)), device_id_type=MESH)
    for i in (1, R - 1):
        for j in (1, C - 1):
            pl.semaphore_signal(
                barrier, inc=1, device_id=(lax.rem(r + i, R), lax.rem(c + j, C)), device_id_type=MESH
            )
    for i in range(1, R):
        pl.semaphore_signal(barrier, inc=1, device_id=(lax.rem(r + i, R), c), device_id_type=MESH)

    is_up, is_down = r > 0, r < R - 1
    is_left, is_right = c > 0, c < C - 1
    chunks = slice(0, OWN_CHUNKS)
    own = slice(0, ROWS)
    near_below, near_above = slice(ROWS, ROWS + NEAR), slice(EXT - NEAR, EXT)
    far = slice(ROWS + NEAR, EXT - NEAR)
    far_rows = EXT - ROWS - 2 * NEAR
    far_below, far_above = slice(0, far_rows // 2), slice(far_rows // 2, far_rows)

    def clear(ref, *where):
        ref[where] = jnp.zeros(ref.at[where].shape, F32)

    every = slice(None)
    clear(nat, every, chunks, far)
    clear(in_left, far)
    clear(in_right, far)

    @pl.when(jnp.logical_not(is_down))
    def _():
        clear(nat, every, chunks, near_below)
        clear(outer, every, chunks, far_below)
        for ref in (in_left, in_right):
            clear(ref, near_below)
        clear(far_corner, every, far_below)

    @pl.when(jnp.logical_not(is_up))
    def _():
        clear(nat, every, chunks, near_above)
        clear(outer, every, chunks, far_above)
        for ref in (in_left, in_right):
            clear(ref, near_above)
        clear(far_corner, every, far_above)

    @pl.when(jnp.logical_not(is_right))
    def _():
        clear(near_got, 0)
        clear(in_right, near_below)
        clear(in_right, near_above)
        clear(far_got, 0)
        clear(far_corner, 0)
        clear(near_right, every)

    @pl.when(jnp.logical_not(is_left))
    def _():
        clear(near_got, 1)
        clear(in_left, near_below)
        clear(in_left, near_above)
        clear(far_got, 1)
        clear(far_corner, 1)
        clear(near_left, every)

    for copy in loads[:3]:
        copy.wait()
    lane = lax.broadcasted_iota(jnp.int32, (32, 128), 1)

    def prepare(i):
        rows = slice(i * 32, i * 32 + 32)
        for k in range(OWN_CHUNKS):
            span = slice(128 * k, 128 * k + 128)
            level = coherence[rows, span].astype(F32) * (1.0 / (NCLASS - 1))
            q = swath[rows, span].astype(F32) * (level * level)
            ph = counts[rows, span].astype(F32) * (1.0 / LEVELS)
            nat[0, k, rows, :] = q
            nat[1, k, rows, :] = ph
            if k == 0:
                left_pack[rows, :] = jnp.where(lane < 64, q, pltpu.roll(ph, 64, 1))
            if k == OWN_CHUNKS - 1:
                right_pack[rows, :] = jnp.where(lane < 64, pltpu.roll(ph, 64, 1), q)

    for i in range(ROWS // 32):
        prepare(i)
    quarter = ROWS // 4
    lane = lax.broadcasted_iota(jnp.int32, (quarter, 128), 1)
    packed = [jnp.zeros((quarter, 128), F32)] * 2
    for g in range(4):
        rows = slice(quarter * g, quarter * g + quarter)
        turned = (pltpu.roll(left_pack[rows, :], NEAR * g, 1), pltpu.roll(right_pack[rows, :], NEAR * g + 80, 1))
        packed = [jnp.where((lane & 48) == NEAR * g, x, y) for x, y in zip(turned, packed)]
    near_pack[0] = packed[0]
    near_pack[1] = packed[1]
    half = ROWS // 2
    lane = lax.broadcasted_iota(jnp.int32, (half, 128), 1)
    for i, pack in enumerate((left_pack, right_pack)):
        x, y = pltpu.roll(pack[0:half, :], 128 - NEAR, 1), pltpu.roll(pack[half:ROWS, :], NEAR, 1)
        far_pack[i] = jnp.where((lane & 32) == 0, x, y)
    pl.semaphore_wait(barrier, R + C + 2)

    both = jnp.logical_and
    first_rows, last_rows = slice(0, NEAR), slice(ROWS - NEAR, ROWS)
    top_far, bottom_far = slice(NEAR, HALO), slice(ROWS - HALO, ROWS - NEAR)
    up_left, down_left = both(is_up, is_left), both(is_down, is_left)
    up_right, down_right = both(is_up, is_right), both(is_down, is_right)
    plan = [
        (is_left, 0, -1, near_pack.at[0], near_got.at[0], is_right),
        (is_right, 0, 1, near_pack.at[1], near_got.at[1], is_left),
        (up_left, -1, -1, left_pack.at[first_rows], in_right.at[near_below], down_right),
        (down_left, 1, -1, left_pack.at[last_rows], in_right.at[near_above], up_right),
        (up_right, -1, 1, right_pack.at[first_rows], in_left.at[near_below], down_left),
        (down_right, 1, 1, right_pack.at[last_rows], in_left.at[near_above], up_left),
        (is_up, -1, 0, nat.at[:, chunks, first_rows, :], nat.at[:, chunks, near_below, :], is_down),
        (is_down, 1, 0, nat.at[:, chunks, last_rows, :], nat.at[:, chunks, near_above, :], is_up),
        (is_left, 0, -1, far_pack.at[0], far_got.at[0], is_right),
        (is_right, 0, 1, far_pack.at[1], far_got.at[1], is_left),
        (up_left, -1, -1, left_pack.at[top_far], far_corner.at[0, far_below], down_right),
        (down_left, 1, -1, left_pack.at[bottom_far], far_corner.at[0, far_above], up_right),
        (up_right, -1, 1, right_pack.at[top_far], far_corner.at[1, far_below], down_left),
        (down_right, 1, 1, right_pack.at[bottom_far], far_corner.at[1, far_above], up_left),
        (is_up, -1, 0, nat.at[:, chunks, top_far, :], outer.at[:, chunks, far_below, :], is_down),
        (is_down, 1, 0, nat.at[:, chunks, bottom_far, :], outer.at[:, chunks, far_above, :], is_up),
    ]
    halo_copies = []
    for i, (sends, dr, dc, source, target, receives) in enumerate(plan):
        copy = pltpu.make_async_remote_copy(
            src_ref=source,
            dst_ref=target,
            send_sem=p1_send.at[i],
            recv_sem=p1_recv.at[i],
            device_id=(lax.rem(r + dr + R, R), lax.rem(c + dc + C, C)),
            device_id_type=MESH,
        )
        halo_copies.append((sends, receives, copy))
        pl.when(sends)(copy.start)

    for copy in loads[3:]:
        copy.wait()
    theta = constants[0:1, :]
    green = constants[1:2, :]
    inverse = constants[2:3, :]
    yy = lax.broadcasted_iota(jnp.int32, (CCOLS, FREQ), 0)
    last = CCOLS - 1
    powers[0] = jnp.exp(-theta * (last - yy).astype(F32))
    powers[1] = jnp.exp(-theta * yy.astype(F32))
    powers[2] = jnp.where(yy <= last - 3, jnp.exp(-theta * jnp.maximum(last - 3 - yy, 0).astype(F32)), 0.0)
    powers[3] = jnp.where(yy >= 3, jnp.exp(-theta * jnp.maximum(yy - 3, 0).astype(F32)), 0.0)

    def decay(n):
        return jnp.exp(-theta * n.astype(F32))

    def directly(n, inside):
        return jnp.where(inside, decay(jnp.maximum(n, 0)), 0.0)

    for i in range(C):
        rev = C - 1 - i
        coef[0, i, 0:1, :] = directly(CCOLS * (c - 1 - i) - 3, i < c - 1) + inverse * decay(
            N + CCOLS * rev + CCOLS * c - 3
        )
        coef[0, i, 1:2, :] = inverse * decay(CCOLS * i + CCOLS * c - 3)
        coef[1, i, 0:1, :] = inverse * decay(CCOLS * (C - 1 - c) + CCOLS * rev - 3)
        coef[1, i, 1:2, :] = directly(CCOLS * (i - c - 1) - 3, i > c + 1) + inverse * decay(
            2 * N - CCOLS * (c + 1) + CCOLS * i - 3
        )
    at = lax.broadcasted_iota(jnp.int32, (COLS, 128), 0)
    to = lax.broadcasted_iota(jnp.int32, (COLS, 128), 1)
    select[...] = jnp.where((to < 64) & (at == STEP * (to & 31)), 1.0, 0.0).astype(F32)
    at = lax.broadcasted_iota(jnp.int32, (PAD, WIDTH), 0)
    to = lax.broadcasted_iota(jnp.int32, (PAD, WIDTH), 1) >> GRIDS
    spread[...] = jnp.where(at == jnp.where(to < CCOLS + 3, to + 8, to + 8 - WIDTH // STEP), 1.0, 0.0).astype(F32)
    ext[...] = jnp.zeros((PAD, FREQ), F32)

    for _, receives, copy in halo_copies[:8]:
        pl.when(receives)(copy.wait_recv)
    lane = lax.broadcasted_iota(jnp.int32, (quarter, 128), 1)
    for g in range(4):
        rows = slice(quarter * g, quarter * g + quarter)
        in_right[rows, :] = jnp.where((lane & 63) < NEAR, pltpu.roll(near_got[0], (128 - NEAR * g) % 128, 1), 0.0)
        in_left[rows, :] = jnp.where((lane & 63) >= 64 - NEAR, pltpu.roll(near_got[1], 48 - NEAR * g, 1), 0.0)

    def arrange():
        lane = lax.broadcasted_iota(jnp.int32, (SUB, 128), 1)
        for p in range(STEP):
            rows = pl.ds(p, SUB, stride=STEP)
            for k in range(OWN_CHUNKS):
                span = slice(128 * k, 128 * k + 128)
                qual[p + 1, :, span] = nat.at[0, k][rows, :]
                phase[p + 1, :, span] = nat.at[1, k][rows, :]
            a, b = in_right[rows, :], in_left[rows, :]
            qual[p + 1, :, COLS:WIDTH] = jnp.where(lane < 64, a, b)
            phase[p + 1, :, COLS:WIDTH] = pltpu.roll(jnp.where(lane < 64, b, a), 64, 1)
        wrap(qual, above=False)
        wrap(phase, above=False)

    def steep(u):
        return u - jnp.floor(u + 0.5)

    def make_faces(p):
        for h in HALVES:
            q, ph = qual[p + 1, h], phase[p + 1, h]
            wd[p + 1, h] = jnp.minimum(q, qual[p + 2, h])
            wr[p, h] = jnp.minimum(q, ahead(q, 1))
            sd[p + 1, h] = steep(phase[p + 2, h] - ph)
            sr[p, h] = steep(ahead(ph, 1) - ph)

    def start_first(p):
        for h in HALVES:
            a, au, b = wd[p + 1, h], wd[p, h], wr[p, h]
            fr = b * sr[p, h]
            source = au * sd[p, h] - a * sd[p + 1, h] + behind(fr, 1) - fr
            rdiv = DAMPING / jnp.maximum(a + au + b + behind(b, 1), DIAG_FLOOR)
            rdiv0[p, h] = rdiv
            v0[p + 1, h] = source * rdiv

    def open_first():
        arrange()
        steps(STEP, make_faces)
        wrap(wd, below=False)
        wrap(sd, below=False)
        steps(STEP, start_first)
        wrap(v0)

    def restrict_fine():
        src, a1, b1 = levels[0][0], levels[0][1], levels[0][2]

        def body(i):
            for h in HALVES:
                va, v1, v2, vb = v0[2 * i, h], v0[2 * i + 1, h], v0[2 * i + 2, h], v0[2 * i + 3, h]
                a_odd = wd[2 * i + 2, h]
                y = a_odd * (vb - v2 - sd[2 * i + 2, h]) - wd[2 * i, h] * (v1 - va - sd[2 * i, h])
                b0, b_odd = wr[2 * i, h], wr[2 * i + 1, h]
                g = b0 * (ahead(v1, 1) - v1 - sr[2 * i, h]) + b_odd * (ahead(v2, 1) - v2 - sr[2 * i + 1, h])
                src[i, h] = y + ahead(y + g, 1) - behind(g, 1)
                a1[i + 1, h] = a_odd + ahead(a_odd, 1)
                b1[i, h] = ahead(b0 + b_odd, 1)

        steps(STEP // 2, body)
        wrap(a1, below=False)

    def down(level):
        s = 2**level
        count = STEP // s
        src, a, b, rdiv, v, _, _ = levels[level - 1]

        def smooth(p):
            for h in HALVES:
                bb = b[p, h]
                d = DAMPING / jnp.maximum(a[p + 1, h] + a[p, h] + bb + behind(bb, s), DIAG_FLOOR)
                rdiv[p, h] = d
                v[p + 1, h] = src[p, h] * d

        steps(count, smooth)
        wrap(v)
        if level < GRIDS - 1:
            src_n, a_n, b_n = levels[level][0], levels[level][1], levels[level][2]
        else:
            src_n, a_n, b_n = None, None, None

        def body(i):
            for h in HALVES:
                va, v1, v2, vb = v[2 * i, h], v[2 * i + 1, h], v[2 * i + 2, h], v[2 * i + 3, h]
                a_odd = a[2 * i + 2, h]
                t = src[2 * i, h] + src[2 * i + 1, h] + a_odd * (vb - v2) - a[2 * i, h] * (v1 - va)
                b0, b_odd = b[2 * i, h], b[2 * i + 1, h]
                g = b0 * (ahead(v1, s) - v1) + b_odd * (ahead(v2, s) - v2)
                out = t + ahead(t + g, s) - behind(g, s)
                if src_n is None:
                    coarse[h] = out
                else:
                    src_n[i, h] = out
                    a_n[i + 1, h] = a_odd + ahead(a_odd, s)
                    b_n[i, h] = ahead(b0 + b_odd, s)

        steps(count // 2, body)
        if a_n is not None:
            wrap(a_n, below=False)

    def settle(level):
        s = 2**level
        count = STEP // s
        src, a, b, rdiv, v, base, _ = levels[level - 1]

        def body(i):
            for h in HALVES:
                va, v1, v2, vb = v[2 * i, h], v[2 * i + 1, h], v[2 * i + 2, h], v[2 * i + 3, h]
                g0 = a[2 * i, h] * (v1 - va)
                g1 = a[2 * i + 1, h] * (v2 - v1)
                g2 = a[2 * i + 2, h] * (vb - v2)
                f1 = b[2 * i, h] * (ahead(v1, s) - v1)
                f2 = b[2 * i + 1, h] * (ahead(v2, s) - v2)
                base[2 * i, h] = v1 + (src[2 * i, h] + g1 - g0 + f1 - behind(f1, s)) * rdiv[2 * i, h]
                base[2 * i + 1, h] = v2 + (src[2 * i + 1, h] + g2 - g1 + f2 - behind(f2, s)) * rdiv[2 * i + 1, h]

        steps(count // 2, body)

    def settle_fine():
        def body(i):
            for h in HALVES:
                va, v1, v2, vb = v0[2 * i, h], v0[2 * i + 1, h], v0[2 * i + 2, h], v0[2 * i + 3, h]
                g0 = wd[2 * i, h] * (v1 - va - sd[2 * i, h])
                g1 = wd[2 * i + 1, h] * (v2 - v1 - sd[2 * i + 1, h])
                g2 = wd[2 * i + 2, h] * (vb - v2 - sd[2 * i + 2, h])
                f1 = wr[2 * i, h] * (ahead(v1, 1) - v1 - sr[2 * i, h])
                f2 = wr[2 * i + 1, h] * (ahead(v2, 1) - v2 - sr[2 * i + 1, h])
                base0[2 * i, h] = v1 + (g1 - g0 + f1 - behind(f1, 1)) * rdiv0[2 * i, h]
                base0[2 * i + 1, h] = v2 + (g2 - g1 + f2 - behind(f2, 1)) * rdiv0[2 * i + 1, h]

        steps(STEP // 2, body)

    def settle_all():
        settle_fine()
        for level in range(1, GRIDS):
            settle(level)

    def climb(level, put):
        s = 2**level
        count = STEP // s
        if level:
            _, a, b, rdiv, _, base, _ = levels[level - 1]
        else:
            a, b, rdiv, base = wd, wr, rdiv0, base0
        if level == GRIDS - 1:
            above_it, below_it = pltpu.roll(coarse[...], 1, 0), pltpu.roll(coarse[...], SUB - 1, 0)

        def correction(i, h):
            if level == GRIDS - 1:
                return (above_it[h], coarse[h], below_it[h])[i + 1]
            x = levels[level][6][i + 1, h]
            column = lax.broadcasted_iota(jnp.int32, x.shape, 1)
            return jnp.where((column & s) == 0, x, behind(x, s))

        for h in HALVES:
            x = correction(0, h)
            upper = x - correction(-1, h)
            for i in range(count // 2):
                after = correction(i + 1, h)
                lower = after - x
                side = ahead(x, s) - x
                f1, f2 = b[2 * i, h] * side, b[2 * i + 1, h] * side
                put(2 * i, h, base[2 * i, h] + x + (f1 - behind(f1, s) - a[2 * i, h] * upper) * rdiv[2 * i, h])
                put(
                    2 * i + 1,
                    h,
                    base[2 * i + 1, h] + x + (f2 - behind(f2, s) + a[2 * i + 2, h] * lower) * rdiv[2 * i + 1, h],
                )
                x, upper = after, lower

    def ascend(put_fine):
        for level in range(GRIDS - 1, 0, -1):
            out = levels[level - 1][6]

            def put(p, h, x, out=out):
                out[p + 1, h] = x

            climb(level, put)
            wrap(out)
        climb(0, put_fine)

    def coarse_solve(turn, meanwhile):
        a3, b3 = levels[2][1:3]
        column = lax.broadcasted_iota(jnp.int32, (SUB, COLS), 1)
        line = lax.broadcasted_iota(jnp.int32, (SUB, COLS), 0)
        here = slice(0, COLS)
        part = jnp.where((column & 7) == 0, a3[2, :, here], 0.0) + jnp.where(
            (column & 15) == 8, b3[0, :, here] + b3[1, :, here], 0.0
        )
        part = jnp.where((line < CROWS) & ((column & 7) == 0), part, 0.0)
        local = jnp.sum(jnp.sum(part, axis=1, keepdims=True), axis=0, keepdims=True)
        mine = jnp.dot(coarse[:, here], select[...], precision=HIGHEST, preferred_element_type=F32)
        spot = lax.broadcasted_iota(jnp.int32, (8, 128), 1)
        blocks[turn, r] = jnp.where(spot < 32, mine[0:8], jnp.where(spot < 64, mine[8:16], local))
        copies = []
        for i in sorted(range(1, R), key=lambda i: -min(i, R - i)):
            copy = pltpu.make_async_remote_copy(
                src_ref=blocks.at[turn, r],
                dst_ref=blocks.at[turn, r],
                send_sem=p2_send.at[turn, i - 1],
                recv_sem=p2_recv.at[turn, i - 1],
                device_id=(lax.rem(r + i, R), c),
                device_id_type=MESH,
            )
            copy.start()
            copies.append(copy)
        for copy in copies:
            copy.wait_recv()
        every = blocks[turn].reshape(R * 8, 128).T
        hat = jnp.dot(every[0:32], forward[0], precision=HIGHEST, preferred_element_type=F32) + jnp.dot(
            every[32:64], forward[1], precision=HIGHEST, preferred_element_type=F32
        )
        rows_sum = jnp.sum(every[64:65], axis=1, keepdims=True) * 0.125

        def total(n):
            return jnp.sum(powers[n] * hat, axis=0, keepdims=True)

        mode = lax.broadcasted_iota(jnp.int32, (1, FREQ), 1)
        amps[turn, c, 0:1, :] = jnp.where(mode < CROWS * R, total(0), rows_sum)
        amps[turn, c, 1:2, :] = total(1)
        near_send[turn, 0, 0:1, :] = total(2)
        near_send[turn, 0, 1:4, :] = hat[CCOLS - 3 : CCOLS]
        near_send[turn, 1, 0:3, :] = hat[0:3]
        near_send[turn, 1, 3:4, :] = total(3)
        for i in sorted(range(1, C), key=lambda i: -min(i, C - i)):
            copy = pltpu.make_async_remote_copy(
                src_ref=amps.at[turn, c],
                dst_ref=amps.at[turn, c],
                send_sem=p3_send.at[turn, i - 1],
                recv_sem=p3_recv.at[turn, i - 1],
                device_id=(r, lax.rem(c + i, C)),
                device_id_type=MESH,
            )
            copy.start()
            copies.append(copy)
        rightward = pltpu.make_async_remote_copy(
            src_ref=near_send.at[turn, 0],
            dst_ref=near_left.at[turn],
            send_sem=nb_send.at[turn, 0],
            recv_sem=nb_recv.at[turn, 0],
            device_id=(r, lax.rem(c + 1, C)),
            device_id_type=MESH,
        )
        leftward = pltpu.make_async_remote_copy(
            src_ref=near_send.at[turn, 1],
            dst_ref=near_right.at[turn],
            send_sem=nb_send.at[turn, 1],
            recv_sem=nb_recv.at[turn, 1],
            device_id=(r, lax.rem(c + C - 1, C)),
            device_id_type=MESH,
        )
        pl.when(is_right)(rightward.start)
        pl.when(is_left)(leftward.start)
        meanwhile()
        pl.when(is_left)(rightward.wait_recv)
        pl.when(is_right)(leftward.wait_recv)
        for copy in copies[R - 1 :]:
            copy.wait_recv()
        into_left = jnp.zeros((2, FREQ), F32)
        into_right = jnp.zeros((2, FREQ), F32)
        weight = jnp.zeros((2, FREQ), F32)
        for i in range(C):
            x = amps[turn, i]
            into_left += coef[0, i] * x
            into_right += coef[1, i] * x
            weight += x
        into_left = into_left[0:1] + into_left[1:2]
        into_right = into_right[0:1] + into_right[1:2]
        weight = jnp.sum(jnp.where(mode == FREQ - 1, weight[0:1], 0.0), axis=1, keepdims=True)
        grid_rows, grid_cols = CROWS * R, CCOLS * C
        mean = weight * (1.0 / ((grid_rows - 1) * grid_cols + grid_rows * (grid_cols - 1))) + EPSILON
        ext[4:8, :] = near_left[turn]
        ext[4:5, :] = near_left[turn, 0:1, :] + into_left
        ext[8 : 8 + CCOLS, :] = hat
        ext[8 + CCOLS : 12 + CCOLS, :] = near_right[turn]
        ext[11 + CCOLS : 12 + CCOLS, :] = near_right[turn, 3:4, :] + into_right
        hats = ext[...]
        place = lax.broadcasted_iota(jnp.int32, (PAD, FREQ), 0)
        going_right = hats
        going_left = hats
        for i, s in enumerate(SHIFTS):
            q = constants[3 + i : 4 + i, :]
            going_right += q * jnp.where(place >= s, pltpu.roll(going_right, s, 0), 0.0)
            going_left += q * jnp.where(place < PAD - s, pltpu.roll(going_left, PAD - s, 0), 0.0)
        modes = (going_right + going_left - hats) * (green / mean)
        values = lax.dot_general(
            backward[...], modes, (((1,), (1,)), ((), ())), precision=HIGHEST, preferred_element_type=F32
        )
        coarse[...] = jnp.dot(values, spread[...], precision=HIGHEST, preferred_element_type=F32)
        return copies, rightward, leftward

    def descend():
        restrict_fine()
        for level in range(1, GRIDS):
            down(level)

    def widen():
        for _, receives, copy in halo_copies[8:]:
            pl.when(receives)(copy.wait_recv)
        nat[:, chunks, far, :] = outer[...]
        lane = lax.broadcasted_iota(jnp.int32, (half, 128), 1) & 63
        for i, ref in enumerate((in_right, in_left)):
            ref[far, :] = far_corner[i]
            for g in range(2):
                rows = slice(half * g, half * g + half)
                x = pltpu.roll(far_got[i], NEAR if g == 0 else 128 - NEAR, 1)
                ref[rows, :] = jnp.where((lane >= NEAR) & (lane < HALO), x, ref[rows, :])
        open_first()
        descend()
        settle_all()

    def put_first(p, h, x):
        first[p + 1, h] = x

    def put_result(p, h, x):
        rows = pl.ds(STEP * h.start + p, 8, stride=STEP)
        for k in range(OWN_CHUNKS):
            result.at[k][rows, :] = x[:, 128 * k : 128 * k + 128] * TURN

    open_first()
    descend()
    sent = [coarse_solve(0, widen)]
    ascend(put_first)
    wrap(first)

    def reweight(p):
        for h in HALVES:
            f = first[p + 1, h]
            e = first[p + 2, h] - f - sd[p + 1, h]
            a = wd[p + 1, h] / jnp.maximum(jnp.abs(e) * TURN, ERROR_FLOOR)
            wd[p + 1, h] = a
            gd[p + 1, h] = a * e
            e = ahead(f, 1) - f - sr[p, h]
            b = wr[p, h] / jnp.maximum(jnp.abs(e) * TURN, ERROR_FLOOR)
            wr[p, h] = b
            gr[p, h] = b * e

    steps(STEP, reweight)
    wrap(wd, below=False)
    wrap(gd, below=False)

    def start_second(p):
        for h in HALVES:
            b, f = wr[p, h], gr[p, h]
            rdiv = DAMPING / jnp.maximum(wd[p + 1, h] + wd[p, h] + b + behind(b, 1), DIAG_FLOOR)
            rdiv0[p, h] = rdiv
            v0[p + 1, h] = first[p + 1, h] + (gd[p + 1, h] - gd[p, h] + f - behind(f, 1)) * rdiv

    steps(STEP, start_second)
    wrap(v0)
    descend()
    sent.append(coarse_solve(1, settle_all))
    ascend(put_result)

    outs = []
    for k in range(OWN_CHUNKS):
        span = slice(128 * k, 128 * k + 128)
        copy = pltpu.make_async_copy(result.at[k, own, :], out_h.at[:, span], out_sem.at[k])
        copy.start()
        outs.append(copy)
    for sends, _, copy in halo_copies:
        pl.when(sends)(copy.wait_send)
    for copies, rightward, leftward in sent:
        for copy in copies:
            copy.wait_send()
        pl.when(is_right)(rightward.wait_send)
        pl.when(is_left)(leftward.wait_send)
    for copy in outs:
        copy.wait()


def scratch(R, C):
    def field(count):
        return pltpu.VMEM((count, SUB, WIDTH), F32)

    shapes = [
        pltpu.VMEM((ROWS, COLS), jnp.int32),
        pltpu.VMEM((ROWS, COLS), jnp.int32),
        pltpu.VMEM((ROWS, COLS), jnp.int32),
        pltpu.VMEM((2, R * 8, FREQ), F32),
        pltpu.VMEM((SUB, FREQ), F32),
        pltpu.VMEM((16, FREQ), F32),
        pltpu.VMEM((2, OWN_CHUNKS, EXT, 128), F32),
        pltpu.VMEM((ROWS, 128), F32),
        pltpu.VMEM((ROWS, 128), F32),
        pltpu.VMEM((2, ROWS // 4, 128), F32),
        pltpu.VMEM((2, ROWS // 4, 128), F32),
        pltpu.VMEM((EXT, 128), F32),
        pltpu.VMEM((EXT, 128), F32),
        pltpu.VMEM((2, OWN_CHUNKS, EXT - ROWS - 2 * NEAR, 128), F32),
        pltpu.VMEM((2, ROWS // 2, 128), F32),
        pltpu.VMEM((2, ROWS // 2, 128), F32),
        pltpu.VMEM((2, EXT - ROWS - 2 * NEAR, 128), F32),
        pltpu.VMEM((OWN_CHUNKS, EXT, 128), F32),
    ]
    padded, plain = STEP + 2, STEP
    shapes += [field(n) for n in (padded, padded, padded, plain, padded, plain, padded, plain, plain, padded, padded, plain)]
    for level in range(1, GRIDS):
        n = STEP >> level
        shapes += [field(m) for m in (n, n + 2, n, n, n + 2, n, n + 2)]
    shapes += [
        pltpu.VMEM((SUB, WIDTH), F32),
        pltpu.VMEM((COLS, 128), F32),
        pltpu.VMEM((PAD, WIDTH), F32),
        pltpu.VMEM((2, R, 8, 128), F32),
        pltpu.VMEM((2, C, 2, FREQ), F32),
        pltpu.VMEM((2, 2, 4, FREQ), F32),
        pltpu.VMEM((2, 4, FREQ), F32),
        pltpu.VMEM((2, 4, FREQ), F32),
        pltpu.VMEM((PAD, FREQ), F32),
        pltpu.VMEM((4, CCOLS, FREQ), F32),
        pltpu.VMEM((2, C, 2, FREQ), F32),
        pltpu.SemaphoreType.DMA((6,)),
        pltpu.SemaphoreType.DMA((16,)),
        pltpu.SemaphoreType.DMA((16,)),
        pltpu.SemaphoreType.DMA((2, R - 1)),
        pltpu.SemaphoreType.DMA((2, R - 1)),
        pltpu.SemaphoreType.DMA((2, C - 1)),
        pltpu.SemaphoreType.DMA((2, C - 1)),
        pltpu.SemaphoreType.DMA((2, 2)),
        pltpu.SemaphoreType.DMA((2, 2)),
        pltpu.SemaphoreType.DMA((OWN_CHUNKS,)),
    ]
    return shapes


def solution(mesh):
    R, C = mesh.shape["row"], mesh.shape["col"]
    forward, backward, constants = tables(CROWS * R, CCOLS * C)

    def body(swath, coherence, counts):
        return pl.pallas_call(
            functools.partial(kernel, R, C),
            out_shape=jax.ShapeDtypeStruct((ROWS, COLS), F32),
            in_specs=[pl.BlockSpec(memory_space=pl.ANY)] * 6,
            out_specs=pl.BlockSpec(memory_space=pl.ANY),
            scratch_shapes=scratch(R, C),
            compiler_params=pltpu.CompilerParams(
                collective_id=0, has_side_effects=True
            ),
        )(swath, coherence, counts, jnp.asarray(forward), jnp.asarray(backward), jnp.asarray(constants))

    return jax.shard_map(
        body,
        mesh=mesh,
        in_specs=(P("row", "col"), P("row", "col"), P("row", "col")),
        out_specs=P("row", "col"),
        check_vma=False,
    )
```

```python
import functools

import jax
import jax.numpy as jnp
import numpy as np
from jax import lax
from jax.experimental import pallas as pl
from jax.experimental.pallas import tpu as pltpu
from jax.sharding import PartitionSpec as P

MESH = pl.DeviceIdType.MESH
HIGHEST = lax.Precision.HIGHEST
F32 = jnp.float32

GRIDS = 4
NCLASS = 8
LEVELS = 256
DAMPING = 0.8
DIAG_FLOOR = 0.5
TURN = 2.0 * np.pi
ERROR_FLOOR = 0.5
EPSILON = 1e-6
SCREEN_WIDTH = 4.0

STEP = 2**GRIDS
HALO = 48
NEAR = 16
ROWS = 160
COLS = 512
CROWS = ROWS // STEP
CCOLS = COLS // STEP
EXT = ROWS + 2 * HALO
SUB = EXT // STEP
OWN_CHUNKS = COLS // 128
CHUNKS = OWN_CHUNKS + 1
WIDTH = CHUNKS * 128
FREQ = 256
PAD = 48
SHIFTS = (1, 2, 4, 8, 16, 32)
UNROLL = 16
HALVES = tuple(slice(h, h + 8) for h in range(0, SUB, 8))


def tables(rows, cols):
    devices = rows // CROWS
    freq = np.arange(rows)[:, None]
    cosine = np.cos(np.pi * (np.arange(rows)[None, :] + 0.5) * freq / rows) * np.sqrt(2.0 / rows)
    cosine[0] *= np.sqrt(0.5)
    forward = np.zeros((2, devices, 8, FREQ))
    backward = np.zeros((devices, SUB, FREQ))
    for d in range(devices):
        for k in range(CROWS):
            forward[k // 8, d, k % 8, :rows] = cosine[:, d * CROWS + k]
        for k in range(SUB):
            place = d * CROWS + (k if k < CROWS + HALO // STEP else k - SUB)
            if 0 <= place < rows:
                backward[d, k, :rows] = cosine[:, place]
    shift = 2.0 - 2.0 * np.cos(np.pi * np.arange(rows) / rows) + (SCREEN_WIDTH / cols) ** 2
    theta = 2.0 * np.arcsinh(np.sqrt(shift) / 2.0)
    constants = np.zeros((16, FREQ))
    constants[0] = 1.0
    constants[0, :rows] = theta
    constants[1, :rows] = 1.0 / (2.0 * np.sinh(theta))
    constants[2] = 1.0
    constants[2, :rows] = 1.0 / (1.0 - np.exp(-2.0 * cols * theta))
    for i, s in enumerate(SHIFTS):
        constants[3 + i] = np.exp(-s * constants[0])
    return (
        forward.reshape(2, devices * 8, FREQ).astype(np.float32),
        backward.astype(np.float32),
        constants.astype(np.float32),
    )


def ahead(x, s):
    return pltpu.roll(x, WIDTH - s, 1)


def behind(x, s):
    return pltpu.roll(x, s, 1)


def wrap(ref, above=True, below=True):
    last = ref.shape[0] - 2
    if above:
        ref[0] = pltpu.roll(ref[last], 1, 0)
    if below:
        ref[last + 1] = pltpu.roll(ref[1], SUB - 1, 0)


def steps(count, body):
    if count <= UNROLL:
        for i in range(count):
            body(i)
    else:

        def step(i, carry):
            for j in range(UNROLL):
                body(i * UNROLL + j)
            return carry

        lax.fori_loop(0, count // UNROLL, step, 0)


def kernel(R, C, *refs):
    (
        swath_h,
        coherence_h,
        counts_h,
        forward_h,
        backward_h,
        constants_h,
        out_h,
        swath,
        coherence,
        counts,
        forward,
        backward,
        constants,
        nat,
        left_pack,
        right_pack,
        near_pack,
        near_got,
        in_left,
        in_right,
        outer,
        far_pack,
        far_got,
        far_corner,
        result,
        qual,
        phase,
        wd,
        wr,
        sd,
        sr,
        v0,
        rdiv0,
        base0,
        first,
        gd,
        gr,
        *rest,
    ) = refs
    levels = []
    for _ in range(3):
        levels.append(rest[:7])
        rest = rest[7:]
    (
        coarse,
        select,
        spread,
        blocks,
        amps,
        near_send,
        near_left,
        near_right,
        ext,
        powers,
        coef,
        load_sem,
        p1_send,
        p1_recv,
        p2_send,
        p2_recv,
        p3_send,
        p3_recv,
        nb_send,
        nb_recv,
        out_sem,
    ) = rest

    r = lax.axis_index("row")
    c = lax.axis_index("col")
    N = CCOLS * C

    loads = [
        pltpu.make_async_copy(swath_h, swath, load_sem.at[0]),
        pltpu.make_async_copy(coherence_h, coherence, load_sem.at[1]),
        pltpu.make_async_copy(counts_h, counts, load_sem.at[2]),
        pltpu.make_async_copy(constants_h, constants, load_sem.at[3]),
        pltpu.make_async_copy(forward_h, forward, load_sem.at[4]),
        pltpu.make_async_copy(backward_h.at[r], backward, load_sem.at[5]),
    ]
    for copy in loads:
        copy.start()

    barrier = pltpu.get_barrier_semaphore()
    for i in sorted(range(1, C), key=lambda i: -min(i, C - i)):
        pl.semaphore_signal(barrier, inc=1, device_id=(r, lax.rem(c + i, C)), device_id_type=MESH)
    for i in (1, R - 1):
        for j in (1, C - 1):
            pl.semaphore_signal(
                barrier, inc=1, device_id=(lax.rem(r + i, R), lax.rem(c + j, C)), device_id_type=MESH
            )
    for i in range(1, R):
        pl.semaphore_signal(barrier, inc=1, device_id=(lax.rem(r + i, R), c), device_id_type=MESH)

    is_up, is_down = r > 0, r < R - 1
    is_left, is_right = c > 0, c < C - 1
    chunks = slice(0, OWN_CHUNKS)
    own = slice(0, ROWS)
    near_below, near_above = slice(ROWS, ROWS + NEAR), slice(EXT - NEAR, EXT)
    far = slice(ROWS + NEAR, EXT - NEAR)
    far_rows = EXT - ROWS - 2 * NEAR
    far_below, far_above = slice(0, far_rows // 2), slice(far_rows // 2, far_rows)

    def clear(ref, *where):
        ref[where] = jnp.zeros(ref.at[where].shape, F32)

    every = slice(None)
    clear(nat, every, chunks, far)
    clear(in_left, far)
    clear(in_right, far)

    @pl.when(jnp.logical_not(is_down))
    def _():
        clear(nat, every, chunks, near_below)
        clear(outer, every, chunks, far_below)
        for ref in (in_left, in_right):
            clear(ref, near_below)
        clear(far_corner, every, far_below)

    @pl.when(jnp.logical_not(is_up))
    def _():
        clear(nat, every, chunks, near_above)
        clear(outer, every, chunks, far_above)
        for ref in (in_left, in_right):
            clear(ref, near_above)
        clear(far_corner, every, far_above)

    @pl.when(jnp.logical_not(is_right))
    def _():
        clear(near_got, 0)
        clear(in_right, near_below)
        clear(in_right, near_above)
        clear(far_got, 0)
        clear(far_corner, 0)
        clear(near_right, every)

    @pl.when(jnp.logical_not(is_left))
    def _():
        clear(near_got, 1)
        clear(in_left, near_below)
        clear(in_left, near_above)
        clear(far_got, 1)
        clear(far_corner, 1)
        clear(near_left, every)

    for copy in loads[:3]:
        copy.wait()
    lane = lax.broadcasted_iota(jnp.int32, (32, 128), 1)

    def prepare(i):
        rows = slice(i * 32, i * 32 + 32)
        for k in range(OWN_CHUNKS):
            span = slice(128 * k, 128 * k + 128)
            level = coherence[rows, span].astype(F32) * (1.0 / (NCLASS - 1))
            q = swath[rows, span].astype(F32) * (level * level)
            ph = counts[rows, span].astype(F32) * (1.0 / LEVELS)
            nat[0, k, rows, :] = q
            nat[1, k, rows, :] = ph
            if k == 0:
                left_pack[rows, :] = jnp.where(lane < 64, q, pltpu.roll(ph, 64, 1))
            if k == OWN_CHUNKS - 1:
                right_pack[rows, :] = jnp.where(lane < 64, pltpu.roll(ph, 64, 1), q)

    for i in range(ROWS // 32):
        prepare(i)
    quarter = ROWS // 4
    lane = lax.broadcasted_iota(jnp.int32, (quarter, 128), 1)
    packed = [jnp.zeros((quarter, 128), F32)] * 2
    for g in range(4):
        rows = slice(quarter * g, quarter * g + quarter)
        turned = (pltpu.roll(left_pack[rows, :], NEAR * g, 1), pltpu.roll(right_pack[rows, :], NEAR * g + 80, 1))
        packed = [jnp.where((lane & 48) == NEAR * g, x, y) for x, y in zip(turned, packed)]
    near_pack[0] = packed[0]
    near_pack[1] = packed[1]
    half = ROWS // 2
    lane = lax.broadcasted_iota(jnp.int32, (half, 128), 1)
    for i, pack in enumerate((left_pack, right_pack)):
        x, y = pltpu.roll(pack[0:half, :], 128 - NEAR, 1), pltpu.roll(pack[half:ROWS, :], NEAR, 1)
        far_pack[i] = jnp.where((lane & 32) == 0, x, y)
    pl.semaphore_wait(barrier, R + C + 2)

    both = jnp.logical_and
    first_rows, last_rows = slice(0, NEAR), slice(ROWS - NEAR, ROWS)
    top_far, bottom_far = slice(NEAR, HALO), slice(ROWS - HALO, ROWS - NEAR)
    up_left, down_left = both(is_up, is_left), both(is_down, is_left)
    up_right, down_right = both(is_up, is_right), both(is_down, is_right)
    plan = [
        (is_left, 0, -1, near_pack.at[0], near_got.at[0], is_right),
        (is_right, 0, 1, near_pack.at[1], near_got.at[1], is_left),
        (up_left, -1, -1, left_pack.at[first_rows], in_right.at[near_below], down_right),
        (down_left, 1, -1, left_pack.at[last_rows], in_right.at[near_above], up_right),
        (up_right, -1, 1, right_pack.at[first_rows], in_left.at[near_below], down_left),
        (down_right, 1, 1, right_pack.at[last_rows], in_left.at[near_above], up_left),
        (is_up, -1, 0, nat.at[:, chunks, first_rows, :], nat.at[:, chunks, near_below, :], is_down),
        (is_down, 1, 0, nat.at[:, chunks, last_rows, :], nat.at[:, chunks, near_above, :], is_up),
        (is_left, 0, -1, far_pack.at[0], far_got.at[0], is_right),
        (is_right, 0, 1, far_pack.at[1], far_got.at[1], is_left),
        (up_left, -1, -1, left_pack.at[top_far], far_corner.at[0, far_below], down_right),
        (down_left, 1, -1, left_pack.at[bottom_far], far_corner.at[0, far_above], up_right),
        (up_right, -1, 1, right_pack.at[top_far], far_corner.at[1, far_below], down_left),
        (down_right, 1, 1, right_pack.at[bottom_far], far_corner.at[1, far_above], up_left),
        (is_up, -1, 0, nat.at[:, chunks, top_far, :], outer.at[:, chunks, far_below, :], is_down),
        (is_down, 1, 0, nat.at[:, chunks, bottom_far, :], outer.at[:, chunks, far_above, :], is_up),
    ]
    halo_copies = []
    for i, (sends, dr, dc, source, target, receives) in enumerate(plan):
        copy = pltpu.make_async_remote_copy(
            src_ref=source,
            dst_ref=target,
            send_sem=p1_send.at[i],
            recv_sem=p1_recv.at[i],
            device_id=(lax.rem(r + dr + R, R), lax.rem(c + dc + C, C)),
            device_id_type=MESH,
        )
        halo_copies.append((sends, receives, copy))
        pl.when(sends)(copy.start)

    for copy in loads[3:]:
        copy.wait()
    theta = constants[0:1, :]
    green = constants[1:2, :]
    inverse = constants[2:3, :]
    yy = lax.broadcasted_iota(jnp.int32, (CCOLS, FREQ), 0)
    last = CCOLS - 1
    powers[0] = jnp.exp(-theta * (last - yy).astype(F32))
    powers[1] = jnp.exp(-theta * yy.astype(F32))
    powers[2] = jnp.where(yy <= last - 3, jnp.exp(-theta * jnp.maximum(last - 3 - yy, 0).astype(F32)), 0.0)
    powers[3] = jnp.where(yy >= 3, jnp.exp(-theta * jnp.maximum(yy - 3, 0).astype(F32)), 0.0)

    def decay(n):
        return jnp.exp(-theta * n.astype(F32))

    def directly(n, inside):
        return jnp.where(inside, decay(jnp.maximum(n, 0)), 0.0)

    for i in range(C):
        rev = C - 1 - i
        coef[0, i, 0:1, :] = directly(CCOLS * (c - 1 - i) - 3, i < c - 1) + inverse * decay(
            N + CCOLS * rev + CCOLS * c - 3
        )
        coef[0, i, 1:2, :] = inverse * decay(CCOLS * i + CCOLS * c - 3)
        coef[1, i, 0:1, :] = inverse * decay(CCOLS * (C - 1 - c) + CCOLS * rev - 3)
        coef[1, i, 1:2, :] = directly(CCOLS * (i - c - 1) - 3, i > c + 1) + inverse * decay(
            2 * N - CCOLS * (c + 1) + CCOLS * i - 3
        )
    at = lax.broadcasted_iota(jnp.int32, (COLS, 128), 0)
    to = lax.broadcasted_iota(jnp.int32, (COLS, 128), 1)
    select[...] = jnp.where((to < 64) & (at == STEP * (to & 31)), 1.0, 0.0).astype(F32)
    at = lax.broadcasted_iota(jnp.int32, (PAD, WIDTH), 0)
    to = lax.broadcasted_iota(jnp.int32, (PAD, WIDTH), 1) >> GRIDS
    spread[...] = jnp.where(at == jnp.where(to < CCOLS + 3, to + 8, to + 8 - WIDTH // STEP), 1.0, 0.0).astype(F32)
    ext[...] = jnp.zeros((PAD, FREQ), F32)

    for _, receives, copy in halo_copies[:8]:
        pl.when(receives)(copy.wait_recv)
    lane = lax.broadcasted_iota(jnp.int32, (quarter, 128), 1)
    for g in range(4):
        rows = slice(quarter * g, quarter * g + quarter)
        in_right[rows, :] = jnp.where((lane & 63) < NEAR, pltpu.roll(near_got[0], (128 - NEAR * g) % 128, 1), 0.0)
        in_left[rows, :] = jnp.where((lane & 63) >= 64 - NEAR, pltpu.roll(near_got[1], 48 - NEAR * g, 1), 0.0)

    def arrange():
        lane = lax.broadcasted_iota(jnp.int32, (SUB, 128), 1)
        for p in range(STEP):
            rows = pl.ds(p, SUB, stride=STEP)
            for k in range(OWN_CHUNKS):
                span = slice(128 * k, 128 * k + 128)
                qual[p + 1, :, span] = nat.at[0, k][rows, :]
                phase[p + 1, :, span] = nat.at[1, k][rows, :]
            a, b = in_right[rows, :], in_left[rows, :]
            qual[p + 1, :, COLS:WIDTH] = jnp.where(lane < 64, a, b)
            phase[p + 1, :, COLS:WIDTH] = pltpu.roll(jnp.where(lane < 64, b, a), 64, 1)
        wrap(qual, above=False)
        wrap(phase, above=False)

    def steep(u):
        return u - jnp.floor(u + 0.5)

    def make_faces(p):
        for h in HALVES:
            q, ph = qual[p + 1, h], phase[p + 1, h]
            wd[p + 1, h] = jnp.minimum(q, qual[p + 2, h])
            wr[p, h] = jnp.minimum(q, ahead(q, 1))
            sd[p + 1, h] = steep(phase[p + 2, h] - ph)
            sr[p, h] = steep(ahead(ph, 1) - ph)

    def start_first(p):
        for h in HALVES:
            a, au, b = wd[p + 1, h], wd[p, h], wr[p, h]
            fr = b * sr[p, h]
            source = au * sd[p, h] - a * sd[p + 1, h] + behind(fr, 1) - fr
            rdiv = DAMPING / jnp.maximum(a + au + b + behind(b, 1), DIAG_FLOOR)
            rdiv0[p, h] = rdiv
            v0[p + 1, h] = source * rdiv

    def open_first():
        arrange()
        steps(STEP, make_faces)
        wrap(wd, below=False)
        wrap(sd, below=False)
        steps(STEP, start_first)
        wrap(v0)

    def restrict_fine():
        src, a1, b1 = levels[0][0], levels[0][1], levels[0][2]

        def body(i):
            for h in HALVES:
                va, v1, v2, vb = v0[2 * i, h], v0[2 * i + 1, h], v0[2 * i + 2, h], v0[2 * i + 3, h]
                a_odd = wd[2 * i + 2, h]
                y = a_odd * (vb - v2 - sd[2 * i + 2, h]) - wd[2 * i, h] * (v1 - va - sd[2 * i, h])
                b0, b_odd = wr[2 * i, h], wr[2 * i + 1, h]
                g = b0 * (ahead(v1, 1) - v1 - sr[2 * i, h]) + b_odd * (ahead(v2, 1) - v2 - sr[2 * i + 1, h])
                src[i, h] = y + ahead(y + g, 1) - behind(g, 1)
                a1[i + 1, h] = a_odd + ahead(a_odd, 1)
                b1[i, h] = ahead(b0 + b_odd, 1)

        steps(STEP // 2, body)
        wrap(a1, below=False)

    def down(level):
        s = 2**level
        count = STEP // s
        src, a, b, rdiv, v, _, _ = levels[level - 1]

        def smooth(p):
            for h in HALVES:
                bb = b[p, h]
                d = DAMPING / jnp.maximum(a[p + 1, h] + a[p, h] + bb + behind(bb, s), DIAG_FLOOR)
                rdiv[p, h] = d
                v[p + 1, h] = src[p, h] * d

        steps(count, smooth)
        wrap(v)
        if level < GRIDS - 1:
            src_n, a_n, b_n = levels[level][0], levels[level][1], levels[level][2]
        else:
            src_n, a_n, b_n = None, None, None

        def body(i):
            for h in HALVES:
                va, v1, v2, vb = v[2 * i, h], v[2 * i + 1, h], v[2 * i + 2, h], v[2 * i + 3, h]
                a_odd = a[2 * i + 2, h]
                t = src[2 * i, h] + src[2 * i + 1, h] + a_odd * (vb - v2) - a[2 * i, h] * (v1 - va)
                b0, b_odd = b[2 * i, h], b[2 * i + 1, h]
                g = b0 * (ahead(v1, s) - v1) + b_odd * (ahead(v2, s) - v2)
                out = t + ahead(t + g, s) - behind(g, s)
                if src_n is None:
                    coarse[h] = out
                else:
                    src_n[i, h] = out
                    a_n[i + 1, h] = a_odd + ahead(a_odd, s)
                    b_n[i, h] = ahead(b0 + b_odd, s)

        steps(count // 2, body)
        if a_n is not None:
            wrap(a_n, below=False)

    def settle(level):
        s = 2**level
        count = STEP // s
        src, a, b, rdiv, v, base, _ = levels[level - 1]

        def body(i):
            for h in HALVES:
                va, v1, v2, vb = v[2 * i, h], v[2 * i + 1, h], v[2 * i + 2, h], v[2 * i + 3, h]
                g0 = a[2 * i, h] * (v1 - va)
                g1 = a[2 * i + 1, h] * (v2 - v1)
                g2 = a[2 * i + 2, h] * (vb - v2)
                f1 = b[2 * i, h] * (ahead(v1, s) - v1)
                f2 = b[2 * i + 1, h] * (ahead(v2, s) - v2)
                base[2 * i, h] = v1 + (src[2 * i, h] + g1 - g0 + f1 - behind(f1, s)) * rdiv[2 * i, h]
                base[2 * i + 1, h] = v2 + (src[2 * i + 1, h] + g2 - g1 + f2 - behind(f2, s)) * rdiv[2 * i + 1, h]

        steps(count // 2, body)

    def settle_fine():
        def body(i):
            for h in HALVES:
                va, v1, v2, vb = v0[2 * i, h], v0[2 * i + 1, h], v0[2 * i + 2, h], v0[2 * i + 3, h]
                g0 = wd[2 * i, h] * (v1 - va - sd[2 * i, h])
                g1 = wd[2 * i + 1, h] * (v2 - v1 - sd[2 * i + 1, h])
                g2 = wd[2 * i + 2, h] * (vb - v2 - sd[2 * i + 2, h])
                f1 = wr[2 * i, h] * (ahead(v1, 1) - v1 - sr[2 * i, h])
                f2 = wr[2 * i + 1, h] * (ahead(v2, 1) - v2 - sr[2 * i + 1, h])
                base0[2 * i, h] = v1 + (g1 - g0 + f1 - behind(f1, 1)) * rdiv0[2 * i, h]
                base0[2 * i + 1, h] = v2 + (g2 - g1 + f2 - behind(f2, 1)) * rdiv0[2 * i + 1, h]

        steps(STEP // 2, body)

    def settle_all():
        settle_fine()
        for level in range(1, GRIDS):
            settle(level)

    def climb(level, put):
        s = 2**level
        count = STEP // s
        if level:
            _, a, b, rdiv, _, base, _ = levels[level - 1]
        else:
            a, b, rdiv, base = wd, wr, rdiv0, base0
        if level == GRIDS - 1:
            above_it, below_it = pltpu.roll(coarse[...], 1, 0), pltpu.roll(coarse[...], SUB - 1, 0)

        def correction(i, h):
            if level == GRIDS - 1:
                return (above_it[h], coarse[h], below_it[h])[i + 1]
            x = levels[level][6][i + 1, h]
            column = lax.broadcasted_iota(jnp.int32, x.shape, 1)
            return jnp.where((column & s) == 0, x, behind(x, s))

        for h in HALVES:
            x = correction(0, h)
            upper = x - correction(-1, h)
            for i in range(count // 2):
                after = correction(i + 1, h)
                lower = after - x
                side = ahead(x, s) - x
                f1, f2 = b[2 * i, h] * side, b[2 * i + 1, h] * side
                put(2 * i, h, base[2 * i, h] + x + (f1 - behind(f1, s) - a[2 * i, h] * upper) * rdiv[2 * i, h])
                put(
                    2 * i + 1,
                    h,
                    base[2 * i + 1, h] + x + (f2 - behind(f2, s) + a[2 * i + 2, h] * lower) * rdiv[2 * i + 1, h],
                )
                x, upper = after, lower

    def ascend(put_fine):
        for level in range(GRIDS - 1, 0, -1):
            out = levels[level - 1][6]

            def put(p, h, x, out=out):
                out[p + 1, h] = x

            climb(level, put)
            wrap(out)
        climb(0, put_fine)

    def coarse_solve(turn, meanwhile):
        a3, b3 = levels[2][1:3]
        column = lax.broadcasted_iota(jnp.int32, (SUB, COLS), 1)
        line = lax.broadcasted_iota(jnp.int32, (SUB, COLS), 0)
        here = slice(0, COLS)
        part = jnp.where((column & 7) == 0, a3[2, :, here], 0.0) + jnp.where(
            (column & 15) == 8, b3[0, :, here] + b3[1, :, here], 0.0
        )
        part = jnp.where((line < CROWS) & ((column & 7) == 0), part, 0.0)
        local = jnp.sum(jnp.sum(part, axis=1, keepdims=True), axis=0, keepdims=True)
        mine = jnp.dot(coarse[:, here], select[...], precision=HIGHEST, preferred_element_type=F32)
        spot = lax.broadcasted_iota(jnp.int32, (8, 128), 1)
        blocks[turn, r] = jnp.where(spot < 32, mine[0:8], jnp.where(spot < 64, mine[8:16], local))
        copies = []
        for i in sorted(range(1, R), key=lambda i: -min(i, R - i)):
            copy = pltpu.make_async_remote_copy(
                src_ref=blocks.at[turn, r],
                dst_ref=blocks.at[turn, r],
                send_sem=p2_send.at[turn, i - 1],
                recv_sem=p2_recv.at[turn, i - 1],
                device_id=(lax.rem(r + i, R), c),
                device_id_type=MESH,
            )
            copy.start()
            copies.append(copy)
        for copy in copies:
            copy.wait_recv()
        every = blocks[turn].reshape(R * 8, 128).T
        hat = jnp.dot(every[0:32], forward[0], precision=HIGHEST, preferred_element_type=F32) + jnp.dot(
            every[32:64], forward[1], precision=HIGHEST, preferred_element_type=F32
        )
        rows_sum = jnp.sum(every[64:65], axis=1, keepdims=True) * 0.125

        def total(n):
            return jnp.sum(powers[n] * hat, axis=0, keepdims=True)

        mode = lax.broadcasted_iota(jnp.int32, (1, FREQ), 1)
        amps[turn, c, 0:1, :] = jnp.where(mode < CROWS * R, total(0), rows_sum)
        amps[turn, c, 1:2, :] = total(1)
        near_send[turn, 0, 0:1, :] = total(2)
        near_send[turn, 0, 1:4, :] = hat[CCOLS - 3 : CCOLS]
        near_send[turn, 1, 0:3, :] = hat[0:3]
        near_send[turn, 1, 3:4, :] = total(3)
        for i in sorted(range(1, C), key=lambda i: -min(i, C - i)):
            copy = pltpu.make_async_remote_copy(
                src_ref=amps.at[turn, c],
                dst_ref=amps.at[turn, c],
                send_sem=p3_send.at[turn, i - 1],
                recv_sem=p3_recv.at[turn, i - 1],
                device_id=(r, lax.rem(c + i, C)),
                device_id_type=MESH,
            )
            copy.start()
            copies.append(copy)
        rightward = pltpu.make_async_remote_copy(
            src_ref=near_send.at[turn, 0],
            dst_ref=near_left.at[turn],
            send_sem=nb_send.at[turn, 0],
            recv_sem=nb_recv.at[turn, 0],
            device_id=(r, lax.rem(c + 1, C)),
            device_id_type=MESH,
        )
        leftward = pltpu.make_async_remote_copy(
            src_ref=near_send.at[turn, 1],
            dst_ref=near_right.at[turn],
            send_sem=nb_send.at[turn, 1],
            recv_sem=nb_recv.at[turn, 1],
            device_id=(r, lax.rem(c + C - 1, C)),
            device_id_type=MESH,
        )
        pl.when(is_right)(rightward.start)
        pl.when(is_left)(leftward.start)
        meanwhile()
        pl.when(is_left)(rightward.wait_recv)
        pl.when(is_right)(leftward.wait_recv)
        for copy in copies[R - 1 :]:
            copy.wait_recv()
        into_left = jnp.zeros((2, FREQ), F32)
        into_right = jnp.zeros((2, FREQ), F32)
        weight = jnp.zeros((2, FREQ), F32)
        for i in range(C):
            x = amps[turn, i]
            into_left += coef[0, i] * x
            into_right += coef[1, i] * x
            weight += x
        into_left = into_left[0:1] + into_left[1:2]
        into_right = into_right[0:1] + into_right[1:2]
        weight = jnp.sum(jnp.where(mode == FREQ - 1, weight[0:1], 0.0), axis=1, keepdims=True)
        grid_rows, grid_cols = CROWS * R, CCOLS * C
        mean = weight * (1.0 / ((grid_rows - 1) * grid_cols + grid_rows * (grid_cols - 1))) + EPSILON
        ext[4:8, :] = near_left[turn]
        ext[4:5, :] = near_left[turn, 0:1, :] + into_left
        ext[8 : 8 + CCOLS, :] = hat
        ext[8 + CCOLS : 12 + CCOLS, :] = near_right[turn]
        ext[11 + CCOLS : 12 + CCOLS, :] = near_right[turn, 3:4, :] + into_right
        hats = ext[...]
        place = lax.broadcasted_iota(jnp.int32, (PAD, FREQ), 0)
        going_right = hats
        going_left = hats
        for i, s in enumerate(SHIFTS):
            q = constants[3 + i : 4 + i, :]
            going_right += q * jnp.where(place >= s, pltpu.roll(going_right, s, 0), 0.0)
            going_left += q * jnp.where(place < PAD - s, pltpu.roll(going_left, PAD - s, 0), 0.0)
        modes = (going_right + going_left - hats) * (green / mean)
        values = lax.dot_general(
            backward[...], modes, (((1,), (1,)), ((), ())), precision=HIGHEST, preferred_element_type=F32
        )
        coarse[...] = jnp.dot(values, spread[...], precision=HIGHEST, preferred_element_type=F32)
        return copies, rightward, leftward

    def descend():
        restrict_fine()
        for level in range(1, GRIDS):
            down(level)

    def widen():
        for _, receives, copy in halo_copies[8:]:
            pl.when(receives)(copy.wait_recv)
        nat[:, chunks, far, :] = outer[...]
        lane = lax.broadcasted_iota(jnp.int32, (half, 128), 1) & 63
        for i, ref in enumerate((in_right, in_left)):
            ref[far, :] = far_corner[i]
            for g in range(2):
                rows = slice(half * g, half * g + half)
                x = pltpu.roll(far_got[i], NEAR if g == 0 else 128 - NEAR, 1)
                ref[rows, :] = jnp.where((lane >= NEAR) & (lane < HALO), x, ref[rows, :])
        open_first()
        descend()
        settle_all()

    def put_first(p, h, x):
        first[p + 1, h] = x

    def put_result(p, h, x):
        rows = pl.ds(STEP * h.start + p, 8, stride=STEP)
        for k in range(OWN_CHUNKS):
            result.at[k][rows, :] = x[:, 128 * k : 128 * k + 128] * TURN

    open_first()
    descend()
    sent = [coarse_solve(0, widen)]
    ascend(put_first)
    wrap(first)

    def reweight(p):
        for h in HALVES:
            f = first[p + 1, h]
            e = first[p + 2, h] - f - sd[p + 1, h]
            a = wd[p + 1, h] / jnp.maximum(jnp.abs(e) * TURN, ERROR_FLOOR)
            wd[p + 1, h] = a
            gd[p + 1, h] = a * e
            e = ahead(f, 1) - f - sr[p, h]
            b = wr[p, h] / jnp.maximum(jnp.abs(e) * TURN, ERROR_FLOOR)
            wr[p, h] = b
            gr[p, h] = b * e

    steps(STEP, reweight)
    wrap(wd, below=False)
    wrap(gd, below=False)

    def start_second(p):
        for h in HALVES:
            b, f = wr[p, h], gr[p, h]
            rdiv = DAMPING / jnp.maximum(wd[p + 1, h] + wd[p, h] + b + behind(b, 1), DIAG_FLOOR)
            rdiv0[p, h] = rdiv
            v0[p + 1, h] = first[p + 1, h] + (gd[p + 1, h] - gd[p, h] + f - behind(f, 1)) * rdiv

    steps(STEP, start_second)
    wrap(v0)
    descend()
    sent.append(coarse_solve(1, settle_all))
    ascend(put_result)

    outs = []
    for k in range(OWN_CHUNKS):
        span = slice(128 * k, 128 * k + 128)
        copy = pltpu.make_async_copy(result.at[k, own, :], out_h.at[:, span], out_sem.at[k])
        copy.start()
        outs.append(copy)
    for sends, _, copy in halo_copies:
        pl.when(sends)(copy.wait_send)
    for copies, rightward, leftward in sent:
        for copy in copies:
            copy.wait_send()
        pl.when(is_right)(rightward.wait_send)
        pl.when(is_left)(leftward.wait_send)
    for copy in outs:
        copy.wait()


def scratch(R, C):
    def field(count):
        return pltpu.VMEM((count, SUB, WIDTH), F32)

    shapes = [
        pltpu.VMEM((ROWS, COLS), jnp.int32),
        pltpu.VMEM((ROWS, COLS), jnp.int32),
        pltpu.VMEM((ROWS, COLS), jnp.int32),
        pltpu.VMEM((2, R * 8, FREQ), F32),
        pltpu.VMEM((SUB, FREQ), F32),
        pltpu.VMEM((16, FREQ), F32),
        pltpu.VMEM((2, OWN_CHUNKS, EXT, 128), F32),
        pltpu.VMEM((ROWS, 128), F32),
        pltpu.VMEM((ROWS, 128), F32),
        pltpu.VMEM((2, ROWS // 4, 128), F32),
        pltpu.VMEM((2, ROWS // 4, 128), F32),
        pltpu.VMEM((EXT, 128), F32),
        pltpu.VMEM((EXT, 128), F32),
        pltpu.VMEM((2, OWN_CHUNKS, EXT - ROWS - 2 * NEAR, 128), F32),
        pltpu.VMEM((2, ROWS // 2, 128), F32),
        pltpu.VMEM((2, ROWS // 2, 128), F32),
        pltpu.VMEM((2, EXT - ROWS - 2 * NEAR, 128), F32),
        pltpu.VMEM((OWN_CHUNKS, EXT, 128), F32),
    ]
    padded, plain = STEP + 2, STEP
    shapes += [field(n) for n in (padded, padded, padded, plain, padded, plain, padded, plain, plain, padded, padded, plain)]
    for level in range(1, GRIDS):
        n = STEP >> level
        shapes += [field(m) for m in (n, n + 2, n, n, n + 2, n, n + 2)]
    shapes += [
        pltpu.VMEM((SUB, WIDTH), F32),
        pltpu.VMEM((COLS, 128), F32),
        pltpu.VMEM((PAD, WIDTH), F32),
        pltpu.VMEM((2, R, 8, 128), F32),
        pltpu.VMEM((2, C, 2, FREQ), F32),
        pltpu.VMEM((2, 2, 4, FREQ), F32),
        pltpu.VMEM((2, 4, FREQ), F32),
        pltpu.VMEM((2, 4, FREQ), F32),
        pltpu.VMEM((PAD, FREQ), F32),
        pltpu.VMEM((4, CCOLS, FREQ), F32),
        pltpu.VMEM((2, C, 2, FREQ), F32),
        pltpu.SemaphoreType.DMA((6,)),
        pltpu.SemaphoreType.DMA((16,)),
        pltpu.SemaphoreType.DMA((16,)),
        pltpu.SemaphoreType.DMA((2, R - 1)),
        pltpu.SemaphoreType.DMA((2, R - 1)),
        pltpu.SemaphoreType.DMA((2, C - 1)),
        pltpu.SemaphoreType.DMA((2, C - 1)),
        pltpu.SemaphoreType.DMA((2, 2)),
        pltpu.SemaphoreType.DMA((2, 2)),
        pltpu.SemaphoreType.DMA((OWN_CHUNKS,)),
    ]
    return shapes


def solution(mesh):
    R, C = mesh.shape["row"], mesh.shape["col"]
    forward, backward, constants = tables(CROWS * R, CCOLS * C)

    def body(swath, coherence, counts):
        return pl.pallas_call(
            functools.partial(kernel, R, C),
            out_shape=jax.ShapeDtypeStruct((ROWS, COLS), F32),
            in_specs=[pl.BlockSpec(memory_space=pl.ANY)] * 6,
            out_specs=pl.BlockSpec(memory_space=pl.ANY),
            scratch_shapes=scratch(R, C),
            compiler_params=pltpu.CompilerParams(
                collective_id=0, has_side_effects=True
            ),
        )(swath, coherence, counts, jnp.asarray(forward), jnp.asarray(backward), jnp.asarray(constants))

    return jax.shard_map(
        body,
        mesh=mesh,
        in_specs=(P("row", "col"), P("row", "col"), P("row", "col")),
        out_specs=P("row", "col"),
        check_vma=False,
    )
```
